512 devices in a mesh: section: 4 (over x), rep: 128 (over y, z, core).
Axes of the slice: x: 4, y: 8, z: 8, core: 2. Of those that a mesh axis runs over, the one named last changes fastest.
Arguments:
- tile_features: bfloat16 [256, 16, 16, 512], P('rep'), may hold values from -6 to 6
- patches: bfloat16 [256, 16, 16, 768], P('rep'), may hold values from -6 to 6
- det_kernel: float32 [4, 7, 7, 512], P('section'), may hold values from -0.875 to 0.875
- det_gain: float32 [4, 512], P('section'), may hold values from 0.1 to 1.9
- det_in: bfloat16 [4, 512, 2048], P('section', None, 'rep'), may hold values from -0.25 to 0.25
- det_out: bfloat16 [4, 2048, 512], P('section', 'rep'), may hold values from -0.125 to 0.125
- det_scale: float32 [4, 512], P('section'), may hold values from 0.3 to 1.5
- cls_embed: bfloat16 [768, 1024], P(None, 'section'), may hold values from -0.21875 to 0.21875
- cls_merge: bfloat16 [512, 1024], P(None, 'section'), may hold values from -0.25 to 0.25
- cls_pos: bfloat16 [196, 1024], P(None, 'section'), may hold values from -3 to 3
- cls_qkv: bfloat16 [1024, 3, 512], P(None, None, 'section'), may hold values from -1.5 to 1.5
- cls_out: bfloat16 [512, 1024], P('section'), may hold values from -0.25 to 0.25
- cls_gain: float32 [2, 1024], replicated, may hold values from 0.1 to 1.9
- crop_plan: int32 [128, 4, 3, 3], P('rep'), may hold values from 0 to 2, as said below
- slot_from: int32 [128, 4], P('rep'), may hold values from 0 to 3, as said below
Outputs:
- crop_class: float32 [128, 4, 1024], P('rep', 'section')
The draws below stay inside these ranges and needn't reach their ends.
Inputs may be any that keep to these rules, and one draw needn't show every extreme that they name: `crop_plan`: each entry is a micro-batch below 2 followed by a top and a left patch offset of 0 to 2; records that no slot names are arbitrary. `slot_from`: 0 marks an empty slot, 1 a crop from the replica one index lower, 2 the replica's own, 3 one from the replica one index higher; the first replica never has 1 and the last never has 3.
All inputs are finite; a program needn't handle non-finite values.
Results may differ from the reference program's by a relative error of at most 0.004.
Values may be sent and summed in bfloat16 or wider, within the bound.
No kernel may reach another device: no remote copies, remote signals or barrier semaphores. Data moves between devices by JAX's collectives and lax.ppermute only.
A program may use at most 64 MiB of HBM per device.

```python
import math
import jax
import jax.numpy as jnp
from jax import lax

DDET = 512
HIDDET = 2048
DCLS = 1024
PATCH = 768
HEAD_DIM = 64
HEADS = 8
TILE = 16
CROP = 14
MICRO = 2
TILES = 256
N_SECTION = 4
N_REP = 128


def draw_crop_plan(key, part):
    micro_part = jax.random.randint(jax.random.fold_in(key, 11), (N_REP, N_SECTION, 3, 1), 0, MICRO)
    corner_part = jax.random.randint(jax.random.fold_in(key, 12), (N_REP, N_SECTION, 3, 2), 0, TILE - CROP + 1)
    plan_table = jnp.concatenate([micro_part, corner_part], axis=3).astype(jnp.int32)
    plan_table = plan_table.at[0, 0, 0].set(jnp.array([MICRO - 1, TILE - CROP, TILE - CROP], jnp.int32))
    plan_table = plan_table.at[0, 0, 1].set(jnp.zeros((3,), jnp.int32))
    return plan_table


def draw_slot_from(key, part):
    picks = jax.random.randint(jax.random.fold_in(key, 21), (N_REP, N_SECTION), 0, 4)
    rep_ids = jnp.arange(N_REP)[:, None]
    picks = jnp.where((rep_ids == 0) & (picks == 1), 2, picks)
    picks = jnp.where((rep_ids == N_REP - 1) & (picks == 3), 2, picks)
    picks = picks.at[1, 0].set(1).at[0, 1].set(3).at[0, 2].set(2).at[0, 3].set(0)
    return picks.astype(jnp.int32)


def draw_cls_qkv(key, part):
    width = HEADS * HEAD_DIM
    base = jax.random.normal(jax.random.fold_in(key, 31), (DCLS, 3, width), jnp.float32) / math.sqrt(DCLS)
    return jnp.clip(base, -1.5, 1.5).astype(jnp.bfloat16)


def block_levels(key, shape, split, least, largest):
    factor_of = 1.0
    for axis_at, blocks in split:
        draws = jax.random.uniform(jax.random.fold_in(jax.random.fold_in(key, 6), axis_at), (blocks,), jnp.float32, least / len(split), largest / len(split))
        factor_of = factor_of * jnp.repeat(jnp.exp(draws), shape[axis_at] // blocks).reshape((-1,) + (1,) * (len(shape) - 1 - axis_at))
    return factor_of


def bell_draw(key, shape, deviation, limit, split=(), kind=jnp.bfloat16):
    level = block_levels(key, shape, split, -0.22, 0.18) if split else 1.0
    drawn = jax.random.normal(key, shape, jnp.float32) * deviation * level
    return jnp.minimum(jnp.maximum(drawn, -limit), limit).astype(kind)


def setup_inputs(seed: int = 0) -> dict:
    splits = jax.random.split(jax.random.key(seed), 16)
    return {
        "tile_features": bell_draw(splits[0], (TILES, TILE, TILE, DDET), 1.0, 6.0, ((0, 128),)),
        "patches": bell_draw(splits[1], (TILES, TILE, TILE, PATCH), 1.0, 6.0, ((0, 128),)),
        "det_kernel": bell_draw(splits[2], (N_SECTION, 7, 7, DDET), 49 ** -0.5, 0.875, ((0, 4),), jnp.float32),
        "det_gain": jnp.clip(1.0 + 0.18 * jax.random.normal(splits[3], (N_SECTION, DDET), jnp.float32), 0.1, 1.9),
        "det_in": bell_draw(splits[4], (N_SECTION, DDET, HIDDET), DDET ** -0.5, 0.25, ((0, 4), (2, 128))),
        "det_out": bell_draw(splits[5], (N_SECTION, HIDDET, DDET), HIDDET ** -0.5, 0.125, ((0, 4), (1, 128))),
        "det_scale": jnp.clip(jnp.exp(math.log(1.5) - 1.60943787 * jax.random.uniform(splits[6], (N_SECTION, DDET), jnp.float32) ** block_levels(splits[6], (N_SECTION, DDET), ((0, 4),), -0.2, 0.2)), 0.3, 1.5),
        "cls_embed": bell_draw(splits[7], (PATCH, DCLS), PATCH ** -0.5, 0.21875, ((1, 4),)),
        "cls_merge": bell_draw(splits[8], (DDET, DCLS), DDET ** -0.5, 0.25, ((1, 4),)),
        "cls_pos": bell_draw(splits[9], (CROP * CROP, DCLS), 0.5, 3.0, ((1, 4),)),
        "cls_qkv": draw_cls_qkv(jax.random.fold_in(splits[15], 71), 0),
        "cls_out": bell_draw(splits[11], (HEADS * HEAD_DIM, DCLS), (HEADS * HEAD_DIM) ** -0.5, 0.25, ((0, 4),)),
        "cls_gain": jnp.clip(1.0 + 0.18 * jax.random.normal(splits[12], (2, DCLS), jnp.float32), 0.1, 1.9),
        "crop_plan": draw_crop_plan(jax.random.fold_in(splits[15], 71), 0),
        "slot_from": draw_slot_from(jax.random.fold_in(splits[15], 71), 0),
    }


epsilon = 1e-06

def layer_norm(values, gain_row):
    row_mean = lax.optimization_barrier(jnp.mean(values, axis=-1, keepdims=True))
    centred = values - row_mean
    row_var = lax.optimization_barrier(jnp.mean(centred * centred, axis=-1, keepdims=True))
    return centred * lax.rsqrt(row_var + epsilon) * gain_row

def detector_block(tile_rows, kernel, gain_row, in_weight, out_weight, scale_row):
    widened = tile_rows.astype(jnp.float32)
    padded = jnp.pad(widened, ((3, 3), (3, 3), (0, 0)))
    conv = jnp.zeros_like(widened)
    for row_shift in range(7):
        for col_shift in range(7):
            conv = conv + padded[row_shift:row_shift + TILE, col_shift:col_shift + TILE] * kernel[row_shift, col_shift]
    normed = layer_norm(conv, gain_row).astype(jnp.bfloat16).reshape(TILE * TILE, -1)
    hidden = jax.nn.gelu(jnp.dot(normed, in_weight, preferred_element_type=jnp.float32)).astype(jnp.bfloat16)
    update = jnp.dot(hidden, out_weight, preferred_element_type=jnp.float32).reshape(widened.shape)
    return (widened + scale_row * update).astype(jnp.bfloat16)

def classify(pixel_rows, feat_rows, cls_embed, cls_merge, cls_pos, cls_qkv, cls_out, cls_gain):
    widened = jnp.dot(pixel_rows, cls_embed, preferred_element_type=jnp.float32) + jnp.dot(feat_rows, cls_merge, preferred_element_type=jnp.float32) + cls_pos.astype(jnp.float32)
    attn_in = layer_norm(widened, cls_gain[0]).astype(jnp.bfloat16)
    qkv_matrix = cls_qkv.reshape(cls_qkv.shape[0], -1)
    qkv = jnp.dot(attn_in, qkv_matrix, preferred_element_type=jnp.float32).astype(jnp.bfloat16)
    width = HEADS * HEAD_DIM
    query_rows = qkv[:, :width].reshape(-1, HEADS, HEAD_DIM).astype(jnp.float32)
    key_rows = qkv[:, width:2 * width].reshape(-1, HEADS, HEAD_DIM).astype(jnp.float32)
    value_rows = qkv[:, 2 * width:].reshape(-1, HEADS, HEAD_DIM).astype(jnp.float32)
    scores = jnp.einsum('qhd,khd->hqk', query_rows, key_rows) * (1.0 / math.sqrt(HEAD_DIM))
    top_score = lax.optimization_barrier(jnp.max(scores, axis=-1, keepdims=True))
    weights = jnp.exp(scores - top_score)
    probs = (weights / lax.optimization_barrier(jnp.sum(weights, axis=-1, keepdims=True))).astype(jnp.bfloat16)
    context = jnp.einsum('hqk,khd->qhd', probs.astype(jnp.float32), value_rows).astype(jnp.bfloat16)
    mixed = widened + jnp.dot(context.reshape(-1, width), cls_out, preferred_element_type=jnp.float32)
    pooled = lax.optimization_barrier(jnp.mean(mixed, axis=0))
    return layer_norm(pooled, cls_gain[1])

def reference(tile_features, patches, det_kernel, det_gain, det_in, det_out, det_scale, cls_embed, cls_merge, cls_pos, cls_qkv, cls_out, cls_gain, crop_plan, slot_from):

    def run_tile(tile_rows):
        for block in range(N_SECTION):
            tile_rows = detector_block(tile_rows, det_kernel[block], det_gain[block], det_in[block], det_out[block], det_scale[block])
        return tile_rows
    finals = lax.map(run_tile, tile_features)

    def one_slot(slot_index):
        owner_rep = slot_index // N_SECTION
        slot_num = slot_index % N_SECTION
        source = slot_from[owner_rep, slot_num]
        offset = jnp.where(source == 1, -1, jnp.where(source == 3, 1, 0)).astype(jnp.int32)
        direction = jnp.where(source == 1, 2, jnp.where(source == 3, 0, 1)).astype(jnp.int32)
        src_rep = jnp.clip(owner_rep + offset, 0, N_REP - 1).astype(jnp.int32)
        record = crop_plan[src_rep, slot_num, direction].astype(jnp.int32)
        tile_num = (src_rep * MICRO + record[0]).astype(jnp.int32)
        zero_index = jnp.int32(0)
        pixel_rows = lax.dynamic_slice(patches, (tile_num, record[1], record[2], zero_index), (1, CROP, CROP, PATCH)).reshape(CROP * CROP, PATCH)
        feat_rows = lax.dynamic_slice(finals, (tile_num, record[1], record[2], zero_index), (1, CROP, CROP, DDET)).reshape(CROP * CROP, DDET)
        result = classify(pixel_rows, feat_rows, cls_embed, cls_merge, cls_pos, cls_qkv, cls_out, cls_gain)
        return jnp.where(source == 0, jnp.zeros_like(result), result)
    results = lax.map(one_slot, jnp.arange(N_REP * N_SECTION, dtype=jnp.int32))
    return results.reshape(N_REP, N_SECTION, DCLS)
```

```python
import math

import jax
import jax.numpy as jnp
from jax import lax
from jax.experimental import pallas as pl
from jax.experimental.pallas import tpu as pltpu
from jax.sharding import PartitionSpec as P

HEAD_DIM = 64
TILE = 16
CELLS = TILE * TILE
CROP = 14
ROWS = CROP * CROP
PADDED = 208
LANES = 128
SIDE = 8
EPSILON = 1e-06

ANY = pl.BlockSpec(memory_space=pl.ANY)
SMEM = pl.BlockSpec(memory_space=pltpu.SMEM)
VMEM = pl.BlockSpec(memory_space=pltpu.VMEM)


def rep_index(y, z, core):
    return (y * SIDE + z) * 2 + core


def line_groups(first):
    along_z = [[rep_index(y, z, 0 if first else 1) for z in range(SIDE)] for y in range(SIDE)]
    along_y = [[rep_index(y, z, 1 if first else 0) for y in range(SIDE)] for z in range(SIDE)]
    return along_z + along_y


def spread_in_groups(block, groups):
    copies = jnp.broadcast_to(block[None], (SIDE,) + block.shape)
    return lax.all_to_all(copies, "rep", 0, 0, axis_index_groups=groups)


def block_body(flag_ref, tile_ref, param_ref, own_ref, other_ref, out_ref, tile_buf, wide, conv, w_in, w_out, sems):
    @pl.when(flag_ref[0] == 1)
    def _():
        count = own_ref.shape[0]
        copies = [
            pltpu.make_async_copy(own_ref.at[:, 0], w_in.at[pl.ds(0, count)], sems.at[0]),
            pltpu.make_async_copy(other_ref.at[:, 0], w_in.at[pl.ds(count, count)], sems.at[1]),
            pltpu.make_async_copy(own_ref.at[:, 1], w_out.at[pl.ds(0, count)], sems.at[2]),
            pltpu.make_async_copy(other_ref.at[:, 1], w_out.at[pl.ds(count, count)], sems.at[3]),
        ]
        tile_copy = pltpu.make_async_copy(tile_ref, tile_buf, sems.at[4])
        tile_copy.start()
        for copy in copies:
            copy.start()
        slabs = wide.shape[0]
        wide[:, :, 0:8, :] = jnp.zeros((slabs, TILE, 8, LANES), jnp.float32)
        wide[:, :, 24:32, :] = jnp.zeros((slabs, TILE, 8, LANES), jnp.float32)
        tile_copy.wait()
        for slab in range(slabs):
            part = tile_buf[:, slab * LANES : (slab + 1) * LANES].astype(jnp.float32)
            wide[slab, :, 8:24, :] = part.reshape(TILE, TILE, LANES)

        def one_slab(slab, carry):
            sums = [None] * TILE
            for col in range(7):
                taps = [param_ref[slab, pl.ds(row * 7 + col, 1), :] for row in range(7)]
                for source in range(TILE):
                    cells = wide[slab, source, pl.ds(5 + col, TILE), :]
                    for row in range(7):
                        target = source + 3 - row
                        if 0 <= target < TILE:
                            term = cells * taps[row]
                            sums[target] = term if sums[target] is None else sums[target] + term
            for target in range(TILE):
                conv[slab, pl.ds(target * TILE, TILE), :] = sums[target]
            return carry

        lax.fori_loop(0, slabs, one_slab, 0)
        width = slabs * LANES
        total = conv[0]
        for slab in range(1, slabs):
            total = total + conv[slab]
        mean = jnp.sum(total, axis=-1, keepdims=True) / width
        squares = None
        for slab in range(slabs):
            centred = conv[slab] - mean
            squares = centred * centred if squares is None else squares + centred * centred
        scale = lax.rsqrt(jnp.sum(squares, axis=-1, keepdims=True) / width + EPSILON)
        normed = jnp.concatenate(
            [
                ((conv[slab] - mean) * scale * param_ref[slab, pl.ds(49, 1), :]).astype(jnp.bfloat16)
                for slab in range(slabs)
            ],
            axis=1,
        )
        for copy in copies:
            copy.wait()
        update = None
        step = 32
        for chunk in range(0, 2 * count, step):
            into = w_in[pl.ds(chunk, step)].reshape(step * 16, width)
            outof = w_out[pl.ds(chunk, step)].reshape(step * 16, width)
            hidden = lax.dot_general(
                normed, into, (((1,), (1,)), ((), ())), preferred_element_type=jnp.float32
            )
            hidden = jax.nn.gelu(hidden, approximate=True).astype(jnp.bfloat16)
            term = jnp.dot(hidden, outof, preferred_element_type=jnp.float32)
            update = term if update is None else update + term
        for slab in range(slabs):
            part = slice(slab * LANES, (slab + 1) * LANES)
            tile_buf[:, part] = (
                tile_buf[:, part].astype(jnp.float32) + param_ref[slab, pl.ds(50, 1), :] * update[:, part]
            ).astype(jnp.bfloat16)
        result_copy = pltpu.make_async_copy(tile_buf, out_ref, sems.at[4])
        result_copy.start()
        result_copy.wait()


def detector_block(flag, tile, params, own, other):
    cells, width = tile.shape
    slabs = width // LANES
    count = own.shape[0]
    return pl.pallas_call(
        block_body,
        out_shape=jax.ShapeDtypeStruct(tile.shape, jnp.bfloat16),
        in_specs=[SMEM, ANY, VMEM, ANY, ANY],
        out_specs=ANY,
        scratch_shapes=[
            pltpu.VMEM((cells, width), jnp.bfloat16),
            pltpu.VMEM((slabs, TILE, 32, LANES), jnp.float32),
            pltpu.VMEM((slabs, cells, LANES), jnp.float32),
            pltpu.VMEM((2 * count, 16, width), jnp.bfloat16),
            pltpu.VMEM((2 * count, 16, width), jnp.bfloat16),
            pltpu.SemaphoreType.DMA((5,)),
        ],
        name="detector_block",
    )(flag, tile, params, own, other)


def selection(top, left):
    row = lax.broadcasted_iota(jnp.int32, (PADDED, CELLS), 0)
    cell = lax.broadcasted_iota(jnp.int32, (PADDED, CELLS), 1)
    crop_row = (row * 4682) >> 16
    wanted = (top + crop_row) * TILE + left + (row - crop_row * CROP)
    return jnp.where((cell == wanted) & (row < ROWS), 1.0, 0.0).astype(jnp.bfloat16)


def cut_body(plan_ref, *refs):
    groups = (len(refs) - 3) // 2
    out_ref, tiles, sems = refs[2 * groups :]
    place = plan_ref[9]
    for group in range(groups):

        @pl.when(place == group)
        def _(group=group):
            copies = [
                pltpu.make_async_copy(refs[2 * group + micro], tiles.at[micro], sems.at[micro])
                for micro in range(2)
            ]
            for copy in copies:
                copy.start()
            for copy in copies:
                copy.wait()

    for turn in range(3):
        chosen = selection(plan_ref[3 * turn + 1], plan_ref[3 * turn + 2])
        rows = jnp.dot(chosen, tiles[plan_ref[3 * turn]], preferred_element_type=jnp.float32)
        out_ref[turn] = rows.astype(jnp.bfloat16)


def cut_crops(plan, place, tile_pairs):
    cells, width = tile_pairs[0][0].shape
    scalars = jnp.concatenate([plan.reshape(-1), place.reshape(1)]).astype(jnp.int32)
    return pl.pallas_call(
        cut_body,
        out_shape=jax.ShapeDtypeStruct((3, PADDED, width), jnp.bfloat16),
        in_specs=[SMEM] + [ANY] * (2 * len(tile_pairs)),
        out_specs=VMEM,
        scratch_shapes=[pltpu.VMEM((2, cells, width), jnp.bfloat16), pltpu.SemaphoreType.DMA((2,))],
        name="cut_crops",
    )(scalars, *[tile for pair in tile_pairs for tile in pair])


def classify_body(source_ref, pix_own, pix_left, pix_right, feat_own, feat_left, feat_right, weight_ref, gain_ref, out_ref, pix, feat, weights, sems):
    source = source_ref[0]
    sections, rows, lanes = weight_ref.shape
    weight_copies = []
    embed_to, merge_to, pos_to, qkv_to = 1536, 2560, 2976, 6048
    for part, (low, high) in enumerate(((0, pos_to), (pos_to, qkv_to), (qkv_to, rows))):
        weight_copies.append(
            pltpu.make_async_copy(
                weight_ref.at[:, pl.ds(low, high - low)],
                weights.at[:, pl.ds(low, high - low)],
                sems.at[part],
            )
        )
    for copy in weight_copies:
        copy.start()
    for number, (pix_ref, feat_ref) in enumerate(
        ((pix_left, feat_left), (pix_own, feat_own), (pix_right, feat_right))
    ):

        @pl.when((source == number + 1) if number != 1 else ((source == 2) | (source == 0)))
        def _(pix_ref=pix_ref, feat_ref=feat_ref):
            first = pltpu.make_async_copy(pix_ref, pix, sems.at[3])
            second = pltpu.make_async_copy(feat_ref, feat, sems.at[4])
            first.start()
            second.start()
            first.wait()
            second.wait()

    weight_copies[0].wait()
    pixel_rows = pix[...]
    feat_rows = feat[...]

    def columns(section, low, height):
        return jnp.concatenate(
            [weights[section, pl.ds(low, height), :], weights[section, pl.ds(low + height, height), :]],
            axis=1,
        )

    parts = []
    for section in range(sections):
        parts.append(
            jnp.dot(pixel_rows, columns(section, 0, 768), preferred_element_type=jnp.float32)
            + jnp.dot(feat_rows, columns(section, embed_to, 512), preferred_element_type=jnp.float32)
            + columns(section, merge_to, PADDED).astype(jnp.float32)
        )
    tokens = jnp.concatenate(parts, axis=1)
    width = tokens.shape[1]
    mean = jnp.sum(tokens, axis=-1, keepdims=True) / width
    centred = tokens - mean
    var = jnp.sum(centred * centred, axis=-1, keepdims=True) / width
    attn_in = (centred * lax.rsqrt(var + EPSILON) * gain_ref[pl.ds(0, 1), :]).astype(jnp.bfloat16)
    token_sum = jnp.sum(tokens, axis=0, keepdims=True)
    weight_copies[1].wait()
    key_ok = lax.broadcasted_iota(jnp.int32, (PADDED, PADDED), 1) < ROWS
    lane = lax.broadcasted_iota(jnp.int32, (PADDED, 2 * HEAD_DIM), 1)
    row_ok = lax.broadcasted_iota(jnp.int32, (PADDED, 2 * HEAD_DIM), 0) < ROWS
    context_sums = []
    for section in range(sections):
        piece = jnp.concatenate(
            [weights[section, pl.ds(pos_to + 1024 * index, 1024), :] for index in range(3)], axis=1
        )
        qkv = jnp.dot(attn_in, piece, preferred_element_type=jnp.float32).astype(jnp.bfloat16)
        query, key, value = qkv[:, :128], qkv[:, 128:256], qkv[:, 256:]
        contexts = []
        for head in range(2):
            mine = (lane >= HEAD_DIM) if head else (lane < HEAD_DIM)
            scores = lax.dot_general(
                jnp.where(mine, query, jnp.zeros_like(query)),
                key,
                (((1,), (1,)), ((), ())),
                preferred_element_type=jnp.float32,
            ) * (1.0 / math.sqrt(HEAD_DIM))
            scores = jnp.where(key_ok, scores, -jnp.inf)
            top = jnp.max(scores, axis=-1, keepdims=True)
            numer = jnp.exp(scores - top)
            probs = (numer * (1.0 / jnp.sum(numer, axis=-1, keepdims=True))).astype(jnp.bfloat16)
            contexts.append(jnp.dot(probs, value, preferred_element_type=jnp.float32))
        context = jnp.where(lane < HEAD_DIM, contexts[0], contexts[1]).astype(jnp.bfloat16)
        context = jnp.where(row_ok, context.astype(jnp.float32), 0.0)
        context_sums.append(jnp.sum(context, axis=0, keepdims=True))
    context_mean = jnp.concatenate(context_sums, axis=1) / ROWS
    high = context_mean.astype(jnp.bfloat16)
    rest = context_mean - high.astype(jnp.float32)
    middle = rest.astype(jnp.bfloat16)
    low = (rest - middle.astype(jnp.float32)).astype(jnp.bfloat16)
    pieces = jnp.concatenate([high, middle, low, jnp.zeros((13, high.shape[1]), jnp.bfloat16)], axis=0)
    weight_copies[2].wait()
    out_weight = jnp.concatenate(
        [
            jnp.concatenate(
                [weights[section, pl.ds(qkv_to + 128 * column, 128), :] for column in range(8)], axis=1
            )
            for section in range(sections)
        ],
        axis=0,
    )
    mixed = jnp.dot(pieces, out_weight, preferred_element_type=jnp.float32)
    pooled = token_sum / ROWS + jnp.sum(mixed, axis=0, keepdims=True)
    pooled_mean = jnp.sum(pooled, axis=-1, keepdims=True) / width
    centred = pooled - pooled_mean
    var = jnp.sum(centred * centred, axis=-1, keepdims=True) / width
    result = centred * lax.rsqrt(var + EPSILON) * gain_ref[pl.ds(1, 1), :]
    out_ref[...] = jnp.where(source == 0, 0.0, result)


def classify(source, pixels, feats, weights, gain):
    return pl.pallas_call(
        classify_body,
        out_shape=jax.ShapeDtypeStruct((1, gain.shape[1]), jnp.float32),
        in_specs=[SMEM] + [ANY] * 7 + [VMEM],
        out_specs=VMEM,
        scratch_shapes=[
            pltpu.VMEM(pixels[0].shape, jnp.bfloat16),
            pltpu.VMEM(feats[0].shape, jnp.bfloat16),
            pltpu.VMEM(weights.shape, jnp.bfloat16),
            pltpu.SemaphoreType.DMA((5,)),
        ],
        name="classify",
    )(source.reshape(1), *pixels, *feats, weights, gain)


def exchanged(crops):
    count = lax.axis_size("rep")
    upward = [(index, index + 1) for index in range(count - 1)]
    downward = [(target, origin) for origin, target in upward]
    return (
        crops[1],
        lax.ppermute(crops[2], "rep", upward),
        lax.ppermute(crops[0], "rep", downward),
    )


def per_device(
    tile_features,
    patches,
    det_kernel,
    det_gain,
    det_in,
    det_out,
    det_scale,
    cls_embed,
    cls_merge,
    cls_pos,
    cls_qkv,
    cls_out,
    cls_gain,
    crop_plan,
    slot_from,
):
    sections = lax.axis_size("section")
    section = lax.axis_index("section")
    width = tile_features.shape[3]
    slabs = width // LANES

    shard = jnp.stack([det_in[0].T, det_out[0]], axis=0)
    line = spread_in_groups(shard, line_groups(True))
    plane = spread_in_groups(line, line_groups(False))
    own = plane.reshape((SIDE * SIDE,) + shard.shape)
    swap = [(index, index ^ 1) for index in range(lax.axis_size("rep"))]
    other = lax.ppermute(own, "rep", swap)

    pos = jnp.pad(cls_pos, ((0, PADDED - ROWS), (0, 0)))
    packed = jnp.concatenate(
        [
            cls_embed[:, :LANES],
            cls_embed[:, LANES:],
            cls_merge[:, :LANES],
            cls_merge[:, LANES:],
            pos[:, :LANES],
            pos[:, LANES:],
            cls_qkv[:, 0],
            cls_qkv[:, 1],
            cls_qkv[:, 2],
        ]
        + [cls_out[:, column * LANES : (column + 1) * LANES] for column in range(8)],
        axis=0,
    )
    weights = lax.all_gather(packed, "section", axis=0)

    plan = lax.dynamic_index_in_dim(crop_plan[0], section, 0, keepdims=False)
    source = lax.dynamic_index_in_dim(slot_from[0], section, 0, keepdims=False)
    patch_tiles = patches.reshape(2, CELLS, patches.shape[3])
    pixels = exchanged(cut_crops(plan, jnp.int32(0), [(patch_tiles[0], patch_tiles[1])]))

    params = jnp.concatenate(
        [det_kernel[0].reshape(49, width), det_gain, det_scale, jnp.zeros((5, width), jnp.float32)], axis=0
    )
    params = params.reshape(56, slabs, LANES).transpose(1, 0, 2)
    start = tile_features.reshape(2, CELLS, width)
    tiles = [start[0], start[1]]
    for number in range(sections):
        flag = (section == number).astype(jnp.int32).reshape(1)
        tiles = [detector_block(flag, tile, params, own, other) for tile in tiles]
        if number + 1 < sections:
            tiles = [lax.ppermute(tile, "section", [(number, number + 1)]) for tile in tiles]
    last = sections - 1
    pairs = [
        [lax.ppermute(tile, "section", [(last, target)]) for tile in tiles] for target in range(last)
    ]
    feats = exchanged(cut_crops(plan, section, pairs + [tiles]))
    result = classify(source, pixels, feats, weights, cls_gain)
    return result[None]


def solution(mesh):
    return jax.shard_map(
        per_device,
        mesh=mesh,
        in_specs=(
            P("rep", None, None, None),
            P("rep", None, None, None),
            P("section", None, None, None),
            P("section", None),
            P("section", None, "rep"),
            P("section", "rep", None),
            P("section", None),
            P(None, "section"),
            P(None, "section"),
            P(None, "section"),
            P(None, None, "section"),
            P("section", None),
            P(),
            P("rep", None, None, None),
            P("rep", None),
        ),
        out_specs=P("rep", "section", None),
        check_vma=False,
    )
```

```python
import functools
import math

import jax
import jax.numpy as jnp
from jax import lax
from jax.experimental import pallas as pl
from jax.experimental.pallas import tpu as pltpu
from jax.sharding import PartitionSpec as P

HEAD_DIM = 64
TILE = 16
CELLS = TILE * TILE
CROP = 14
ROWS = CROP * CROP
PADDED = 208
LANES = 128
SIDE = 8
REP = ("y", "z", "core")
EPSILON = 1e-06
SLOT_AT = 36
SECTION_AT = 40

ANY = pl.BlockSpec(memory_space=pl.ANY)
SMEM = pl.BlockSpec(memory_space=pltpu.SMEM)
VMEM = pl.BlockSpec(memory_space=pltpu.VMEM)
LIMITED = pltpu.CompilerParams(vmem_limit_bytes=16 << 20)


def rep_index(y, z, core):
    return (y * SIDE + z) * 2 + core


def line_groups(first):
    along_z = [[rep_index(y, z, 0 if first else 1) for z in range(SIDE)] for y in range(SIDE)]
    along_y = [[rep_index(y, z, 1 if first else 0) for y in range(SIDE)] for z in range(SIDE)]
    return along_z + along_y


def spread_in_groups(block, groups):
    copies = jnp.broadcast_to(block[None], (SIDE,) + block.shape)
    return lax.all_to_all(copies, REP, 0, 0, axis_index_groups=groups)


def resident(array):
    return pltpu.with_memory_space_constraint(array, pltpu.VMEM)


def in_hbm(array):
    return pltpu.with_memory_space_constraint(array, pltpu.HBM)


def active(ints_ref, number):
    return ints_ref[SECTION_AT] == number


def block_body(ints_ref, tile_ref, param_ref, own_ref, other_ref, out_ref, wide, conv, *, number):
    @pl.when(active(ints_ref, number))
    def _():
        slabs = wide.shape[0]
        wide[:, :, 0:8, :] = jnp.zeros((slabs, TILE, 8, LANES), jnp.float32)
        wide[:, :, 24:32, :] = jnp.zeros((slabs, TILE, 8, LANES), jnp.float32)
        for slab in range(slabs):
            part = tile_ref[:, slab * LANES : (slab + 1) * LANES].astype(jnp.float32)
            wide[slab, :, 8:24, :] = part.reshape(TILE, TILE, LANES)

        def one_slab(slab, carry):
            sums = [None] * TILE
            for col in range(7):
                taps = [param_ref[slab, pl.ds(row * 7 + col, 1), :] for row in range(7)]
                for source in range(TILE):
                    cells = wide[slab, source, pl.ds(5 + col, TILE), :]
                    for row in range(7):
                        target = source + 3 - row
                        if 0 <= target < TILE:
                            term = cells * taps[row]
                            sums[target] = term if sums[target] is None else sums[target] + term
            for target in range(TILE):
                conv[slab, pl.ds(target * TILE, TILE), :] = sums[target]
            return carry

        lax.fori_loop(0, slabs, one_slab, 0)
        width = slabs * LANES
        total = conv[0]
        for slab in range(1, slabs):
            total = total + conv[slab]
        mean = jnp.sum(total, axis=-1, keepdims=True) / width
        squares = None
        for slab in range(slabs):
            centred = conv[slab] - mean
            squares = centred * centred if squares is None else squares + centred * centred
        scale = lax.rsqrt(jnp.sum(squares, axis=-1, keepdims=True) / width + EPSILON)
        normed = jnp.concatenate(
            [
                ((conv[slab] - mean) * scale * param_ref[slab, pl.ds(49, 1), :]).astype(jnp.bfloat16)
                for slab in range(slabs)
            ],
            axis=1,
        )
        update = None
        step = 32
        for ref in (own_ref, other_ref):
            for chunk in range(0, ref.shape[0], step):
                into = ref[pl.ds(chunk, step), 0].reshape(step * 16, width)
                outof = ref[pl.ds(chunk, step), 1].reshape(step * 16, width)
                hidden = lax.dot_general(
                    normed, into, (((1,), (1,)), ((), ())), preferred_element_type=jnp.float32
                )
                hidden = jax.nn.gelu(hidden, approximate=True).astype(jnp.bfloat16)
                term = jnp.dot(hidden, outof, preferred_element_type=jnp.float32)
                update = term if update is None else update + term
        for slab in range(slabs):
            part = slice(slab * LANES, (slab + 1) * LANES)
            out_ref[:, part] = (
                tile_ref[:, part].astype(jnp.float32) + param_ref[slab, pl.ds(50, 1), :] * update[:, part]
            ).astype(jnp.bfloat16)


def detector_block(number, ints, tile, params, own, other):
    cells, width = tile.shape
    slabs = width // LANES
    return pl.pallas_call(
        functools.partial(block_body, number=number),
        out_shape=pltpu.VMEM(tile.shape, jnp.bfloat16),
        in_specs=[SMEM, VMEM, VMEM, VMEM, VMEM],
        out_specs=VMEM,
        scratch_shapes=[
            pltpu.VMEM((slabs, TILE, 32, LANES), jnp.float32),
            pltpu.VMEM((slabs, cells, LANES), jnp.float32),
        ],
        compiler_params=LIMITED,
        name="detector_block",
    )(ints, *map(resident, (tile, params, own, other)))


def selection(top, left):
    row = lax.broadcasted_iota(jnp.int32, (PADDED, CELLS), 0)
    cell = lax.broadcasted_iota(jnp.int32, (PADDED, CELLS), 1)
    crop_row = (row * 4682) >> 16
    wanted = (top + crop_row) * TILE + left + (row - crop_row * CROP)
    return jnp.where((cell == wanted) & (row < ROWS), 1.0, 0.0).astype(jnp.bfloat16)


def cut_body(ints_ref, tile_ref, *refs):
    out_refs, buffer, sems = refs[:3], refs[3], refs[4]
    base = ints_ref[SECTION_AT] * 9
    copies = []
    for turn in range(3):
        copies.append(
            pltpu.make_async_copy(tile_ref.at[ints_ref[base + 3 * turn]], buffer.at[turn], sems.at[turn])
        )
        copies[-1].start()
    for turn in range(3):
        chosen = selection(ints_ref[base + 3 * turn + 1], ints_ref[base + 3 * turn + 2])
        copies[turn].wait()
        rows = jnp.dot(chosen, buffer[turn], preferred_element_type=jnp.float32)
        out_refs[turn][...] = rows.astype(jnp.bfloat16)


def cut_pixels(ints, tiles):
    micro, cells, width = tiles.shape
    return pl.pallas_call(
        cut_body,
        out_shape=[pltpu.VMEM((PADDED, width), jnp.bfloat16)] * 3,
        in_specs=[SMEM, ANY],
        out_specs=[VMEM] * 3,
        scratch_shapes=[pltpu.VMEM((3, cells, width), jnp.bfloat16), pltpu.SemaphoreType.DMA((3,))],
        compiler_params=LIMITED,
        name="cut_pixels",
    )(ints, tiles)


def pick_body(ints_ref, below_ref, above_ref, *refs):
    tiles, out_refs = refs[:6], refs[6:]

    @pl.when(active(ints_ref, len(out_refs) - 1))
    def _():
        for slot, out_ref in enumerate(out_refs):
            source = ints_ref[SLOT_AT + slot]
            for number, (plan_ref, turn) in enumerate(((below_ref, 2), (ints_ref, 1), (above_ref, 0))):
                base = slot * 9 + turn * 3
                wanted = (source == number + 1) if number != 1 else ((source == 2) | (source == 0))
                for micro in range(2):

                    @pl.when(wanted & (plan_ref[base] == micro))
                    def _(plan_ref=plan_ref, base=base, tile=tiles[2 * number + micro], out_ref=out_ref):
                        chosen = selection(plan_ref[base + 1], plan_ref[base + 2])
                        rows = jnp.dot(chosen, tile[...], preferred_element_type=jnp.float32)
                        out_ref[...] = rows.astype(jnp.bfloat16)


def pick_crops(ints, below, above, tiles, slots):
    width = tiles[0].shape[1]
    return pl.pallas_call(
        pick_body,
        out_shape=[pltpu.VMEM((PADDED, width), jnp.bfloat16)] * slots,
        in_specs=[SMEM] * 3 + [VMEM] * len(tiles),
        out_specs=[VMEM] * slots,
        compiler_params=LIMITED,
        name="pick_crops",
    )(ints, below, above, *map(resident, tiles))


EMBED, MERGE, QUERY = 0, 1536, 2560
KEY, VALUE, OUT, POS, HALF = 0, 1024, 2048, 3072, 3584


def pack_body(parity_ref, embed, merge, pos, qkv, out, packed, buffer, sems):
    first = [
        (embed.at[:, pl.ds(0, LANES)], EMBED),
        (embed.at[:, pl.ds(LANES, LANES)], EMBED + 768),
        (merge.at[:, pl.ds(0, LANES)], MERGE),
        (merge.at[:, pl.ds(LANES, LANES)], MERGE + 512),
        (qkv.at[0], QUERY),
    ]
    second = [(qkv.at[1], KEY), (qkv.at[2], VALUE)]
    second += [(out.at[:, pl.ds(column * LANES, LANES)], OUT + column * LANES) for column in range(8)]
    second += [
        (pos.at[:, pl.ds(0, LANES)], POS),
        (pos.at[:, pl.ds(LANES, LANES)], POS + PADDED),
    ]
    for parity, pieces in enumerate((first, second)):

        @pl.when(parity_ref[0] == parity)
        def _(pieces=pieces):
            copies = [
                pltpu.make_async_copy(piece, buffer.at[pl.ds(at, piece.shape[0])], sems.at[number])
                for number, (piece, at) in enumerate(pieces)
            ]
            for copy in copies:
                copy.start()
            for copy in copies:
                copy.wait()

    result = pltpu.make_async_copy(buffer, packed, sems.at[12])
    result.start()
    result.wait()


def packed_half(parity, embed, merge, pos, qkv, out):
    return pl.pallas_call(
        pack_body,
        out_shape=jax.ShapeDtypeStruct((HALF, LANES), jnp.bfloat16),
        in_specs=[SMEM] + [ANY] * 5,
        out_specs=ANY,
        scratch_shapes=[pltpu.VMEM((HALF, LANES), jnp.bfloat16), pltpu.SemaphoreType.DMA((13,))],
        compiler_params=LIMITED,
        name="pack_weights",
    )(parity, *map(in_hbm, (embed, merge, pos, qkv, out)))


def columns(ref, section, low, height):
    return jnp.concatenate(
        [ref[section, pl.ds(low, height), :], ref[section, pl.ds(low + height, height), :]], axis=1
    )


def stage_body(ints_ref, pix_below, pix_own, pix_above, packed, weights, base_ref, pix, sems):
    source = ints_ref[SLOT_AT + ints_ref[SECTION_AT]]
    sections = packed.shape[0] // 2
    spans = [(0, EMBED, MERGE), (1, POS, HALF), (0, MERGE, HALF), (1, KEY, POS)]
    copies = []
    for part, low, high in spans:
        for section in range(sections):
            place = (2 * section + part, pl.ds(low, high - low))
            copies.append(
                pltpu.make_async_copy(packed.at[place], weights.at[place], sems.at[1 + len(copies)])
            )
    for number, pix_ref in enumerate((pix_below, pix_own, pix_above)):

        @pl.when((source == number + 1) if number != 1 else ((source == 2) | (source == 0)))
        def _(pix_ref=pix_ref):
            copy = pltpu.make_async_copy(pix_ref, pix, sems.at[0])
            copy.start()
            copy.wait()

    for copy in copies:
        copy.start()
    for copy in copies[: 2 * sections]:
        copy.wait()
    rows = pix[...]
    row_ok = lax.broadcasted_iota(jnp.int32, (PADDED, 2 * LANES), 0) < ROWS
    for section in range(sections):
        pos = jnp.where(row_ok, columns(weights, 2 * section + 1, POS, PADDED).astype(jnp.float32), 0.0)
        base_ref[:, pl.ds(section * 2 * LANES, 2 * LANES)] = pos + jnp.dot(
            rows, columns(weights, 2 * section, EMBED, 768), preferred_element_type=jnp.float32
        )
    for copy in copies[2 * sections :]:
        copy.wait()


def staged(ints, pixels, packed):
    width = LANES * packed.shape[0]
    return pl.pallas_call(
        stage_body,
        out_shape=[pltpu.VMEM(packed.shape, jnp.bfloat16), pltpu.VMEM((PADDED, width), jnp.float32)],
        in_specs=[SMEM] + [ANY] * 4,
        out_specs=[VMEM] * 2,
        scratch_shapes=[
            pltpu.VMEM(pixels[0].shape, jnp.bfloat16),
            pltpu.SemaphoreType.DMA((1 + 2 * packed.shape[0],)),
        ],
        compiler_params=LIMITED,
        name="stage_weights",
    )(ints, *map(in_hbm, (*pixels, packed)))


def classify_body(ints_ref, *refs):
    feat_refs = refs[:4]
    base_ref, weights, gain_ref, out_ref, feat = refs[4:]
    place = ints_ref[SECTION_AT]
    source = ints_ref[SLOT_AT + place]
    sections = weights.shape[0] // 2
    for number, feat_ref in enumerate(feat_refs):

        @pl.when(place == number)
        def _(feat_ref=feat_ref):
            feat[...] = feat_ref[...]

    feat_rows = feat[...]
    tokens = base_ref[...] + jnp.concatenate(
        [
            jnp.dot(feat_rows, columns(weights, 2 * section, MERGE, 512), preferred_element_type=jnp.float32)
            for section in range(sections)
        ],
        axis=1,
    )
    width = tokens.shape[1]
    mean = jnp.sum(tokens, axis=-1, keepdims=True) / width
    centred = tokens - mean
    var = jnp.sum(centred * centred, axis=-1, keepdims=True) / width
    attn_in = (centred * lax.rsqrt(var + EPSILON) * gain_ref[pl.ds(0, 1), :]).astype(jnp.bfloat16)
    token_sum = jnp.sum(tokens, axis=0, keepdims=True)
    key_ok = lax.broadcasted_iota(jnp.int32, (PADDED, PADDED), 1) < ROWS
    lane = lax.broadcasted_iota(jnp.int32, (PADDED, 2 * HEAD_DIM), 1)
    row_ok = lax.broadcasted_iota(jnp.int32, (PADDED, 2 * HEAD_DIM), 0) < ROWS
    context_sums = []
    for section in range(sections):
        first, second = 2 * section, 2 * section + 1
        piece = jnp.concatenate(
            [
                weights[first, pl.ds(QUERY, 1024), :],
                weights[second, pl.ds(KEY, 1024), :],
                weights[second, pl.ds(VALUE, 1024), :],
            ],
            axis=1,
        )
        qkv = jnp.dot(attn_in, piece, preferred_element_type=jnp.float32).astype(jnp.bfloat16)
        query, key, value = qkv[:, :128], qkv[:, 128:256], qkv[:, 256:]
        contexts = []
        for head in range(2):
            mine = (lane >= HEAD_DIM) if head else (lane < HEAD_DIM)
            scores = lax.dot_general(
                jnp.where(mine, query, jnp.zeros_like(query)),
                key,
                (((1,), (1,)), ((), ())),
                preferred_element_type=jnp.float32,
            ) * (1.0 / math.sqrt(HEAD_DIM))
            scores = jnp.where(key_ok, scores, -jnp.inf)
            top = jnp.max(scores, axis=-1, keepdims=True)
            numer = jnp.exp(scores - top)
            probs = (numer * (1.0 / jnp.sum(numer, axis=-1, keepdims=True))).astype(jnp.bfloat16)
            contexts.append(jnp.dot(probs, value, preferred_element_type=jnp.float32))
        context = jnp.where(lane < HEAD_DIM, contexts[0], contexts[1]).astype(jnp.bfloat16)
        context = jnp.where(row_ok, context.astype(jnp.float32), 0.0)
        context_sums.append(jnp.sum(context, axis=0, keepdims=True))
    context_mean = jnp.concatenate(context_sums, axis=1) / ROWS
    high = context_mean.astype(jnp.bfloat16)
    rest = context_mean - high.astype(jnp.float32)
    middle = rest.astype(jnp.bfloat16)
    low = (rest - middle.astype(jnp.float32)).astype(jnp.bfloat16)
    pieces = jnp.concatenate([high, middle, low, jnp.zeros((13, high.shape[1]), jnp.bfloat16)], axis=0)
    out_weight = jnp.concatenate(
        [
            jnp.concatenate(
                [weights[2 * section + 1, pl.ds(OUT + LANES * column, LANES), :] for column in range(8)], axis=1
            )
            for section in range(sections)
        ],
        axis=0,
    )
    mixed = jnp.dot(pieces, out_weight, preferred_element_type=jnp.float32)
    pooled = token_sum / ROWS + jnp.sum(mixed, axis=0, keepdims=True)
    pooled_mean = jnp.sum(pooled, axis=-1, keepdims=True) / width
    centred = pooled - pooled_mean
    var = jnp.sum(centred * centred, axis=-1, keepdims=True) / width
    result = centred * lax.rsqrt(var + EPSILON) * gain_ref[pl.ds(1, 1), :]
    out_ref[...] = jnp.where(source == 0, 0.0, result)


def classify(ints, feats, base, weights, gain):
    return pl.pallas_call(
        classify_body,
        out_shape=jax.ShapeDtypeStruct((1, gain.shape[1]), jnp.float32),
        in_specs=[SMEM] + [VMEM] * 7,
        out_specs=VMEM,
        scratch_shapes=[pltpu.VMEM(feats[0].shape, jnp.bfloat16)],
        compiler_params=LIMITED,
        name="classify",
    )(ints, *map(resident, (*feats, base, weights, gain)))


def after(value, *others):
    return lax.optimization_barrier((value,) + others)[0]


def per_device(
    tile_features,
    patches,
    det_kernel,
    det_gain,
    det_in,
    det_out,
    det_scale,
    cls_embed,
    cls_merge,
    cls_pos,
    cls_qkv,
    cls_out,
    cls_gain,
    crop_plan,
    slot_from,
):
    sections = lax.axis_size("section")
    count = lax.axis_size(REP)
    section = lax.axis_index("section").astype(jnp.int32)
    parity = (lax.axis_index(REP) % 2).astype(jnp.int32).reshape(1)
    width = tile_features.shape[3]
    slabs = width // LANES
    last = sections - 1
    upward = [(index, index + 1) for index in range(count - 1)]
    downward = [(target, origin) for origin, target in upward]
    swap = [(index, index ^ 1) for index in range(count)]
    ints = jnp.concatenate([crop_plan.reshape(-1), slot_from.reshape(-1), section.reshape(1)])

    half = packed_half(parity, cls_embed, cls_merge, cls_pos, cls_qkv.transpose(1, 0, 2), cls_out)
    weights = lax.all_gather(half, ("section", "core"), axis=0)

    shard = jnp.stack([det_in[0].T, det_out[0]], axis=0)
    line = spread_in_groups(shard, line_groups(True))
    plane = spread_in_groups(after(line, half), line_groups(False))
    cut = cut_pixels(ints, patches.reshape(2, CELLS, patches.shape[3]))
    pixels = (lax.ppermute(cut[2], REP, upward), cut[1], lax.ppermute(cut[0], REP, downward))
    below = lax.ppermute(ints, REP, upward)
    above = lax.ppermute(ints, REP, downward)
    params = jnp.concatenate(
        [det_kernel[0].reshape(49, width), det_gain, det_scale, jnp.zeros((5, width), jnp.float32)], axis=0
    )
    params = params.reshape(56, slabs, LANES).transpose(1, 0, 2)
    plane = after(plane, below, above, params, *pixels)
    own = plane.reshape((SIDE * SIDE,) + shard.shape)
    other = lax.ppermute(own, REP, swap)

    start = tile_features.reshape(2, CELLS, width)
    tiles = [start[0], start[1]]
    for number in range(sections):
        done = [detector_block(number, ints, tile, params, own, other) for tile in tiles]
        if number < last:
            tiles = [lax.ppermute(tile, "section", [(number, number + 1)]) for tile in done]

    along = [(last * count + origin, last * count + target) for origin, target in upward]
    back = [(target, origin) for origin, target in along]
    from_below = [lax.ppermute(tile, ("section",) + REP, along) for tile in done]
    from_above = [lax.ppermute(tile, ("section",) + REP, back) for tile in done]
    crops = pick_crops(after(ints, weights), below, above, from_below + done + from_above, sections)
    feats = [lax.ppermute(crops[slot], "section", [(last, slot)]) for slot in range(last)] + [crops[last]]
    weights, base = staged(after(ints, *crops), pixels, weights)
    result = classify(ints, feats, base, weights, cls_gain)
    return result[None]


def solution(mesh):
    sections = mesh.shape["section"]
    fine = jax.sharding.Mesh(mesh.devices.reshape(sections, SIDE, SIDE, 2), ("section",) + REP)
    return jax.shard_map(
        per_device,
        mesh=fine,
        in_specs=(
            P(REP, None, None, None),
            P(REP, None, None, None),
            P("section", None, None, None),
            P("section", None),
            P("section", None, REP),
            P("section", REP, None),
            P("section", None),
            P(None, "section"),
            P(None, "section"),
            P(None, "section"),
            P(None, None, "section"),
            P("section", None),
            P(),
            P(REP, None, None, None),
            P(REP, None),
        ),
        out_specs=P(REP, "section", None),
        check_vma=False,
    )
```

```python
import functools
import math

import jax
import jax.numpy as jnp
from jax import lax
from jax.experimental import pallas as pl
from jax.experimental.pallas import tpu as pltpu
from jax.sharding import PartitionSpec as P

HEAD_DIM = 64
TILE = 16
CELLS = TILE * TILE
CROP = 14
ROWS = CROP * CROP
PADDED = 208
LANES = 128
SIDE = 8
REP = ("y", "z", "core")
EPSILON = 1e-06
SLOT_AT = 36
SECTION_AT = 40
CORE_AT = 41

ANY = pl.BlockSpec(memory_space=pl.ANY)
SMEM = pl.BlockSpec(memory_space=pltpu.SMEM)
VMEM = pl.BlockSpec(memory_space=pltpu.VMEM)
LIMITED = pltpu.CompilerParams(vmem_limit_bytes=16 << 20)


def rep_index(y, z, core):
    return (y * SIDE + z) * 2 + core


def line_groups(first):
    along_z = [[rep_index(y, z, 0 if first else 1) for z in range(SIDE)] for y in range(SIDE)]
    along_y = [[rep_index(y, z, 1 if first else 0) for y in range(SIDE)] for z in range(SIDE)]
    return along_z + along_y


def spread_in_groups(block, groups):
    copies = jnp.broadcast_to(block[None], (SIDE,) + block.shape)
    return lax.all_to_all(copies, REP, 0, 0, axis_index_groups=groups)


def resident(array):
    return pltpu.with_memory_space_constraint(array, pltpu.VMEM)


def in_hbm(array):
    return pltpu.with_memory_space_constraint(array, pltpu.HBM)


def active(ints_ref, number):
    return ints_ref[SECTION_AT] == number


def conv_norm(tile_ref, param_ref, normed_ref, wide, conv):
    slabs = wide.shape[0]
    wide[:, :, 0:8, :] = jnp.zeros((slabs, TILE, 8, LANES), jnp.float32)
    wide[:, :, 24:32, :] = jnp.zeros((slabs, TILE, 8, LANES), jnp.float32)
    for slab in range(slabs):
        part = tile_ref[:, slab * LANES : (slab + 1) * LANES].astype(jnp.float32)
        wide[slab, :, 8:24, :] = part.reshape(TILE, TILE, LANES)

    def one_slab(slab, carry):
        sums = [None] * TILE
        for col in range(7):
            taps = [param_ref[slab, pl.ds(row * 7 + col, 1), :] for row in range(7)]
            for source in range(TILE):
                cells = wide[slab, source, pl.ds(5 + col, TILE), :]
                for row in range(7):
                    target = source + 3 - row
                    if 0 <= target < TILE:
                        term = cells * taps[row]
                        sums[target] = term if sums[target] is None else sums[target] + term
        for target in range(TILE):
            conv[slab, pl.ds(target * TILE, TILE), :] = sums[target]
        return carry

    lax.fori_loop(0, slabs, one_slab, 0)
    width = slabs * LANES
    total = conv[0]
    for slab in range(1, slabs):
        total = total + conv[slab]
    mean = jnp.sum(total, axis=-1, keepdims=True) / width
    squares = None
    for slab in range(slabs):
        centred = conv[slab] - mean
        squares = centred * centred if squares is None else squares + centred * centred
    scale = lax.rsqrt(jnp.sum(squares, axis=-1, keepdims=True) / width + EPSILON)
    for slab in range(slabs):
        normed_ref[:, slab * LANES : (slab + 1) * LANES] = (
            (conv[slab] - mean) * scale * param_ref[slab, pl.ds(49, 1), :]
        ).astype(jnp.bfloat16)


def early_body(ints_ref, tile_ref, param_ref, normed_ref, wide, conv):
    @pl.when(active(ints_ref, 0) & (ints_ref[CORE_AT] == 0))
    def _():
        conv_norm(tile_ref, param_ref, normed_ref, wide, conv)


def conv_scratch(tile):
    cells, width = tile.shape
    slabs = width // LANES
    return [
        pltpu.VMEM((slabs, TILE, 32, LANES), jnp.float32),
        pltpu.VMEM((slabs, cells, LANES), jnp.float32),
    ]


def early_norm(ints, tile, params):
    return pl.pallas_call(
        early_body,
        out_shape=pltpu.VMEM(tile.shape, jnp.bfloat16),
        in_specs=[SMEM, VMEM, VMEM],
        out_specs=VMEM,
        scratch_shapes=conv_scratch(tile),
        compiler_params=LIMITED,
        name="early_norm",
    )(ints, resident(tile), resident(params))


def block_body(ints_ref, tile_ref, param_ref, own_ref, other_ref, *refs, number):
    early_refs, (out_ref, normed, wide, conv) = refs[:-4], refs[-4:]

    @pl.when(active(ints_ref, number))
    def _():
        if early_refs:

            @pl.when(ints_ref[CORE_AT] == 0)
            def _():
                normed[...] = early_refs[0][...]

            @pl.when(ints_ref[CORE_AT] == 1)
            def _():
                conv_norm(tile_ref, param_ref, normed, wide, conv)

        else:
            conv_norm(tile_ref, param_ref, normed, wide, conv)
        slabs = wide.shape[0]
        width = slabs * LANES
        rows = normed[...]
        update = None
        step = 32
        for ref in (own_ref, other_ref):
            for chunk in range(0, ref.shape[0], step):
                into = ref[pl.ds(chunk, step), 0].reshape(step * 16, width)
                outof = ref[pl.ds(chunk, step), 1].reshape(step * 16, width)
                hidden = lax.dot_general(
                    rows, into, (((1,), (1,)), ((), ())), preferred_element_type=jnp.float32
                )
                hidden = jax.nn.gelu(hidden, approximate=True).astype(jnp.bfloat16)
                term = jnp.dot(hidden, outof, preferred_element_type=jnp.float32)
                update = term if update is None else update + term
        for slab in range(slabs):
            part = slice(slab * LANES, (slab + 1) * LANES)
            out_ref[:, part] = (
                tile_ref[:, part].astype(jnp.float32) + param_ref[slab, pl.ds(50, 1), :] * update[:, part]
            ).astype(jnp.bfloat16)


def detector_block(number, ints, tile, params, own, other, *early):
    return pl.pallas_call(
        functools.partial(block_body, number=number),
        out_shape=pltpu.VMEM(tile.shape, jnp.bfloat16),
        in_specs=[SMEM] + [VMEM] * (4 + len(early)),
        out_specs=VMEM,
        scratch_shapes=[pltpu.VMEM(tile.shape, jnp.bfloat16)] + conv_scratch(tile),
        compiler_params=LIMITED,
        name="detector_block",
    )(ints, *map(resident, (tile, params, own, other, *early)))


def selection(top, left):
    row = lax.broadcasted_iota(jnp.int32, (PADDED, CELLS), 0)
    cell = lax.broadcasted_iota(jnp.int32, (PADDED, CELLS), 1)
    crop_row = (row * 4682) >> 16
    wanted = (top + crop_row) * TILE + left + (row - crop_row * CROP)
    return jnp.where((cell == wanted) & (row < ROWS), 1.0, 0.0).astype(jnp.bfloat16)


def cut_body(ints_ref, tile_ref, *refs):
    out_refs, buffer, sems = refs[:3], refs[3], refs[4]
    base = ints_ref[SECTION_AT] * 9
    copies = []
    for turn in range(3):
        copies.append(
            pltpu.make_async_copy(tile_ref.at[ints_ref[base + 3 * turn]], buffer.at[turn], sems.at[turn])
        )
        copies[-1].start()
    for turn in range(3):
        chosen = selection(ints_ref[base + 3 * turn + 1], ints_ref[base + 3 * turn + 2])
        copies[turn].wait()
        rows = jnp.dot(chosen, buffer[turn], preferred_element_type=jnp.float32)
        out_refs[turn][...] = rows.astype(jnp.bfloat16)


def cut_pixels(ints, tiles):
    micro, cells, width = tiles.shape
    return pl.pallas_call(
        cut_body,
        out_shape=[pltpu.VMEM((PADDED, width), jnp.bfloat16)] * 3,
        in_specs=[SMEM, ANY],
        out_specs=[VMEM] * 3,
        scratch_shapes=[pltpu.VMEM((3, cells, width), jnp.bfloat16), pltpu.SemaphoreType.DMA((3,))],
        compiler_params=LIMITED,
        name="cut_pixels",
    )(ints, tiles)


def pick_body(ints_ref, below_ref, above_ref, *refs):
    tiles, out_refs = refs[:6], refs[6:]

    @pl.when(active(ints_ref, len(out_refs) - 1))
    def _():
        core = ints_ref[CORE_AT]
        for slot, out_ref in enumerate(out_refs):
            source = ints_ref[SLOT_AT + slot]
            base = slot * 9

            def entry(part, source=source, base=base):
                inner = jnp.where(source == 3, above_ref[base + part], ints_ref[base + 3 + part])
                return jnp.where(source == 1, below_ref[base + 6 + part], inner)

            same_chip = ((source == 1) & (core == 1)) | ((source == 3) & (core == 0))
            away = (source == 1) | (source == 3)
            micro = entry(0)
            chosen = selection(entry(1), entry(2))
            for number, wanted in enumerate((same_chip, ~away, away & ~same_chip)):
                for index in range(2):

                    @pl.when(wanted & (micro == index))
                    def _(chosen=chosen, tile=tiles[2 * number + index], out_ref=out_ref):
                        rows = jnp.dot(chosen, tile[...], preferred_element_type=jnp.float32)
                        out_ref[...] = rows.astype(jnp.bfloat16)


def pick_crops(ints, below, above, tiles, slots):
    width = tiles[0].shape[1]
    return pl.pallas_call(
        pick_body,
        out_shape=[pltpu.VMEM((PADDED, width), jnp.bfloat16)] * slots,
        in_specs=[SMEM] * 3 + [VMEM] * len(tiles),
        out_specs=[VMEM] * slots,
        compiler_params=LIMITED,
        name="pick_crops",
    )(ints, below, above, *map(resident, tiles))


EMBED, MERGE, QUERY = 0, 1536, 2560
KEY, VALUE, OUT, POS, HALF = 0, 1024, 2048, 3072, 3584


def pack_body(parity_ref, embed, merge, pos, qkv, out, packed, buffer, sems):
    first = [
        (embed.at[:, pl.ds(0, LANES)], EMBED),
        (embed.at[:, pl.ds(LANES, LANES)], EMBED + 768),
        (merge.at[:, pl.ds(0, LANES)], MERGE),
        (merge.at[:, pl.ds(LANES, LANES)], MERGE + 512),
        (qkv.at[0], QUERY),
    ]
    second = [(qkv.at[1], KEY), (qkv.at[2], VALUE)]
    second += [(out.at[:, pl.ds(column * LANES, LANES)], OUT + column * LANES) for column in range(8)]
    second += [
        (pos.at[:, pl.ds(0, LANES)], POS),
        (pos.at[:, pl.ds(LANES, LANES)], POS + PADDED),
    ]
    for parity, pieces in enumerate((first, second)):

        @pl.when(parity_ref[0] == parity)
        def _(pieces=pieces):
            copies = [
                pltpu.make_async_copy(piece, buffer.at[pl.ds(at, piece.shape[0])], sems.at[number])
                for number, (piece, at) in enumerate(pieces)
            ]
            for copy in copies:
                copy.start()
            for copy in copies:
                copy.wait()

    result = pltpu.make_async_copy(buffer, packed, sems.at[12])
    result.start()
    result.wait()


def packed_half(parity, embed, merge, pos, qkv, out):
    return pl.pallas_call(
        pack_body,
        out_shape=jax.ShapeDtypeStruct((HALF, LANES), jnp.bfloat16),
        in_specs=[SMEM] + [ANY] * 5,
        out_specs=ANY,
        scratch_shapes=[pltpu.VMEM((HALF, LANES), jnp.bfloat16), pltpu.SemaphoreType.DMA((13,))],
        compiler_params=LIMITED,
        name="pack_weights",
    )(parity, *map(in_hbm, (embed, merge, pos, qkv, out)))


def columns(ref, section, low, height):
    return jnp.concatenate(
        [ref[section, pl.ds(low, height), :], ref[section, pl.ds(low + height, height), :]], axis=1
    )


def stage_body(ints_ref, pix_below, pix_own, pix_above, packed, weights, base_ref, pix, sems):
    source = ints_ref[SLOT_AT + ints_ref[SECTION_AT]]
    sections = packed.shape[0] // 2
    spans = [(0, EMBED, MERGE), (1, POS, HALF), (0, MERGE, HALF), (1, KEY, POS)]
    copies = []
    for part, low, high in spans:
        for section in range(sections):
            place = (2 * section + part, pl.ds(low, high - low))
            copies.append(
                pltpu.make_async_copy(packed.at[place], weights.at[place], sems.at[1 + len(copies)])
            )
    for number, pix_ref in enumerate((pix_below, pix_own, pix_above)):

        @pl.when((source == number + 1) if number != 1 else ((source == 2) | (source == 0)))
        def _(pix_ref=pix_ref):
            copy = pltpu.make_async_copy(pix_ref, pix, sems.at[0])
            copy.start()
            copy.wait()

    for copy in copies:
        copy.start()
    for copy in copies[: 2 * sections]:
        copy.wait()
    rows = pix[...]
    row_ok = lax.broadcasted_iota(jnp.int32, (PADDED, 2 * LANES), 0) < ROWS
    for section in range(sections):
        pos = jnp.where(row_ok, columns(weights, 2 * section + 1, POS, PADDED).astype(jnp.float32), 0.0)
        base_ref[:, pl.ds(section * 2 * LANES, 2 * LANES)] = pos + jnp.dot(
            rows, columns(weights, 2 * section, EMBED, 768), preferred_element_type=jnp.float32
        )
    for copy in copies[2 * sections :]:
        copy.wait()


def staged(ints, pixels, packed):
    width = LANES * packed.shape[0]
    return pl.pallas_call(
        stage_body,
        out_shape=[pltpu.VMEM(packed.shape, jnp.bfloat16), pltpu.VMEM((PADDED, width), jnp.float32)],
        in_specs=[SMEM] + [ANY] * 4,
        out_specs=[VMEM] * 2,
        scratch_shapes=[
            pltpu.VMEM(pixels[0].shape, jnp.bfloat16),
            pltpu.SemaphoreType.DMA((1 + 2 * packed.shape[0],)),
        ],
        compiler_params=LIMITED,
        name="stage_weights",
    )(ints, *map(in_hbm, (*pixels, packed)))


def classify_body(ints_ref, *refs):
    feat_refs = refs[:4]
    base_ref, weights, gain_ref, out_ref, feat = refs[4:]
    place = ints_ref[SECTION_AT]
    source = ints_ref[SLOT_AT + place]
    sections = weights.shape[0] // 2
    for number, feat_ref in enumerate(feat_refs):

        @pl.when(place == number)
        def _(feat_ref=feat_ref):
            feat[...] = feat_ref[...]

    feat_rows = feat[...]
    tokens = base_ref[...] + jnp.concatenate(
        [
            jnp.dot(feat_rows, columns(weights, 2 * section, MERGE, 512), preferred_element_type=jnp.float32)
            for section in range(sections)
        ],
        axis=1,
    )
    width = tokens.shape[1]
    mean = jnp.sum(tokens, axis=-1, keepdims=True) / width
    centred = tokens - mean
    var = jnp.sum(centred * centred, axis=-1, keepdims=True) / width
    attn_in = (centred * lax.rsqrt(var + EPSILON) * gain_ref[pl.ds(0, 1), :]).astype(jnp.bfloat16)
    token_sum = jnp.sum(tokens, axis=0, keepdims=True)
    key_ok = lax.broadcasted_iota(jnp.int32, (PADDED, PADDED), 1) < ROWS
    lane = lax.broadcasted_iota(jnp.int32, (PADDED, 2 * HEAD_DIM), 1)
    row_ok = lax.broadcasted_iota(jnp.int32, (PADDED, 2 * HEAD_DIM), 0) < ROWS
    context_sums = []
    for section in range(sections):
        first, second = 2 * section, 2 * section + 1
        piece = jnp.concatenate(
            [
                weights[first, pl.ds(QUERY, 1024), :],
                weights[second, pl.ds(KEY, 1024), :],
                weights[second, pl.ds(VALUE, 1024), :],
            ],
            axis=1,
        )
        qkv = jnp.dot(attn_in, piece, preferred_element_type=jnp.float32).astype(jnp.bfloat16)
        query, key, value = qkv[:, :128], qkv[:, 128:256], qkv[:, 256:]
        contexts = []
        for head in range(2):
            mine = (lane >= HEAD_DIM) if head else (lane < HEAD_DIM)
            scores = lax.dot_general(
                jnp.where(mine, query, jnp.zeros_like(query)),
                key,
                (((1,), (1,)), ((), ())),
                preferred_element_type=jnp.float32,
            ) * (1.0 / math.sqrt(HEAD_DIM))
            scores = jnp.where(key_ok, scores, -jnp.inf)
            top = jnp.max(scores, axis=-1, keepdims=True)
            numer = jnp.exp(scores - top)
            probs = (numer * (1.0 / jnp.sum(numer, axis=-1, keepdims=True))).astype(jnp.bfloat16)
            contexts.append(jnp.dot(probs, value, preferred_element_type=jnp.float32))
        context = jnp.where(lane < HEAD_DIM, contexts[0], contexts[1]).astype(jnp.bfloat16)
        context = jnp.where(row_ok, context.astype(jnp.float32), 0.0)
        context_sums.append(jnp.sum(context, axis=0, keepdims=True))
    context_mean = jnp.concatenate(context_sums, axis=1) / ROWS
    high = context_mean.astype(jnp.bfloat16)
    rest = context_mean - high.astype(jnp.float32)
    middle = rest.astype(jnp.bfloat16)
    low = (rest - middle.astype(jnp.float32)).astype(jnp.bfloat16)
    pieces = jnp.concatenate([high, middle, low, jnp.zeros((13, high.shape[1]), jnp.bfloat16)], axis=0)
    out_weight = jnp.concatenate(
        [
            jnp.concatenate(
                [weights[2 * section + 1, pl.ds(OUT + LANES * column, LANES), :] for column in range(8)], axis=1
            )
            for section in range(sections)
        ],
        axis=0,
    )
    mixed = jnp.dot(pieces, out_weight, preferred_element_type=jnp.float32)
    pooled = token_sum / ROWS + jnp.sum(mixed, axis=0, keepdims=True)
    pooled_mean = jnp.sum(pooled, axis=-1, keepdims=True) / width
    centred = pooled - pooled_mean
    var = jnp.sum(centred * centred, axis=-1, keepdims=True) / width
    result = centred * lax.rsqrt(var + EPSILON) * gain_ref[pl.ds(1, 1), :]
    out_ref[...] = jnp.where(source == 0, 0.0, result)


def classify(ints, feats, base, weights, gain):
    return pl.pallas_call(
        classify_body,
        out_shape=jax.ShapeDtypeStruct((1, gain.shape[1]), jnp.float32),
        in_specs=[SMEM] + [VMEM] * 7,
        out_specs=VMEM,
        scratch_shapes=[pltpu.VMEM(feats[0].shape, jnp.bfloat16)],
        compiler_params=LIMITED,
        name="classify",
    )(ints, *map(resident, (*feats, base, weights, gain)))


def after(value, *others):
    return lax.optimization_barrier((value,) + others)[0]


def per_device(
    tile_features,
    patches,
    det_kernel,
    det_gain,
    det_in,
    det_out,
    det_scale,
    cls_embed,
    cls_merge,
    cls_pos,
    cls_qkv,
    cls_out,
    cls_gain,
    crop_plan,
    slot_from,
):
    sections = lax.axis_size("section")
    count = lax.axis_size(REP)
    section = lax.axis_index("section").astype(jnp.int32)
    core = lax.axis_index("core").astype(jnp.int32)
    width = tile_features.shape[3]
    slabs = width // LANES
    last = sections - 1
    upward = [(index, index + 1) for index in range(count - 1)]
    downward = [(target, origin) for origin, target in upward]
    swap = [(index, index ^ 1) for index in range(count)]
    ints = jnp.concatenate([crop_plan.reshape(-1), slot_from.reshape(-1), section.reshape(1), core.reshape(1)])

    half = packed_half(core.reshape(1), cls_embed, cls_merge, cls_pos, cls_qkv.transpose(1, 0, 2), cls_out)
    weights = lax.all_gather(half, ("section", "core"), axis=0)

    shard = jnp.stack([det_in[0].T, det_out[0]], axis=0)
    line = spread_in_groups(shard, line_groups(True))
    plane = spread_in_groups(after(line, half), line_groups(False))
    cut = cut_pixels(ints, patches.reshape(2, CELLS, patches.shape[3]))
    pixels = (lax.ppermute(cut[2], REP, upward), cut[1], lax.ppermute(cut[0], REP, downward))
    below = lax.ppermute(ints, REP, upward)
    above = lax.ppermute(ints, REP, downward)
    params = jnp.concatenate(
        [det_kernel[0].reshape(49, width), det_gain, det_scale, jnp.zeros((5, width), jnp.float32)], axis=0
    )
    params = params.reshape(56, slabs, LANES).transpose(1, 0, 2)
    start = tile_features.reshape(2, CELLS, width)
    tiles = [start[0], start[1]]
    early = early_norm(ints, tiles[0], params)
    plane = after(plane, below, above, early, *pixels)
    own = plane.reshape((SIDE * SIDE,) + shard.shape)
    other = lax.ppermute(own, REP, swap)

    for number in range(sections):
        ahead = [(early,), ()] if number == 0 else [(), ()]
        done = [
            detector_block(number, ints, tile, params, own, other, *more) for tile, more in zip(tiles, ahead)
        ]
        if number < last:
            tiles = [lax.ppermute(tile, "section", [(number, number + 1)]) for tile in done]

    within = [(last * count + origin, last * count + target) for origin, target in swap]
    across = [(last * count + index, last * count + index + 1) for index in range(1, count - 1, 2)]
    across += [(target, origin) for origin, target in across]
    near = [lax.ppermute(tile, ("section",) + REP, within) for tile in done]
    far = [lax.ppermute(tile, ("section",) + REP, across) for tile in done]
    crops = pick_crops(after(ints, weights), below, above, near + done + far, sections)
    feats = [lax.ppermute(crops[slot], "section", [(last, slot)]) for slot in range(last)] + [crops[last]]
    weights, base = staged(after(ints, *crops), pixels, weights)
    result = classify(ints, feats, base, weights, cls_gain)
    return result[None]


def solution(mesh):
    sections = mesh.shape["section"]
    fine = jax.sharding.Mesh(mesh.devices.reshape(sections, SIDE, SIDE, 2), ("section",) + REP)
    return jax.shard_map(
        per_device,
        mesh=fine,
        in_specs=(
            P(REP, None, None, None),
            P(REP, None, None, None),
            P("section", None, None, None),
            P("section", None),
            P("section", None, REP),
            P("section", REP, None),
            P("section", None),
            P(None, "section"),
            P(None, "section"),
            P(None, "section"),
            P(None, None, "section"),
            P("section", None),
            P(),
            P(REP, None, None, None),
            P(REP, None),
        ),
        out_specs=P(REP, "section", None),
        check_vma=False,
    )
```

```python
import functools
import math

import jax
import jax.numpy as jnp
from jax import lax
from jax.experimental import pallas as pl
from jax.experimental.pallas import tpu as pltpu
from jax.sharding import PartitionSpec as P

HEAD_DIM = 64
TILE = 16
CELLS = TILE * TILE
CROP = 14
ROWS = CROP * CROP
PADDED = 208
LANES = 128
SIDE = 8
REP = ("y", "z", "core")
EPSILON = 1e-06
SLOT_AT = 36
SECTION_AT = 40
CORE_AT = 41

ANY = pl.BlockSpec(memory_space=pl.ANY)
SMEM = pl.BlockSpec(memory_space=pltpu.SMEM)
VMEM = pl.BlockSpec(memory_space=pltpu.VMEM)
LIMITED = pltpu.CompilerParams(vmem_limit_bytes=16 << 20)


def rep_index(y, z, core):
    return (y * SIDE + z) * 2 + core


def line_groups(first):
    along_z = [[rep_index(y, z, 0 if first else 1) for z in range(SIDE)] for y in range(SIDE)]
    along_y = [[rep_index(y, z, 1 if first else 0) for y in range(SIDE)] for z in range(SIDE)]
    return along_z + along_y


def spread_in_groups(block, groups):
    copies = jnp.broadcast_to(block[None], (SIDE,) + block.shape)
    return lax.all_to_all(copies, REP, 0, 0, axis_index_groups=groups)


def resident(array):
    return pltpu.with_memory_space_constraint(array, pltpu.VMEM)


def in_hbm(array):
    return pltpu.with_memory_space_constraint(array, pltpu.HBM)


def active(ints_ref, number):
    return ints_ref[SECTION_AT] == number


def conv_norm(tile_ref, param_ref, normed_ref, wide, conv):
    slabs = wide.shape[0]
    wide[:, :, 0:8, :] = jnp.zeros((slabs, TILE, 8, LANES), jnp.float32)
    wide[:, :, 24:32, :] = jnp.zeros((slabs, TILE, 8, LANES), jnp.float32)
    for slab in range(slabs):
        part = tile_ref[:, slab * LANES : (slab + 1) * LANES].astype(jnp.float32)
        wide[slab, :, 8:24, :] = part.reshape(TILE, TILE, LANES)

    def one_slab(slab, carry):
        sums = [None] * TILE
        for col in range(7):
            taps = [param_ref[slab, pl.ds(row * 7 + col, 1), :] for row in range(7)]
            for source in range(TILE):
                cells = wide[slab, source, pl.ds(5 + col, TILE), :]
                for row in range(7):
                    target = source + 3 - row
                    if 0 <= target < TILE:
                        term = cells * taps[row]
                        sums[target] = term if sums[target] is None else sums[target] + term
        for target in range(TILE):
            conv[slab, pl.ds(target * TILE, TILE), :] = sums[target]
        return carry

    lax.fori_loop(0, slabs, one_slab, 0)
    width = slabs * LANES
    total = conv[0]
    for slab in range(1, slabs):
        total = total + conv[slab]
    mean = jnp.sum(total, axis=-1, keepdims=True) / width
    squares = None
    for slab in range(slabs):
        centred = conv[slab] - mean
        squares = centred * centred if squares is None else squares + centred * centred
    scale = lax.rsqrt(jnp.sum(squares, axis=-1, keepdims=True) / width + EPSILON)
    for slab in range(slabs):
        normed_ref[:, slab * LANES : (slab + 1) * LANES] = (
            (conv[slab] - mean) * scale * param_ref[slab, pl.ds(49, 1), :]
        ).astype(jnp.bfloat16)


def early_body(ints_ref, tile_ref, param_ref, normed_ref, wide, conv):
    @pl.when(active(ints_ref, 0) & (ints_ref[CORE_AT] == 0))
    def _():
        conv_norm(tile_ref, param_ref, normed_ref, wide, conv)


def conv_scratch(tile):
    cells, width = tile.shape
    slabs = width // LANES
    return [
        pltpu.VMEM((slabs, TILE, 32, LANES), jnp.float32),
        pltpu.VMEM((slabs, cells, LANES), jnp.float32),
    ]


def early_norm(ints, tile, params):
    return pl.pallas_call(
        early_body,
        out_shape=pltpu.VMEM(tile.shape, jnp.bfloat16),
        in_specs=[SMEM, VMEM, VMEM],
        out_specs=VMEM,
        scratch_shapes=conv_scratch(tile),
        compiler_params=LIMITED,
        name="early_norm",
    )(ints, resident(tile), resident(params))


def block_body(ints_ref, tile_ref, param_ref, own_ref, other_ref, *refs, number):
    early_refs, (out_ref, normed, wide, conv) = refs[:-4], refs[-4:]

    @pl.when(active(ints_ref, number))
    def _():
        if early_refs:

            @pl.when(ints_ref[CORE_AT] == 0)
            def _():
                normed[...] = early_refs[0][...]

            @pl.when(ints_ref[CORE_AT] == 1)
            def _():
                conv_norm(tile_ref, param_ref, normed, wide, conv)

        else:
            conv_norm(tile_ref, param_ref, normed, wide, conv)
        slabs = wide.shape[0]
        width = slabs * LANES
        rows = normed[...]
        update = None
        step = 32
        for ref in (own_ref, other_ref):
            for chunk in range(0, ref.shape[0], step):
                into = ref[pl.ds(chunk, step), 0].reshape(step * 16, width)
                outof = ref[pl.ds(chunk, step), 1].reshape(step * 16, width)
                hidden = lax.dot_general(
                    rows, into, (((1,), (1,)), ((), ())), preferred_element_type=jnp.float32
                )
                hidden = jax.nn.gelu(hidden, approximate=True).astype(jnp.bfloat16)
                term = jnp.dot(hidden, outof, preferred_element_type=jnp.float32)
                update = term if update is None else update + term
        for slab in range(slabs):
            part = slice(slab * LANES, (slab + 1) * LANES)
            out_ref[:, part] = (
                tile_ref[:, part].astype(jnp.float32) + param_ref[slab, pl.ds(50, 1), :] * update[:, part]
            ).astype(jnp.bfloat16)


def detector_block(number, ints, tile, params, own, other, *early):
    return pl.pallas_call(
        functools.partial(block_body, number=number),
        out_shape=pltpu.VMEM(tile.shape, jnp.bfloat16),
        in_specs=[SMEM] + [VMEM] * (4 + len(early)),
        out_specs=VMEM,
        scratch_shapes=[pltpu.VMEM(tile.shape, jnp.bfloat16)] + conv_scratch(tile),
        compiler_params=LIMITED,
        name="detector_block",
    )(ints, *map(resident, (tile, params, own, other, *early)))


def selection(top, left):
    row = lax.broadcasted_iota(jnp.int32, (PADDED, CELLS), 0)
    cell = lax.broadcasted_iota(jnp.int32, (PADDED, CELLS), 1)
    crop_row = (row * 4682) >> 16
    wanted = (top + crop_row) * TILE + left + (row - crop_row * CROP)
    return jnp.where((cell == wanted) & (row < ROWS), 1.0, 0.0).astype(jnp.bfloat16)


def cut_body(ints_ref, tile_ref, *refs):
    out_refs, buffer, sems = refs[:3], refs[3], refs[4]
    base = ints_ref[SECTION_AT] * 9
    copies = []
    for turn in range(3):
        copies.append(
            pltpu.make_async_copy(tile_ref.at[ints_ref[base + 3 * turn]], buffer.at[turn], sems.at[turn])
        )
        copies[-1].start()
    for turn in range(3):
        chosen = selection(ints_ref[base + 3 * turn + 1], ints_ref[base + 3 * turn + 2])
        copies[turn].wait()
        rows = jnp.dot(chosen, buffer[turn], preferred_element_type=jnp.float32)
        out_refs[turn][...] = rows.astype(jnp.bfloat16)


def cut_pixels(ints, tiles):
    micro, cells, width = tiles.shape
    return pl.pallas_call(
        cut_body,
        out_shape=[pltpu.VMEM((PADDED, width), jnp.bfloat16)] * 3,
        in_specs=[SMEM, ANY],
        out_specs=[VMEM] * 3,
        scratch_shapes=[pltpu.VMEM((3, cells, width), jnp.bfloat16), pltpu.SemaphoreType.DMA((3,))],
        compiler_params=LIMITED,
        name="cut_pixels",
    )(ints, tiles)


def pick_body(ints_ref, below_ref, above_ref, *refs):
    tiles, out_refs = refs[:6], refs[6:]

    @pl.when(active(ints_ref, len(out_refs) - 1))
    def _():
        core = ints_ref[CORE_AT]
        for slot, out_ref in enumerate(out_refs):
            source = ints_ref[SLOT_AT + slot]
            base = slot * 9

            def entry(part, source=source, base=base):
                inner = jnp.where(source == 3, above_ref[base + part], ints_ref[base + 3 + part])
                return jnp.where(source == 1, below_ref[base + 6 + part], inner)

            same_chip = ((source == 1) & (core == 1)) | ((source == 3) & (core == 0))
            away = (source == 1) | (source == 3)
            micro = entry(0)
            chosen = selection(entry(1), entry(2))
            for number, wanted in enumerate((same_chip, ~away, away & ~same_chip)):
                for index in range(2):

                    @pl.when(wanted & (micro == index))
                    def _(chosen=chosen, tile=tiles[2 * number + index], out_ref=out_ref):
                        rows = jnp.dot(chosen, tile[...], preferred_element_type=jnp.float32)
                        out_ref[...] = rows.astype(jnp.bfloat16)


def pick_crops(ints, below, above, tiles, slots):
    width = tiles[0].shape[1]
    return pl.pallas_call(
        pick_body,
        out_shape=[pltpu.VMEM((PADDED, width), jnp.bfloat16)] * slots,
        in_specs=[SMEM] * 3 + [VMEM] * len(tiles),
        out_specs=[VMEM] * slots,
        compiler_params=LIMITED,
        name="pick_crops",
    )(ints, below, above, *map(resident, tiles))


EMBED, MERGE, QUERY = 0, 1536, 2560
KEY, VALUE, OUT, POS, HALF = 0, 1024, 2048, 3072, 3584


def pack_body(parity_ref, embed, merge, pos, qkv, out, packed, buffer, sems):
    first = [
        (embed.at[:, pl.ds(0, LANES)], EMBED),
        (embed.at[:, pl.ds(LANES, LANES)], EMBED + 768),
        (merge.at[:, pl.ds(0, LANES)], MERGE),
        (merge.at[:, pl.ds(LANES, LANES)], MERGE + 512),
        (qkv.at[0], QUERY),
    ]
    second = [(qkv.at[1], KEY), (qkv.at[2], VALUE)]
    second += [(out.at[:, pl.ds(column * LANES, LANES)], OUT + column * LANES) for column in range(8)]
    second += [
        (pos.at[:, pl.ds(0, LANES)], POS),
        (pos.at[:, pl.ds(LANES, LANES)], POS + PADDED),
    ]
    for parity, pieces in enumerate((first, second)):

        @pl.when(parity_ref[0] == parity)
        def _(pieces=pieces):
            copies, results = [], []
            for number, (piece, at) in enumerate(pieces):
                place = pl.ds(at, piece.shape[0])
                copies.append(pltpu.make_async_copy(piece, buffer.at[place], sems.at[2 * number]))
                results.append(
                    pltpu.make_async_copy(buffer.at[place], packed.at[place], sems.at[2 * number + 1])
                )
                copies[-1].start()
            for copy, result in zip(copies, results):
                copy.wait()
                result.start()
            for result in results:
                result.wait()


def packed_half(parity, embed, merge, pos, qkv, out):
    return pl.pallas_call(
        pack_body,
        out_shape=jax.ShapeDtypeStruct((HALF, LANES), jnp.bfloat16),
        in_specs=[SMEM] + [ANY] * 5,
        out_specs=ANY,
        scratch_shapes=[pltpu.VMEM((HALF, LANES), jnp.bfloat16), pltpu.SemaphoreType.DMA((24,))],
        compiler_params=LIMITED,
        name="pack_weights",
    )(parity, *map(in_hbm, (embed, merge, pos, qkv, out)))


def columns(ref, section, low, height):
    return jnp.concatenate(
        [ref[section, pl.ds(low, height), :], ref[section, pl.ds(low + height, height), :]], axis=1
    )


def stage_body(ints_ref, pix_below, pix_own, pix_above, packed, weights, base_ref, pix, sems):
    source = ints_ref[SLOT_AT + ints_ref[SECTION_AT]]
    sections = packed.shape[0] // 2
    spans = [(0, EMBED, MERGE), (1, POS, HALF), (0, MERGE, HALF), (1, KEY, POS)]
    copies = []
    for part, low, high in spans:
        for section in range(sections):
            place = (2 * section + part, pl.ds(low, high - low))
            copies.append(
                pltpu.make_async_copy(packed.at[place], weights.at[place], sems.at[1 + len(copies)])
            )
    for number, pix_ref in enumerate((pix_below, pix_own, pix_above)):

        @pl.when((source == number + 1) if number != 1 else ((source == 2) | (source == 0)))
        def _(pix_ref=pix_ref):
            copy = pltpu.make_async_copy(pix_ref, pix, sems.at[0])
            copy.start()
            copy.wait()

    for copy in copies:
        copy.start()
    for copy in copies[: 2 * sections]:
        copy.wait()
    rows = pix[...]
    row_ok = lax.broadcasted_iota(jnp.int32, (PADDED, 2 * LANES), 0) < ROWS
    for section in range(sections):
        pos = jnp.where(row_ok, columns(weights, 2 * section + 1, POS, PADDED).astype(jnp.float32), 0.0)
        base_ref[:, pl.ds(section * 2 * LANES, 2 * LANES)] = pos + jnp.dot(
            rows, columns(weights, 2 * section, EMBED, 768), preferred_element_type=jnp.float32
        )
    for copy in copies[2 * sections :]:
        copy.wait()


def staged(ints, pixels, packed):
    width = LANES * packed.shape[0]
    return pl.pallas_call(
        stage_body,
        out_shape=[pltpu.VMEM(packed.shape, jnp.bfloat16), pltpu.VMEM((PADDED, width), jnp.float32)],
        in_specs=[SMEM] + [ANY] * 4,
        out_specs=[VMEM] * 2,
        scratch_shapes=[
            pltpu.VMEM(pixels[0].shape, jnp.bfloat16),
            pltpu.SemaphoreType.DMA((1 + 2 * packed.shape[0],)),
        ],
        compiler_params=LIMITED,
        name="stage_weights",
    )(ints, *map(in_hbm, (*pixels, packed)))


def classify_body(ints_ref, *refs):
    feat_refs = refs[:4]
    base_ref, weights, gain_ref, out_ref, feat = refs[4:]
    place = ints_ref[SECTION_AT]
    source = ints_ref[SLOT_AT + place]
    sections = weights.shape[0] // 2
    for number, feat_ref in enumerate(feat_refs):

        @pl.when(place == number)
        def _(feat_ref=feat_ref):
            feat[...] = feat_ref[...]

    feat_rows = feat[...]
    tokens = base_ref[...] + jnp.concatenate(
        [
            jnp.dot(feat_rows, columns(weights, 2 * section, MERGE, 512), preferred_element_type=jnp.float32)
            for section in range(sections)
        ],
        axis=1,
    )
    width = tokens.shape[1]
    mean = jnp.sum(tokens, axis=-1, keepdims=True) / width
    centred = tokens - mean
    var = jnp.sum(centred * centred, axis=-1, keepdims=True) / width
    attn_in = (centred * lax.rsqrt(var + EPSILON) * gain_ref[pl.ds(0, 1), :]).astype(jnp.bfloat16)
    token_sum = jnp.sum(tokens, axis=0, keepdims=True)
    key_ok = lax.broadcasted_iota(jnp.int32, (PADDED, PADDED), 1) < ROWS
    lane = lax.broadcasted_iota(jnp.int32, (PADDED, 2 * HEAD_DIM), 1)
    row_ok = lax.broadcasted_iota(jnp.int32, (PADDED, 2 * HEAD_DIM), 0) < ROWS
    context_sums = []
    for section in range(sections):
        first, second = 2 * section, 2 * section + 1
        piece = jnp.concatenate(
            [
                weights[first, pl.ds(QUERY, 1024), :],
                weights[second, pl.ds(KEY, 1024), :],
                weights[second, pl.ds(VALUE, 1024), :],
            ],
            axis=1,
        )
        qkv = jnp.dot(attn_in, piece, preferred_element_type=jnp.float32).astype(jnp.bfloat16)
        query, key, value = qkv[:, :128], qkv[:, 128:256], qkv[:, 256:]
        contexts = []
        for head in range(2):
            mine = (lane >= HEAD_DIM) if head else (lane < HEAD_DIM)
            scores = lax.dot_general(
                jnp.where(mine, query, jnp.zeros_like(query)),
                key,
                (((1,), (1,)), ((), ())),
                preferred_element_type=jnp.float32,
            ) * (1.0 / math.sqrt(HEAD_DIM))
            scores = jnp.where(key_ok, scores, -jnp.inf)
            top = jnp.max(scores, axis=-1, keepdims=True)
            numer = jnp.exp(scores - top)
            probs = (numer * (1.0 / jnp.sum(numer, axis=-1, keepdims=True))).astype(jnp.bfloat16)
            contexts.append(jnp.dot(probs, value, preferred_element_type=jnp.float32))
        context = jnp.where(lane < HEAD_DIM, contexts[0], contexts[1]).astype(jnp.bfloat16)
        context = jnp.where(row_ok, context.astype(jnp.float32), 0.0)
        context_sums.append(jnp.sum(context, axis=0, keepdims=True))
    context_mean = jnp.concatenate(context_sums, axis=1) / ROWS
    high = context_mean.astype(jnp.bfloat16)
    rest = context_mean - high.astype(jnp.float32)
    middle = rest.astype(jnp.bfloat16)
    low = (rest - middle.astype(jnp.float32)).astype(jnp.bfloat16)
    pieces = jnp.concatenate([high, middle, low, jnp.zeros((13, high.shape[1]), jnp.bfloat16)], axis=0)
    out_weight = jnp.concatenate(
        [
            jnp.concatenate(
                [weights[2 * section + 1, pl.ds(OUT + LANES * column, LANES), :] for column in range(8)], axis=1
            )
            for section in range(sections)
        ],
        axis=0,
    )
    mixed = jnp.dot(pieces, out_weight, preferred_element_type=jnp.float32)
    pooled = token_sum / ROWS + jnp.sum(mixed, axis=0, keepdims=True)
    pooled_mean = jnp.sum(pooled, axis=-1, keepdims=True) / width
    centred = pooled - pooled_mean
    var = jnp.sum(centred * centred, axis=-1, keepdims=True) / width
    result = centred * lax.rsqrt(var + EPSILON) * gain_ref[pl.ds(1, 1), :]
    out_ref[...] = jnp.where(source == 0, 0.0, result)


def classify(ints, feats, base, weights, gain):
    return pl.pallas_call(
        classify_body,
        out_shape=jax.ShapeDtypeStruct((1, gain.shape[1]), jnp.float32),
        in_specs=[SMEM] + [VMEM] * 7,
        out_specs=VMEM,
        scratch_shapes=[pltpu.VMEM(feats[0].shape, jnp.bfloat16)],
        compiler_params=LIMITED,
        name="classify",
    )(ints, *map(resident, (*feats, base, weights, gain)))


def after(value, *others):
    return lax.optimization_barrier((value,) + others)[0]


def per_device(
    tile_features,
    patches,
    det_kernel,
    det_gain,
    det_in,
    det_out,
    det_scale,
    cls_embed,
    cls_merge,
    cls_pos,
    cls_qkv,
    cls_out,
    cls_gain,
    crop_plan,
    slot_from,
):
    sections = lax.axis_size("section")
    count = lax.axis_size(REP)
    section = lax.axis_index("section").astype(jnp.int32)
    core = lax.axis_index("core").astype(jnp.int32)
    width = tile_features.shape[3]
    slabs = width // LANES
    last = sections - 1
    upward = [(index, index + 1) for index in range(count - 1)]
    downward = [(target, origin) for origin, target in upward]
    swap = [(index, index ^ 1) for index in range(count)]
    ints = jnp.concatenate([crop_plan.reshape(-1), slot_from.reshape(-1), section.reshape(1), core.reshape(1)])

    half = packed_half(core.reshape(1), cls_embed, cls_merge, cls_pos, cls_qkv.transpose(1, 0, 2), cls_out)
    weights = lax.all_gather(half, ("section", "core"), axis=0)

    shard = jnp.stack([det_in[0].T, det_out[0]], axis=0)
    line = spread_in_groups(shard, line_groups(True))
    plane = spread_in_groups(after(line, half), line_groups(False))
    cut = cut_pixels(ints, patches.reshape(2, CELLS, patches.shape[3]))
    pixels = (lax.ppermute(cut[2], REP, upward), cut[1], lax.ppermute(cut[0], REP, downward))
    below = lax.ppermute(ints, REP, upward)
    above = lax.ppermute(ints, REP, downward)
    params = jnp.concatenate(
        [det_kernel[0].reshape(49, width), det_gain, det_scale, jnp.zeros((5, width), jnp.float32)], axis=0
    )
    params = params.reshape(56, slabs, LANES).transpose(1, 0, 2)
    start = tile_features.reshape(2, CELLS, width)
    tiles = [start[0], start[1]]
    early = early_norm(ints, tiles[0], params)
    plane = after(plane, below, above, early, *pixels)
    own = plane.reshape((SIDE * SIDE,) + shard.shape)
    other = lax.ppermute(own, REP, swap)

    for number in range(sections):
        ahead = [(early,), ()] if number == 0 else [(), ()]
        done = []
        for tile, more in zip(tiles, ahead):
            order = after(ints, *done)
            done.append(detector_block(number, order, tile, params, own, other, *more))
        if number < last:
            tiles = [lax.ppermute(tile, "section", [(number, number + 1)]) for tile in done]

    within = [(last * count + origin, last * count + target) for origin, target in swap]
    across = [(last * count + index, last * count + index + 1) for index in range(1, count - 1, 2)]
    across += [(target, origin) for origin, target in across]
    far = [lax.ppermute(tile, ("section",) + REP, across) for tile in done]
    near = [lax.ppermute(tile, ("section",) + REP, within) for tile in lax.optimization_barrier(tuple(done))]
    crops = pick_crops(after(ints, weights), below, above, near + done + far, sections)
    feats = [lax.ppermute(crops[slot], "section", [(last, slot)]) for slot in range(last)] + [crops[last]]
    weights, base = staged(after(ints, *crops), pixels, weights)
    result = classify(ints, feats, base, weights, cls_gain)
    return result[None]


def solution(mesh):
    sections = mesh.shape["section"]
    fine = jax.sharding.Mesh(mesh.devices.reshape(sections, SIDE, SIDE, 2), ("section",) + REP)
    return jax.shard_map(
        per_device,
        mesh=fine,
        in_specs=(
            P(REP, None, None, None),
            P(REP, None, None, None),
            P("section", None, None, None),
            P("section", None),
            P("section", None, REP),
            P("section", REP, None),
            P("section", None),
            P(None, "section"),
            P(None, "section"),
            P(None, "section"),
            P(None, None, "section"),
            P("section", None),
            P(),
            P(REP, None, None, None),
            P(REP, None),
        ),
        out_specs=P(REP, "section", None),
        check_vma=False,
    )
```

```python
import functools
import math

import jax
import jax.numpy as jnp
from jax import lax
from jax.experimental import pallas as pl
from jax.experimental.pallas import tpu as pltpu
from jax.sharding import PartitionSpec as P

HEAD_DIM = 64
TILE = 16
CELLS = TILE * TILE
CROP = 14
ROWS = CROP * CROP
PADDED = 208
LANES = 128
SIDE = 8
REP = ("y", "z", "core")
EPSILON = 1e-06
SLOT_AT = 36
SECTION_AT = 40
CORE_AT = 41

ANY = pl.BlockSpec(memory_space=pl.ANY)
SMEM = pl.BlockSpec(memory_space=pltpu.SMEM)
VMEM = pl.BlockSpec(memory_space=pltpu.VMEM)
LIMITED = pltpu.CompilerParams(vmem_limit_bytes=16 << 20)


def rep_index(y, z, core):
    return (y * SIDE + z) * 2 + core


def line_groups(first):
    along_z = [[rep_index(y, z, 0 if first else 1) for z in range(SIDE)] for y in range(SIDE)]
    along_y = [[rep_index(y, z, 1 if first else 0) for y in range(SIDE)] for z in range(SIDE)]
    return along_z + along_y


def resident(array):
    return pltpu.with_memory_space_constraint(array, pltpu.VMEM)


def spread_in_groups(block, groups):
    copies = jnp.broadcast_to(block[None], (SIDE,) + block.shape)
    return lax.all_to_all(copies, REP, 0, 0, axis_index_groups=groups)


def in_hbm(array):
    return pltpu.with_memory_space_constraint(array, pltpu.HBM)


def active(ints_ref, number):
    return ints_ref[SECTION_AT] == number


def conv_norm(tile_ref, param_ref, normed_ref, wide, conv):
    slabs = wide.shape[0]
    wide[:, :, 0:8, :] = jnp.zeros((slabs, TILE, 8, LANES), jnp.float32)
    wide[:, :, 24:32, :] = jnp.zeros((slabs, TILE, 8, LANES), jnp.float32)
    for slab in range(slabs):
        part = tile_ref[:, slab * LANES : (slab + 1) * LANES].astype(jnp.float32)
        wide[slab, :, 8:24, :] = part.reshape(TILE, TILE, LANES)

    def one_slab(slab, carry):
        sums = [None] * TILE
        for col in range(7):
            taps = [param_ref[slab, pl.ds(row * 7 + col, 1), :] for row in range(7)]
            for source in range(TILE):
                cells = wide[slab, source, pl.ds(5 + col, TILE), :]
                for row in range(7):
                    target = source + 3 - row
                    if 0 <= target < TILE:
                        term = cells * taps[row]
                        sums[target] = term if sums[target] is None else sums[target] + term
        for target in range(TILE):
            conv[slab, pl.ds(target * TILE, TILE), :] = sums[target]
        return carry

    lax.fori_loop(0, slabs, one_slab, 0)
    width = slabs * LANES
    total = conv[0]
    for slab in range(1, slabs):
        total = total + conv[slab]
    mean = jnp.sum(total, axis=-1, keepdims=True) / width
    squares = None
    for slab in range(slabs):
        centred = conv[slab] - mean
        squares = centred * centred if squares is None else squares + centred * centred
    scale = lax.rsqrt(jnp.sum(squares, axis=-1, keepdims=True) / width + EPSILON)
    for slab in range(slabs):
        normed_ref[:, slab * LANES : (slab + 1) * LANES] = (
            (conv[slab] - mean) * scale * param_ref[slab, pl.ds(49, 1), :]
        ).astype(jnp.bfloat16)


def early_body(ints_ref, tile_ref, param_ref, normed_ref, wide, conv):
    @pl.when(active(ints_ref, 0))
    def _():
        conv_norm(tile_ref, param_ref, normed_ref, wide, conv)


def conv_scratch(tile):
    cells, width = tile.shape
    slabs = width // LANES
    return [
        pltpu.VMEM((slabs, TILE, 32, LANES), jnp.float32),
        pltpu.VMEM((slabs, cells, LANES), jnp.float32),
    ]


def early_norm(ints, tile, params):
    return pl.pallas_call(
        early_body,
        out_shape=pltpu.VMEM(tile.shape, jnp.bfloat16),
        in_specs=[SMEM, VMEM, VMEM],
        out_specs=VMEM,
        scratch_shapes=conv_scratch(tile),
        compiler_params=LIMITED,
        name="early_norm",
    )(ints, resident(tile), resident(params))


def mlp(normed_ref, own_ref, other_ref, tile_ref, param_ref, out_ref):
    width = tile_ref.shape[1]
    slabs = width // LANES
    rows = normed_ref[...]
    update = None
    step = 64
    for ref in (own_ref, other_ref):
        for chunk in range(0, ref.shape[0], step):
            into = ref[pl.ds(chunk, step), 0].reshape(step * 16, width)
            outof = ref[pl.ds(chunk, step), 1].reshape(step * 16, width)
            hidden = lax.dot_general(
                rows, into, (((1,), (1,)), ((), ())), preferred_element_type=jnp.float32
            )
            hidden = jax.nn.gelu(hidden, approximate=True).astype(jnp.bfloat16)
            term = jnp.dot(hidden, outof, preferred_element_type=jnp.float32)
            update = term if update is None else update + term
    for slab in range(slabs):
        part = slice(slab * LANES, (slab + 1) * LANES)
        out_ref[:, part] = (
            tile_ref[:, part].astype(jnp.float32) + param_ref[slab, pl.ds(50, 1), :] * update[:, part]
        ).astype(jnp.bfloat16)


def early_block_body(ints_ref, tile_ref, param_ref, own_ref, other_ref, normed_ref, out_ref):
    @pl.when(active(ints_ref, 0))
    def _():
        mlp(normed_ref, own_ref, other_ref, tile_ref, param_ref, out_ref)


def block_body(ints_ref, tile_ref, param_ref, own_ref, other_ref, *refs, number):
    before, (out_ref, normed, wide, conv) = refs[:-4], refs[-4:]

    @pl.when(active(ints_ref, number))
    def _():
        conv_norm(tile_ref, param_ref, normed, wide, conv)
        result_ref = out_ref
        if before:
            out_ref[0] = before[0][...]
            result_ref = out_ref.at[1]
        mlp(normed, own_ref, other_ref, tile_ref, param_ref, result_ref)


def early_block(ints, tile, params, own, other, normed):
    return pl.pallas_call(
        early_block_body,
        out_shape=pltpu.VMEM(tile.shape, jnp.bfloat16),
        in_specs=[SMEM] + [VMEM] * 5,
        out_specs=VMEM,
        compiler_params=LIMITED,
        name="early_block",
    )(ints, *map(resident, (tile, params, own, other, normed)))


def detector_block(number, ints, tile, params, own, other, *before):
    shape = (2,) + tile.shape if before else tile.shape
    return pl.pallas_call(
        functools.partial(block_body, number=number),
        out_shape=pltpu.VMEM(shape, jnp.bfloat16),
        in_specs=[SMEM] + [VMEM] * (4 + len(before)),
        out_specs=VMEM,
        scratch_shapes=[pltpu.VMEM(tile.shape, jnp.bfloat16)] + conv_scratch(tile),
        compiler_params=LIMITED,
        name="detector_block",
    )(ints, *map(resident, (tile, params, own, other, *before)))


def selection(top, left):
    row = lax.broadcasted_iota(jnp.int32, (PADDED, CELLS), 0)
    cell = lax.broadcasted_iota(jnp.int32, (PADDED, CELLS), 1)
    crop_row = (row * 4682) >> 16
    wanted = (top + crop_row) * TILE + left + (row - crop_row * CROP)
    return jnp.where((cell == wanted) & (row < ROWS), 1.0, 0.0).astype(jnp.bfloat16)


def cut_body(ints_ref, tile_ref, *refs):
    out_refs, buffer, sems = refs[:3], refs[3], refs[4]
    base = ints_ref[SECTION_AT] * 9
    copies = []
    for turn in range(3):
        copies.append(
            pltpu.make_async_copy(tile_ref.at[ints_ref[base + 3 * turn]], buffer.at[turn], sems.at[turn])
        )
        copies[-1].start()
    for turn in range(3):
        chosen = selection(ints_ref[base + 3 * turn + 1], ints_ref[base + 3 * turn + 2])
        copies[turn].wait()
        rows = jnp.dot(chosen, buffer[turn], preferred_element_type=jnp.float32)
        out_refs[turn][...] = rows.astype(jnp.bfloat16)


def cut_pixels(ints, tiles):
    micro, cells, width = tiles.shape
    return pl.pallas_call(
        cut_body,
        out_shape=[pltpu.VMEM((PADDED, width), jnp.bfloat16)] * 3,
        in_specs=[SMEM, ANY],
        out_specs=[VMEM] * 3,
        scratch_shapes=[pltpu.VMEM((3, cells, width), jnp.bfloat16), pltpu.SemaphoreType.DMA((3,))],
        compiler_params=LIMITED,
        name="cut_pixels",
    )(ints, tiles)


def pick_body(ints_ref, below_ref, above_ref, *refs):
    pairs, out_refs = refs[:3], refs[3:]

    @pl.when(active(ints_ref, len(out_refs) - 1))
    def _():
        core = ints_ref[CORE_AT]
        for slot, out_ref in enumerate(out_refs):
            source = ints_ref[SLOT_AT + slot]
            base = slot * 9

            def entry(part, source=source, base=base):
                inner = jnp.where(source == 3, above_ref[base + part], ints_ref[base + 3 + part])
                return jnp.where(source == 1, below_ref[base + 6 + part], inner)

            same_chip = ((source == 1) & (core == 1)) | ((source == 3) & (core == 0))
            away = (source == 1) | (source == 3)
            micro = entry(0)
            chosen = selection(entry(1), entry(2))
            for pair, wanted in zip(pairs, (same_chip, ~away, away & ~same_chip)):

                @pl.when(wanted)
                def _(chosen=chosen, pair=pair, micro=micro, out_ref=out_ref):
                    rows = jnp.dot(chosen, pair[micro], preferred_element_type=jnp.float32)
                    out_ref[...] = rows.astype(jnp.bfloat16)


def pick_crops(ints, below, above, pairs, slots):
    width = pairs[0].shape[2]
    return pl.pallas_call(
        pick_body,
        out_shape=[pltpu.VMEM((PADDED, width), jnp.bfloat16)] * slots,
        in_specs=[SMEM] * 3 + [VMEM] * len(pairs),
        out_specs=[VMEM] * slots,
        compiler_params=LIMITED,
        name="pick_crops",
    )(ints, below, above, *map(resident, pairs))


EMBED, MERGE, QUERY = 0, 1536, 2560
KEY, VALUE, OUT, POS, HALF = 0, 1024, 2048, 3072, 3584


def pack_body(parity_ref, embed, merge, pos, qkv, out, packed, buffer, sems):
    first = [
        (embed.at[:, pl.ds(0, LANES)], EMBED),
        (embed.at[:, pl.ds(LANES, LANES)], EMBED + 768),
        (merge.at[:, pl.ds(0, LANES)], MERGE),
        (merge.at[:, pl.ds(LANES, LANES)], MERGE + 512),
        (qkv.at[0], QUERY),
    ]
    second = [(qkv.at[1], KEY), (qkv.at[2], VALUE)]
    second += [(out.at[:, pl.ds(column * LANES, LANES)], OUT + column * LANES) for column in range(8)]
    second += [
        (pos.at[:, pl.ds(0, LANES)], POS),
        (pos.at[:, pl.ds(LANES, LANES)], POS + PADDED),
    ]
    for parity, pieces in enumerate((first, second)):

        @pl.when(parity_ref[0] == parity)
        def _(pieces=pieces):
            copies, results = [], []
            for number, (piece, at) in enumerate(pieces):
                place = pl.ds(at, piece.shape[0])
                copies.append(pltpu.make_async_copy(piece, buffer.at[place], sems.at[2 * number]))
                results.append(
                    pltpu.make_async_copy(buffer.at[place], packed.at[place], sems.at[2 * number + 1])
                )
                copies[-1].start()
            for copy, result in zip(copies, results):
                copy.wait()
                result.start()
            for result in results:
                result.wait()


def packed_half(parity, embed, merge, pos, qkv, out):
    return pl.pallas_call(
        pack_body,
        out_shape=jax.ShapeDtypeStruct((HALF, LANES), jnp.bfloat16),
        in_specs=[SMEM] + [ANY] * 5,
        out_specs=ANY,
        scratch_shapes=[pltpu.VMEM((HALF, LANES), jnp.bfloat16), pltpu.SemaphoreType.DMA((24,))],
        compiler_params=LIMITED,
        name="pack_weights",
    )(parity, *map(in_hbm, (embed, merge, pos, qkv, out)))


def columns(ref, section, low, height):
    return jnp.concatenate(
        [ref[section, pl.ds(low, height), :], ref[section, pl.ds(low + height, height), :]], axis=1
    )


def stage_body(ints_ref, pix_below, pix_own, pix_above, packed, weights, base_ref, pix, sems):
    source = ints_ref[SLOT_AT + ints_ref[SECTION_AT]]
    sections = packed.shape[0] // 2
    spans = [(0, EMBED, MERGE), (1, POS, HALF), (0, MERGE, HALF), (1, KEY, POS)]
    copies = []
    for part, low, high in spans:
        for section in range(sections):
            place = (2 * section + part, pl.ds(low, high - low))
            copies.append(
                pltpu.make_async_copy(packed.at[place], weights.at[place], sems.at[1 + len(copies)])
            )
    for number, pix_ref in enumerate((pix_below, pix_own, pix_above)):

        @pl.when((source == number + 1) if number != 1 else ((source == 2) | (source == 0)))
        def _(pix_ref=pix_ref):
            copy = pltpu.make_async_copy(pix_ref, pix, sems.at[0])
            copy.start()
            copy.wait()

    for copy in copies:
        copy.start()
    for copy in copies[: 2 * sections]:
        copy.wait()
    rows = pix[...]
    row_ok = lax.broadcasted_iota(jnp.int32, (PADDED, 2 * LANES), 0) < ROWS
    for section in range(sections):
        pos = jnp.where(row_ok, columns(weights, 2 * section + 1, POS, PADDED).astype(jnp.float32), 0.0)
        base_ref[:, pl.ds(section * 2 * LANES, 2 * LANES)] = pos + jnp.dot(
            rows, columns(weights, 2 * section, EMBED, 768), preferred_element_type=jnp.float32
        )
    for copy in copies[2 * sections :]:
        copy.wait()


def staged(ints, pixels, packed):
    width = LANES * packed.shape[0]
    return pl.pallas_call(
        stage_body,
        out_shape=[pltpu.VMEM(packed.shape, jnp.bfloat16), pltpu.VMEM((PADDED, width), jnp.float32)],
        in_specs=[SMEM] + [ANY] * 4,
        out_specs=[VMEM] * 2,
        scratch_shapes=[
            pltpu.VMEM(pixels[0].shape, jnp.bfloat16),
            pltpu.SemaphoreType.DMA((1 + 2 * packed.shape[0],)),
        ],
        compiler_params=LIMITED,
        name="stage_weights",
    )(ints, *map(in_hbm, (*pixels, packed)))


def classify_body(ints_ref, *refs):
    feat_refs = refs[:4]
    base_ref, weights, gain_ref, out_ref, feat = refs[4:]
    place = ints_ref[SECTION_AT]
    source = ints_ref[SLOT_AT + place]
    sections = weights.shape[0] // 2
    for number, feat_ref in enumerate(feat_refs):

        @pl.when(place == number)
        def _(feat_ref=feat_ref):
            feat[...] = feat_ref[...]

    feat_rows = feat[...]
    tokens = base_ref[...] + jnp.concatenate(
        [
            jnp.dot(feat_rows, columns(weights, 2 * section, MERGE, 512), preferred_element_type=jnp.float32)
            for section in range(sections)
        ],
        axis=1,
    )
    width = tokens.shape[1]
    mean = jnp.sum(tokens, axis=-1, keepdims=True) / width
    centred = tokens - mean
    var = jnp.sum(centred * centred, axis=-1, keepdims=True) / width
    attn_in = (centred * lax.rsqrt(var + EPSILON) * gain_ref[pl.ds(0, 1), :]).astype(jnp.bfloat16)
    token_sum = jnp.sum(tokens, axis=0, keepdims=True)
    key_ok = lax.broadcasted_iota(jnp.int32, (PADDED, PADDED), 1) < ROWS
    lane = lax.broadcasted_iota(jnp.int32, (PADDED, 2 * HEAD_DIM), 1)
    row_ok = lax.broadcasted_iota(jnp.int32, (PADDED, 2 * HEAD_DIM), 0) < ROWS
    context_sums = []
    for section in range(sections):
        first, second = 2 * section, 2 * section + 1
        piece = jnp.concatenate(
            [
                weights[first, pl.ds(QUERY, 1024), :],
                weights[second, pl.ds(KEY, 1024), :],
                weights[second, pl.ds(VALUE, 1024), :],
            ],
            axis=1,
        )
        qkv = jnp.dot(attn_in, piece, preferred_element_type=jnp.float32).astype(jnp.bfloat16)
        query, key, value = qkv[:, :128], qkv[:, 128:256], qkv[:, 256:]
        contexts = []
        for head in range(2):
            mine = (lane >= HEAD_DIM) if head else (lane < HEAD_DIM)
            scores = lax.dot_general(
                jnp.where(mine, query, jnp.zeros_like(query)),
                key,
                (((1,), (1,)), ((), ())),
                preferred_element_type=jnp.float32,
            ) * (1.0 / math.sqrt(HEAD_DIM))
            scores = jnp.where(key_ok, scores, -jnp.inf)
            top = jnp.max(scores, axis=-1, keepdims=True)
            numer = jnp.exp(scores - top)
            share = 1.0 / jnp.sum(numer, axis=-1, keepdims=True)
            summed = jnp.dot(numer.astype(jnp.bfloat16), value, preferred_element_type=jnp.float32)
            contexts.append(summed * share)
        context = jnp.where(lane < HEAD_DIM, contexts[0], contexts[1]).astype(jnp.bfloat16)
        context = jnp.where(row_ok, context.astype(jnp.float32), 0.0)
        context_sums.append(jnp.sum(context, axis=0, keepdims=True))
    context_mean = jnp.concatenate(context_sums, axis=1) / ROWS
    high = context_mean.astype(jnp.bfloat16)
    rest = context_mean - high.astype(jnp.float32)
    middle = rest.astype(jnp.bfloat16)
    low = (rest - middle.astype(jnp.float32)).astype(jnp.bfloat16)
    pieces = jnp.concatenate([high, middle, low, jnp.zeros((13, high.shape[1]), jnp.bfloat16)], axis=0)
    out_weight = jnp.concatenate(
        [
            jnp.concatenate(
                [weights[2 * section + 1, pl.ds(OUT + LANES * column, LANES), :] for column in range(8)], axis=1
            )
            for section in range(sections)
        ],
        axis=0,
    )
    mixed = jnp.dot(pieces, out_weight, preferred_element_type=jnp.float32)
    pooled = token_sum / ROWS + jnp.sum(mixed, axis=0, keepdims=True)
    pooled_mean = jnp.sum(pooled, axis=-1, keepdims=True) / width
    centred = pooled - pooled_mean
    var = jnp.sum(centred * centred, axis=-1, keepdims=True) / width
    result = centred * lax.rsqrt(var + EPSILON) * gain_ref[pl.ds(1, 1), :]
    out_ref[...] = jnp.where(source == 0, 0.0, result)


def classify(ints, feats, base, weights, gain):
    return pl.pallas_call(
        classify_body,
        out_shape=jax.ShapeDtypeStruct((1, gain.shape[1]), jnp.float32),
        in_specs=[SMEM] + [VMEM] * 7,
        out_specs=VMEM,
        scratch_shapes=[pltpu.VMEM(feats[0].shape, jnp.bfloat16)],
        compiler_params=LIMITED,
        name="classify",
    )(ints, *map(resident, (*feats, base, weights, gain)))


def after(value, *others):
    return lax.optimization_barrier((value,) + others)[0]


def per_device(
    tile_features,
    patches,
    det_kernel,
    det_gain,
    det_in,
    det_out,
    det_scale,
    cls_embed,
    cls_merge,
    cls_pos,
    cls_qkv,
    cls_out,
    cls_gain,
    crop_plan,
    slot_from,
):
    sections = lax.axis_size("section")
    count = lax.axis_size(REP)
    section = lax.axis_index("section").astype(jnp.int32)
    core = lax.axis_index("core").astype(jnp.int32)
    width = tile_features.shape[3]
    slabs = width // LANES
    last = sections - 1
    upward = [(index, index + 1) for index in range(count - 1)]
    downward = [(target, origin) for origin, target in upward]
    swap = [(index, index ^ 1) for index in range(count)]
    ints = jnp.concatenate([crop_plan.reshape(-1), slot_from.reshape(-1), section.reshape(1), core.reshape(1)])

    half = packed_half(core.reshape(1), cls_embed, cls_merge, cls_pos, cls_qkv.transpose(1, 0, 2), cls_out)
    weights = lax.all_gather(half, ("section", "core"), axis=0)

    shard = jnp.stack([det_in[0].T, det_out[0]], axis=0)
    line = spread_in_groups(shard, line_groups(True))
    plane = spread_in_groups(after(line, half), line_groups(False))
    cut = cut_pixels(ints, patches.reshape(2, CELLS, patches.shape[3]))
    pixels = (lax.ppermute(cut[2], REP, upward), cut[1], lax.ppermute(cut[0], REP, downward))
    below = lax.ppermute(ints, REP, upward)
    above = lax.ppermute(ints, REP, downward)
    params = jnp.concatenate(
        [det_kernel[0].reshape(49, width), det_gain, det_scale, jnp.zeros((5, width), jnp.float32)], axis=0
    )
    params = params.reshape(56, slabs, LANES).transpose(1, 0, 2)
    start = tile_features.reshape(2, CELLS, width)
    tiles = [start[0], start[1]]
    early = early_norm(ints, tiles[0], params)
    plane = after(plane, below, above, early, *pixels)
    own = plane.reshape((SIDE * SIDE,) + shard.shape)
    other = lax.ppermute(own, REP, swap)

    for number in range(sections):
        if number == 0:
            first = early_block(ints, tiles[0], params, own, other, early)
        else:
            first = detector_block(number, ints, tiles[0], params, own, other)
        before = (first,) if number == last else ()
        second = detector_block(number, after(ints, first), tiles[1], params, own, other, *before)
        if number < last:
            tiles = [lax.ppermute(tile, "section", [(number, number + 1)]) for tile in (first, second)]

    within = [(last * count + origin, last * count + target) for origin, target in swap]
    across = [(last * count + index, last * count + index + 1) for index in range(1, count - 1, 2)]
    across += [(target, origin) for origin, target in across]
    far = lax.ppermute(second, ("section",) + REP, across)
    near = lax.ppermute(second, ("section",) + REP, within)
    crops = pick_crops(after(ints, weights), below, above, (near, second, far), sections)
    feats = [lax.ppermute(crops[slot], "section", [(last, slot)]) for slot in range(last)] + [crops[last]]
    weights, base = staged(after(ints, *crops), pixels, weights)
    result = classify(ints, feats, base, weights, cls_gain)
    return result[None]


def solution(mesh):
    sections = mesh.shape["section"]
    fine = jax.sharding.Mesh(mesh.devices.reshape(sections, SIDE, SIDE, 2), ("section",) + REP)
    return jax.shard_map(
        per_device,
        mesh=fine,
        in_specs=(
            P(REP, None, None, None),
            P(REP, None, None, None),
            P("section", None, None, None),
            P("section", None),
            P("section", None, REP),
            P("section", REP, None),
            P("section", None),
            P(None, "section"),
            P(None, "section"),
            P(None, "section"),
            P(None, None, "section"),
            P("section", None),
            P(),
            P(REP, None, None, None),
            P(REP, None),
        ),
        out_specs=P(REP, "section", None),
        check_vma=False,
    )
```

```python
import functools
import math

import jax
import jax.numpy as jnp
from jax import lax
from jax.experimental import pallas as pl
from jax.experimental.pallas import tpu as pltpu
from jax.sharding import PartitionSpec as P

HEAD_DIM = 64
TILE = 16
CELLS = TILE * TILE
CROP = 14
ROWS = CROP * CROP
PADDED = 208
LANES = 128
SIDE = 8
REP = ("y", "z", "core")
EPSILON = 1e-06
SLOT_AT = 36
SECTION_AT = 40
CORE_AT = 41

ANY = pl.BlockSpec(memory_space=pl.ANY)
SMEM = pl.BlockSpec(memory_space=pltpu.SMEM)
VMEM = pl.BlockSpec(memory_space=pltpu.VMEM)
LIMITED = pltpu.CompilerParams(vmem_limit_bytes=16 << 20)


def rep_index(y, z, core):
    return (y * SIDE + z) * 2 + core


def line_groups(first):
    along_z = [[rep_index(y, z, 0 if first else 1) for z in range(SIDE)] for y in range(SIDE)]
    along_y = [[rep_index(y, z, 1 if first else 0) for y in range(SIDE)] for z in range(SIDE)]
    return along_z + along_y


def resident(array):
    return pltpu.with_memory_space_constraint(array, pltpu.VMEM)


def spread_in_groups(block, groups):
    copies = jnp.broadcast_to(block[None], (SIDE,) + block.shape)
    return lax.all_to_all(copies, REP, 0, 0, axis_index_groups=groups)


def in_hbm(array):
    return pltpu.with_memory_space_constraint(array, pltpu.HBM)


def active(ints_ref, number):
    return ints_ref[SECTION_AT] == number


def conv_norm(tile_ref, param_ref, normed_ref, wide, conv):
    slabs = wide.shape[0]
    wide[:, :, 0:8, :] = jnp.zeros((slabs, TILE, 8, LANES), jnp.float32)
    wide[:, :, 24:32, :] = jnp.zeros((slabs, TILE, 8, LANES), jnp.float32)
    for slab in range(slabs):
        part = tile_ref[:, slab * LANES : (slab + 1) * LANES].astype(jnp.float32)
        wide[slab, :, 8:24, :] = part.reshape(TILE, TILE, LANES)

    def one_slab(slab, carry):
        sums = [None] * TILE
        for col in range(7):
            taps = [param_ref[slab, pl.ds(row * 7 + col, 1), :] for row in range(7)]
            for source in range(TILE):
                cells = wide[slab, source, pl.ds(5 + col, TILE), :]
                for row in range(7):
                    target = source + 3 - row
                    if 0 <= target < TILE:
                        term = cells * taps[row]
                        sums[target] = term if sums[target] is None else sums[target] + term
        for target in range(TILE):
            conv[slab, pl.ds(target * TILE, TILE), :] = sums[target]
        return carry

    lax.fori_loop(0, slabs, one_slab, 0)
    width = slabs * LANES
    total = conv[0]
    for slab in range(1, slabs):
        total = total + conv[slab]
    mean = jnp.sum(total, axis=-1, keepdims=True) / width
    squares = None
    for slab in range(slabs):
        centred = conv[slab] - mean
        squares = centred * centred if squares is None else squares + centred * centred
    scale = lax.rsqrt(jnp.sum(squares, axis=-1, keepdims=True) / width + EPSILON)
    for slab in range(slabs):
        normed_ref[:, slab * LANES : (slab + 1) * LANES] = (
            (conv[slab] - mean) * scale * param_ref[slab, pl.ds(49, 1), :]
        ).astype(jnp.bfloat16)


def early_body(ints_ref, tile_ref, param_ref, normed_ref, wide, conv):
    @pl.when(active(ints_ref, 0))
    def _():
        conv_norm(tile_ref, param_ref, normed_ref, wide, conv)


def conv_scratch(tile):
    cells, width = tile.shape
    slabs = width // LANES
    return [
        pltpu.VMEM((slabs, TILE, 32, LANES), jnp.float32),
        pltpu.VMEM((slabs, cells, LANES), jnp.float32),
    ]


def early_norm(ints, tile, params):
    return pl.pallas_call(
        early_body,
        out_shape=pltpu.VMEM(tile.shape, jnp.bfloat16),
        in_specs=[SMEM, VMEM, VMEM],
        out_specs=VMEM,
        scratch_shapes=conv_scratch(tile),
        compiler_params=LIMITED,
        name="early_norm",
    )(ints, resident(tile), resident(params))


def mlp(normed_ref, own_ref, other_ref, tile_ref, param_ref, out_ref):
    width = tile_ref.shape[1]
    slabs = width // LANES
    rows = normed_ref[...]
    update = None
    step = 64
    for ref in (own_ref, other_ref):
        for chunk in range(0, ref.shape[0], step):
            into = ref[pl.ds(chunk, step), 0].reshape(step * 16, width)
            outof = ref[pl.ds(chunk, step), 1].reshape(step * 16, width)
            hidden = lax.dot_general(
                rows, into, (((1,), (1,)), ((), ())), preferred_element_type=jnp.float32
            )
            hidden = jax.nn.gelu(hidden, approximate=True).astype(jnp.bfloat16)
            term = jnp.dot(hidden, outof, preferred_element_type=jnp.float32)
            update = term if update is None else update + term
    for slab in range(slabs):
        part = slice(slab * LANES, (slab + 1) * LANES)
        out_ref[:, part] = (
            tile_ref[:, part].astype(jnp.float32) + param_ref[slab, pl.ds(50, 1), :] * update[:, part]
        ).astype(jnp.bfloat16)


def early_block_body(ints_ref, tile_ref, param_ref, own_ref, other_ref, normed_ref, out_ref):
    @pl.when(active(ints_ref, 0))
    def _():
        mlp(normed_ref, own_ref, other_ref, tile_ref, param_ref, out_ref)


def block_body(ints_ref, tile_ref, param_ref, own_ref, other_ref, *refs, number):
    before, (out_ref, normed, wide, conv) = refs[:-4], refs[-4:]

    @pl.when(active(ints_ref, number))
    def _():
        conv_norm(tile_ref, param_ref, normed, wide, conv)
        result_ref = out_ref
        if before:
            out_ref[0] = before[0][...]
            result_ref = out_ref.at[1]
        mlp(normed, own_ref, other_ref, tile_ref, param_ref, result_ref)


def early_block(ints, tile, params, own, other, normed):
    return pl.pallas_call(
        early_block_body,
        out_shape=pltpu.VMEM(tile.shape, jnp.bfloat16),
        in_specs=[SMEM] + [VMEM] * 5,
        out_specs=VMEM,
        compiler_params=LIMITED,
        name="early_block",
    )(ints, *map(resident, (tile, params, own, other, normed)))


def detector_block(number, ints, tile, params, own, other, *before):
    shape = (2,) + tile.shape if before else tile.shape
    return pl.pallas_call(
        functools.partial(block_body, number=number),
        out_shape=pltpu.VMEM(shape, jnp.bfloat16),
        in_specs=[SMEM] + [VMEM] * (4 + len(before)),
        out_specs=VMEM,
        scratch_shapes=[pltpu.VMEM(tile.shape, jnp.bfloat16)] + conv_scratch(tile),
        compiler_params=LIMITED,
        name="detector_block",
    )(ints, *map(resident, (tile, params, own, other, *before)))


def selection(top, left):
    row = lax.broadcasted_iota(jnp.int32, (PADDED, CELLS), 0)
    cell = lax.broadcasted_iota(jnp.int32, (PADDED, CELLS), 1)
    crop_row = (row * 4682) >> 16
    wanted = (top + crop_row) * TILE + left + (row - crop_row * CROP)
    return jnp.where((cell == wanted) & (row < ROWS), 1.0, 0.0).astype(jnp.bfloat16)


def cut_body(ints_ref, tile_ref, *refs):
    out_refs, buffer, sems = refs[:3], refs[3], refs[4]
    core = ints_ref[CORE_AT]
    bases = [ints_ref[SECTION_AT] * 9 + 3 * turn for turn in (2 - 2 * core, 1, 2 * core)]
    copies = []
    for turn, base in enumerate(bases):
        copies.append(pltpu.make_async_copy(tile_ref.at[ints_ref[base]], buffer.at[turn], sems.at[turn]))
        copies[-1].start()
    for turn, base in enumerate(bases):
        chosen = selection(ints_ref[base + 1], ints_ref[base + 2])
        copies[turn].wait()
        rows = jnp.dot(chosen, buffer[turn], preferred_element_type=jnp.float32)
        out_refs[turn][...] = rows.astype(jnp.bfloat16)


def cut_pixels(ints, tiles):
    micro, cells, width = tiles.shape
    return pl.pallas_call(
        cut_body,
        out_shape=[pltpu.VMEM((PADDED, width), jnp.bfloat16)] * 3,
        in_specs=[SMEM, ANY],
        out_specs=[VMEM] * 3,
        scratch_shapes=[pltpu.VMEM((3, cells, width), jnp.bfloat16), pltpu.SemaphoreType.DMA((3,))],
        compiler_params=LIMITED,
        name="cut_pixels",
    )(ints, tiles)


def pick_body(ints_ref, below_ref, above_ref, *refs):
    pairs, out_refs = refs[:3], refs[3:]

    @pl.when(active(ints_ref, len(out_refs) - 1))
    def _():
        core = ints_ref[CORE_AT]
        for slot, out_ref in enumerate(out_refs):
            source = ints_ref[SLOT_AT + slot]
            base = slot * 9

            def entry(part, source=source, base=base):
                inner = jnp.where(source == 3, above_ref[base + part], ints_ref[base + 3 + part])
                return jnp.where(source == 1, below_ref[base + 6 + part], inner)

            same_chip = ((source == 1) & (core == 1)) | ((source == 3) & (core == 0))
            away = (source == 1) | (source == 3)
            micro = entry(0)
            chosen = selection(entry(1), entry(2))
            for pair, wanted in zip(pairs, (same_chip, ~away, away & ~same_chip)):

                @pl.when(wanted)
                def _(chosen=chosen, pair=pair, micro=micro, out_ref=out_ref):
                    rows = jnp.dot(chosen, pair[micro], preferred_element_type=jnp.float32)
                    out_ref[...] = rows.astype(jnp.bfloat16)


def pick_crops(ints, below, above, pairs, slots):
    width = pairs[0].shape[2]
    return pl.pallas_call(
        pick_body,
        out_shape=[pltpu.VMEM((PADDED, width), jnp.bfloat16)] * slots,
        in_specs=[SMEM] * 3 + [VMEM] * len(pairs),
        out_specs=[VMEM] * slots,
        compiler_params=LIMITED,
        name="pick_crops",
    )(ints, below, above, *map(resident, pairs))


EMBED, MERGE, QUERY = 0, 1536, 2560
KEY, VALUE, OUT, POS, HALF = 0, 1024, 2048, 3072, 3584


def pack_body(parity_ref, embed, merge, pos, qkv, out, packed, buffer, sems):
    first = [
        (embed.at[:, pl.ds(0, LANES)], EMBED),
        (embed.at[:, pl.ds(LANES, LANES)], EMBED + 768),
        (merge.at[:, pl.ds(0, LANES)], MERGE),
        (merge.at[:, pl.ds(LANES, LANES)], MERGE + 512),
        (qkv.at[0], QUERY),
    ]
    second = [(qkv.at[1], KEY), (qkv.at[2], VALUE)]
    second += [(out.at[:, pl.ds(column * LANES, LANES)], OUT + column * LANES) for column in range(8)]
    second += [
        (pos.at[:, pl.ds(0, LANES)], POS),
        (pos.at[:, pl.ds(LANES, LANES)], POS + PADDED),
    ]
    for parity, pieces in enumerate((first, second)):

        @pl.when(parity_ref[0] == parity)
        def _(pieces=pieces):
            copies, results = [], []
            for number, (piece, at) in enumerate(pieces):
                place = pl.ds(at, piece.shape[0])
                copies.append(pltpu.make_async_copy(piece, buffer.at[place], sems.at[2 * number]))
                results.append(
                    pltpu.make_async_copy(buffer.at[place], packed.at[place], sems.at[2 * number + 1])
                )
                copies[-1].start()
            for copy, result in zip(copies, results):
                copy.wait()
                result.start()
            for result in results:
                result.wait()


def packed_half(parity, embed, merge, pos, qkv, out):
    return pl.pallas_call(
        pack_body,
        out_shape=jax.ShapeDtypeStruct((HALF, LANES), jnp.bfloat16),
        in_specs=[SMEM] + [ANY] * 5,
        out_specs=ANY,
        scratch_shapes=[pltpu.VMEM((HALF, LANES), jnp.bfloat16), pltpu.SemaphoreType.DMA((24,))],
        compiler_params=LIMITED,
        name="pack_weights",
    )(parity, *map(in_hbm, (embed, merge, pos, qkv, out)))


def columns(ref, section, low, height):
    return jnp.concatenate(
        [ref[section, pl.ds(low, height), :], ref[section, pl.ds(low + height, height), :]], axis=1
    )


def stage_body(ints_ref, pix_near, pix_own, pix_far, packed, weights, base_ref, pix, sems):
    source = ints_ref[SLOT_AT + ints_ref[SECTION_AT]]
    sections = packed.shape[0] // 2
    spans = [(0, EMBED, MERGE), (1, POS, HALF), (0, MERGE, HALF), (1, KEY, POS)]
    copies = []
    for part, low, high in spans:
        for section in range(sections):
            place = (2 * section + part, pl.ds(low, high - low))
            copies.append(
                pltpu.make_async_copy(packed.at[place], weights.at[place], sems.at[1 + len(copies)])
            )
    core = ints_ref[CORE_AT]
    same_chip = ((source == 1) & (core == 1)) | ((source == 3) & (core == 0))
    away = (source == 1) | (source == 3)
    for pix_ref, wanted in ((pix_near, same_chip), (pix_own, ~away), (pix_far, away & ~same_chip)):

        @pl.when(wanted)
        def _(pix_ref=pix_ref):
            copy = pltpu.make_async_copy(pix_ref, pix, sems.at[0])
            copy.start()
            copy.wait()

    for copy in copies:
        copy.start()
    for copy in copies[: 2 * sections]:
        copy.wait()
    rows = pix[...]
    row_ok = lax.broadcasted_iota(jnp.int32, (PADDED, 2 * LANES), 0) < ROWS
    for section in range(sections):
        pos = jnp.where(row_ok, columns(weights, 2 * section + 1, POS, PADDED).astype(jnp.float32), 0.0)
        base_ref[:, pl.ds(section * 2 * LANES, 2 * LANES)] = pos + jnp.dot(
            rows, columns(weights, 2 * section, EMBED, 768), preferred_element_type=jnp.float32
        )
    for copy in copies[2 * sections :]:
        copy.wait()


def staged(ints, pixels, packed):
    width = LANES * packed.shape[0]
    return pl.pallas_call(
        stage_body,
        out_shape=[pltpu.VMEM(packed.shape, jnp.bfloat16), pltpu.VMEM((PADDED, width), jnp.float32)],
        in_specs=[SMEM] + [ANY] * 4,
        out_specs=[VMEM] * 2,
        scratch_shapes=[
            pltpu.VMEM(pixels[0].shape, jnp.bfloat16),
            pltpu.SemaphoreType.DMA((1 + 2 * packed.shape[0],)),
        ],
        compiler_params=LIMITED,
        name="stage_weights",
    )(ints, *map(in_hbm, (*pixels, packed)))


def classify_body(ints_ref, *refs):
    feat_refs = refs[:4]
    base_ref, weights, gain_ref, out_ref, feat = refs[4:]
    place = ints_ref[SECTION_AT]
    source = ints_ref[SLOT_AT + place]
    sections = weights.shape[0] // 2
    for number, feat_ref in enumerate(feat_refs):

        @pl.when(place == number)
        def _(feat_ref=feat_ref):
            feat[...] = feat_ref[...]

    feat_rows = feat[...]
    tokens = base_ref[...] + jnp.concatenate(
        [
            jnp.dot(feat_rows, columns(weights, 2 * section, MERGE, 512), preferred_element_type=jnp.float32)
            for section in range(sections)
        ],
        axis=1,
    )
    width = tokens.shape[1]
    mean = jnp.sum(tokens, axis=-1, keepdims=True) / width
    centred = tokens - mean
    var = jnp.sum(centred * centred, axis=-1, keepdims=True) / width
    attn_in = (centred * lax.rsqrt(var + EPSILON) * gain_ref[pl.ds(0, 1), :]).astype(jnp.bfloat16)
    token_sum = jnp.sum(tokens, axis=0, keepdims=True)
    key_ok = lax.broadcasted_iota(jnp.int32, (PADDED, PADDED), 1) < ROWS
    lane = lax.broadcasted_iota(jnp.int32, (PADDED, 2 * HEAD_DIM), 1)
    row_ok = lax.broadcasted_iota(jnp.int32, (PADDED, 2 * HEAD_DIM), 0) < ROWS
    context_sums = []
    for section in range(sections):
        first, second = 2 * section, 2 * section + 1
        piece = jnp.concatenate(
            [
                weights[first, pl.ds(QUERY, 1024), :],
                weights[second, pl.ds(KEY, 1024), :],
                weights[second, pl.ds(VALUE, 1024), :],
            ],
            axis=1,
        )
        qkv = jnp.dot(attn_in, piece, preferred_element_type=jnp.float32).astype(jnp.bfloat16)
        query, key, value = qkv[:, :128], qkv[:, 128:256], qkv[:, 256:]
        contexts = []
        for head in range(2):
            mine = (lane >= HEAD_DIM) if head else (lane < HEAD_DIM)
            scores = lax.dot_general(
                jnp.where(mine, query, jnp.zeros_like(query)),
                key,
                (((1,), (1,)), ((), ())),
                preferred_element_type=jnp.float32,
            ) * (1.0 / math.sqrt(HEAD_DIM))
            scores = jnp.where(key_ok, scores, -jnp.inf)
            top = jnp.max(scores, axis=-1, keepdims=True)
            numer = jnp.exp(scores - top)
            share = 1.0 / jnp.sum(numer, axis=-1, keepdims=True)
            summed = jnp.dot(numer.astype(jnp.bfloat16), value, preferred_element_type=jnp.float32)
            contexts.append(summed * share)
        context = jnp.where(lane < HEAD_DIM, contexts[0], contexts[1]).astype(jnp.bfloat16)
        context = jnp.where(row_ok, context.astype(jnp.float32), 0.0)
        context_sums.append(jnp.sum(context, axis=0, keepdims=True))
    context_mean = jnp.concatenate(context_sums, axis=1) / ROWS
    high = context_mean.astype(jnp.bfloat16)
    rest = context_mean - high.astype(jnp.float32)
    middle = rest.astype(jnp.bfloat16)
    low = (rest - middle.astype(jnp.float32)).astype(jnp.bfloat16)
    pieces = jnp.concatenate([high, middle, low, jnp.zeros((13, high.shape[1]), jnp.bfloat16)], axis=0)
    out_weight = jnp.concatenate(
        [
            jnp.concatenate(
                [weights[2 * section + 1, pl.ds(OUT + LANES * column, LANES), :] for column in range(8)], axis=1
            )
            for section in range(sections)
        ],
        axis=0,
    )
    mixed = jnp.dot(pieces, out_weight, preferred_element_type=jnp.float32)
    pooled = token_sum / ROWS + jnp.sum(mixed, axis=0, keepdims=True)
    pooled_mean = jnp.sum(pooled, axis=-1, keepdims=True) / width
    centred = pooled - pooled_mean
    var = jnp.sum(centred * centred, axis=-1, keepdims=True) / width
    result = centred * lax.rsqrt(var + EPSILON) * gain_ref[pl.ds(1, 1), :]
    out_ref[...] = jnp.where(source == 0, 0.0, result)


def classify(ints, feats, base, weights, gain):
    return pl.pallas_call(
        classify_body,
        out_shape=jax.ShapeDtypeStruct((1, gain.shape[1]), jnp.float32),
        in_specs=[SMEM] + [VMEM] * 7,
        out_specs=VMEM,
        scratch_shapes=[pltpu.VMEM(feats[0].shape, jnp.bfloat16)],
        compiler_params=LIMITED,
        name="classify",
    )(ints, *map(resident, (*feats, base, weights, gain)))


def after(value, *others):
    return lax.optimization_barrier((value,) + others)[0]


def per_device(
    tile_features,
    patches,
    det_kernel,
    det_gain,
    det_in,
    det_out,
    det_scale,
    cls_embed,
    cls_merge,
    cls_pos,
    cls_qkv,
    cls_out,
    cls_gain,
    crop_plan,
    slot_from,
):
    sections = lax.axis_size("section")
    count = lax.axis_size(REP)
    section = lax.axis_index("section").astype(jnp.int32)
    core = lax.axis_index("core").astype(jnp.int32)
    width = tile_features.shape[3]
    slabs = width // LANES
    last = sections - 1
    upward = [(index, index + 1) for index in range(count - 1)]
    downward = [(target, origin) for origin, target in upward]
    swap = [(index, index ^ 1) for index in range(count)]
    ints = jnp.concatenate([crop_plan.reshape(-1), slot_from.reshape(-1), section.reshape(1), core.reshape(1)])

    half = packed_half(core.reshape(1), cls_embed, cls_merge, cls_pos, cls_qkv.transpose(1, 0, 2), cls_out)
    weights = lax.all_gather(half, ("section", "core"), axis=0)

    shard = jnp.stack([det_in[0].T, det_out[0]], axis=0)
    line = spread_in_groups(shard, line_groups(True))
    plane = spread_in_groups(after(line, half), line_groups(False))
    cut = cut_pixels(ints, patches.reshape(2, CELLS, patches.shape[3]))
    below = lax.ppermute(ints, REP, upward)
    above = lax.ppermute(ints, REP, downward)
    params = jnp.concatenate(
        [det_kernel[0].reshape(49, width), det_gain, det_scale, jnp.zeros((5, width), jnp.float32)], axis=0
    )
    params = params.reshape(56, slabs, LANES).transpose(1, 0, 2)
    start = tile_features.reshape(2, CELLS, width)
    tiles = [start[0], start[1]]
    early = early_norm(ints, tiles[0], params)
    plane = after(plane, below, above, early, *cut)
    cut = lax.optimization_barrier((*cut, plane))[:3]
    beyond = [(index, index + 1) for index in range(1, count - 1, 2)]
    beyond += [(target, origin) for origin, target in beyond]
    pixels = (lax.ppermute(cut[0], REP, swap), cut[1], lax.ppermute(cut[2], REP, beyond))
    own = plane.reshape((SIDE * SIDE,) + shard.shape)
    other = lax.ppermute(own, REP, swap)

    for number in range(sections):
        if number == 0:
            first = early_block(ints, tiles[0], params, own, other, early)
        else:
            order = after(ints, *pixels) if number == 1 else ints
            first = detector_block(number, order, tiles[0], params, own, other)
        before = (first,) if number == last else ()
        second = detector_block(number, after(ints, first), tiles[1], params, own, other, *before)
        if number < last:
            tiles = [lax.ppermute(tile, "section", [(number, number + 1)]) for tile in (first, second)]

    within = [(last * count + origin, last * count + target) for origin, target in swap]
    across = [(last * count + origin, last * count + target) for origin, target in beyond]
    far = lax.ppermute(second, ("section",) + REP, across)
    near = lax.ppermute(second, ("section",) + REP, within)
    crops = pick_crops(after(ints, weights), below, above, (near, second, far), sections)
    feats = [lax.ppermute(crops[slot], "section", [(last, slot)]) for slot in range(last)] + [crops[last]]
    weights, base = staged(after(ints, *crops), pixels, weights)
    result = classify(ints, feats, base, weights, cls_gain)
    return result[None]


def solution(mesh):
    sections = mesh.shape["section"]
    fine = jax.sharding.Mesh(mesh.devices.reshape(sections, SIDE, SIDE, 2), ("section",) + REP)
    return jax.shard_map(
        per_device,
        mesh=fine,
        in_specs=(
            P(REP, None, None, None),
            P(REP, None, None, None),
            P("section", None, None, None),
            P("section", None),
            P("section", None, REP),
            P("section", REP, None),
            P("section", None),
            P(None, "section"),
            P(None, "section"),
            P(None, "section"),
            P(None, None, "section"),
            P("section", None),
            P(),
            P(REP, None, None, None),
            P(REP, None),
        ),
        out_specs=P(REP, "section", None),
        check_vma=False,
    )
```

```python
import functools
import math

import jax
import jax.numpy as jnp
from jax import lax
from jax.experimental import pallas as pl
from jax.experimental.pallas import tpu as pltpu
from jax.sharding import PartitionSpec as P

HEAD_DIM = 64
TILE = 16
CELLS = TILE * TILE
CROP = 14
ROWS = CROP * CROP
PADDED = 208
LANES = 128
SIDE = 8
REP = ("y", "z", "core")
EPSILON = 1e-06
SLOT_AT = 36
SECTION_AT = 40
CORE_AT = 41
INTS = 42

ANY = pl.BlockSpec(memory_space=pl.ANY)
SMEM = pl.BlockSpec(memory_space=pltpu.SMEM)
VMEM = pl.BlockSpec(memory_space=pltpu.VMEM)
LIMITED = pltpu.CompilerParams(vmem_limit_bytes=16 << 20)


def rep_index(y, z, core):
    return (y * SIDE + z) * 2 + core


def line_groups(first):
    along_z = [[rep_index(y, z, 0 if first else 1) for z in range(SIDE)] for y in range(SIDE)]
    along_y = [[rep_index(y, z, 1 if first else 0) for y in range(SIDE)] for z in range(SIDE)]
    return along_z + along_y


def resident(array):
    return pltpu.with_memory_space_constraint(array, pltpu.VMEM)


def spread_in_groups(block, groups):
    copies = jnp.broadcast_to(block[None], (SIDE,) + block.shape)
    return lax.all_to_all(copies, REP, 0, 0, axis_index_groups=groups)


def in_hbm(array):
    return pltpu.with_memory_space_constraint(array, pltpu.HBM)


def active(number):
    return lax.axis_index("section") == number


def conv_norm(tile_ref, param_ref, normed_ref, wide, conv):
    slabs = wide.shape[0]
    wide[:, :, 0:8, :] = jnp.zeros((slabs, TILE, 8, LANES), jnp.float32)
    wide[:, :, 24:32, :] = jnp.zeros((slabs, TILE, 8, LANES), jnp.float32)
    for slab in range(slabs):
        part = tile_ref[:, slab * LANES : (slab + 1) * LANES].astype(jnp.float32)
        wide[slab, :, 8:24, :] = part.reshape(TILE, TILE, LANES)

    def one_slab(slab, carry):
        sums = [None] * TILE
        for col in range(7):
            taps = [param_ref[slab, pl.ds(row * 7 + col, 1), :] for row in range(7)]
            for source in range(TILE):
                cells = wide[slab, source, pl.ds(5 + col, TILE), :]
                for row in range(7):
                    target = source + 3 - row
                    if 0 <= target < TILE:
                        term = cells * taps[row]
                        sums[target] = term if sums[target] is None else sums[target] + term
        for target in range(TILE):
            conv[slab, pl.ds(target * TILE, TILE), :] = sums[target]
        return carry

    lax.fori_loop(0, slabs, one_slab, 0)
    width = slabs * LANES
    total = conv[0]
    for slab in range(1, slabs):
        total = total + conv[slab]
    mean = jnp.sum(total, axis=-1, keepdims=True) / width
    squares = None
    for slab in range(slabs):
        centred = conv[slab] - mean
        squares = centred * centred if squares is None else squares + centred * centred
    scale = lax.rsqrt(jnp.sum(squares, axis=-1, keepdims=True) / width + EPSILON)
    for slab in range(slabs):
        normed_ref[:, slab * LANES : (slab + 1) * LANES] = (
            (conv[slab] - mean) * scale * param_ref[slab, pl.ds(49, 1), :]
        ).astype(jnp.bfloat16)


def early_body(tile_ref, param_ref, normed_ref, wide, conv):
    @pl.when(active(0))
    def _():
        conv_norm(tile_ref, param_ref, normed_ref, wide, conv)


def conv_scratch(tile):
    cells, width = tile.shape
    slabs = width // LANES
    return [
        pltpu.VMEM((slabs, TILE, 32, LANES), jnp.float32),
        pltpu.VMEM((slabs, cells, LANES), jnp.float32),
    ]


def early_norm(tile, params):
    return pl.pallas_call(
        early_body,
        out_shape=pltpu.VMEM(tile.shape, jnp.bfloat16),
        in_specs=[VMEM, VMEM],
        out_specs=VMEM,
        scratch_shapes=conv_scratch(tile),
        compiler_params=LIMITED,
        name="early_norm",
    )(resident(tile), resident(params))


def mlp(normed_ref, own_ref, other_ref, tile_ref, param_ref, out_ref):
    width = tile_ref.shape[1]
    slabs = width // LANES
    rows = normed_ref[...]
    update = None
    step = 64
    for ref in (own_ref, other_ref):
        for chunk in range(0, ref.shape[0], step):
            into = ref[pl.ds(chunk, step), 0].reshape(step * 16, width)
            outof = ref[pl.ds(chunk, step), 1].reshape(step * 16, width)
            hidden = lax.dot_general(
                rows, into, (((1,), (1,)), ((), ())), preferred_element_type=jnp.float32
            )
            hidden = jax.nn.gelu(hidden, approximate=True).astype(jnp.bfloat16)
            term = jnp.dot(hidden, outof, preferred_element_type=jnp.float32)
            update = term if update is None else update + term
    for slab in range(slabs):
        part = slice(slab * LANES, (slab + 1) * LANES)
        out_ref[:, part] = (
            tile_ref[:, part].astype(jnp.float32) + param_ref[slab, pl.ds(50, 1), :] * update[:, part]
        ).astype(jnp.bfloat16)


def early_block_body(tile_ref, param_ref, own_ref, other_ref, normed_ref, out_ref):
    @pl.when(active(0))
    def _():
        mlp(normed_ref, own_ref, other_ref, tile_ref, param_ref, out_ref)


def block_body(tile_ref, param_ref, own_ref, other_ref, *refs, number):
    before, (out_ref, normed, wide, conv) = refs[:-4], refs[-4:]

    @pl.when(active(number))
    def _():
        conv_norm(tile_ref, param_ref, normed, wide, conv)
        result_ref = out_ref
        if before:
            out_ref[0] = before[0][...]
            result_ref = out_ref.at[1]
        mlp(normed, own_ref, other_ref, tile_ref, param_ref, result_ref)


def early_block(tile, params, own, other, normed):
    return pl.pallas_call(
        early_block_body,
        out_shape=pltpu.VMEM(tile.shape, jnp.bfloat16),
        in_specs=[VMEM] * 5,
        out_specs=VMEM,
        compiler_params=LIMITED,
        name="early_block",
    )(*map(resident, (tile, params, own, other, normed)))


def detector_block(number, tile, params, own, other, *before):
    shape = (2,) + tile.shape if before else tile.shape
    return pl.pallas_call(
        functools.partial(block_body, number=number),
        out_shape=pltpu.VMEM(shape, jnp.bfloat16),
        in_specs=[VMEM] * (4 + len(before)),
        out_specs=VMEM,
        scratch_shapes=[pltpu.VMEM(tile.shape, jnp.bfloat16)] + conv_scratch(tile),
        compiler_params=LIMITED,
        name="detector_block",
    )(*map(resident, (tile, params, own, other, *before)))


def selection(top, left):
    row = lax.broadcasted_iota(jnp.int32, (PADDED, CELLS), 0)
    cell = lax.broadcasted_iota(jnp.int32, (PADDED, CELLS), 1)
    crop_row = (row * 4682) >> 16
    wanted = (top + crop_row) * TILE + left + (row - crop_row * CROP)
    return jnp.where((cell == wanted) & (row < ROWS), 1.0, 0.0).astype(jnp.bfloat16)


def cut_body(ints_ref, tile_ref, *refs):
    out_refs, buffer, sems = refs[:3], refs[3], refs[4]
    core = ints_ref[CORE_AT]
    bases = [ints_ref[SECTION_AT] * 9 + 3 * turn for turn in (2 - 2 * core, 1, 2 * core)]
    copies = []
    for turn, base in enumerate(bases):
        copies.append(pltpu.make_async_copy(tile_ref.at[ints_ref[base]], buffer.at[turn], sems.at[turn]))
        copies[-1].start()
    for turn, base in enumerate(bases):
        chosen = selection(ints_ref[base + 1], ints_ref[base + 2])
        copies[turn].wait()
        rows = jnp.dot(chosen, buffer[turn], preferred_element_type=jnp.float32)
        out_refs[turn][...] = rows.astype(jnp.bfloat16)


def cut_pixels(ints, tiles):
    micro, cells, width = tiles.shape
    return pl.pallas_call(
        cut_body,
        out_shape=[pltpu.VMEM((PADDED, width), jnp.bfloat16)] * 3,
        in_specs=[SMEM, ANY],
        out_specs=[VMEM] * 3,
        scratch_shapes=[pltpu.VMEM((3, cells, width), jnp.bfloat16), pltpu.SemaphoreType.DMA((3,))],
        compiler_params=LIMITED,
        name="cut_pixels",
    )(ints, tiles)


def pick_body(ints_ref, *refs):
    pairs, out_refs = refs[:3], refs[3:]

    @pl.when(active(len(out_refs) - 1))
    def _():
        core = ints_ref[CORE_AT]
        for slot, out_ref in enumerate(out_refs):
            source = ints_ref[SLOT_AT + slot]
            base = slot * 9

            def entry(part, source=source, base=base):
                inner = jnp.where(source == 3, ints_ref[2 * INTS + base + part], ints_ref[base + 3 + part])
                return jnp.where(source == 1, ints_ref[INTS + base + 6 + part], inner)

            same_chip = ((source == 1) & (core == 1)) | ((source == 3) & (core == 0))
            away = (source == 1) | (source == 3)
            micro = entry(0)
            chosen = selection(entry(1), entry(2))
            for pair, wanted in zip(pairs, (same_chip, ~away, away & ~same_chip)):

                @pl.when(wanted)
                def _(chosen=chosen, pair=pair, micro=micro, out_ref=out_ref):
                    rows = jnp.dot(chosen, pair[micro], preferred_element_type=jnp.float32)
                    out_ref[...] = rows.astype(jnp.bfloat16)


def pick_crops(ints, pairs, slots):
    width = pairs[0].shape[2]
    return pl.pallas_call(
        pick_body,
        out_shape=[pltpu.VMEM((PADDED, width), jnp.bfloat16)] * slots,
        in_specs=[SMEM] + [VMEM] * len(pairs),
        out_specs=[VMEM] * slots,
        compiler_params=LIMITED,
        name="pick_crops",
    )(ints, *map(resident, pairs))


EMBED, MERGE, QUERY = 0, 1536, 2560
KEY, VALUE, OUT, POS, HALF = 0, 1024, 2048, 3072, 3584


def pack_body(parity_ref, embed, merge, pos, qkv, out, packed, buffer, sems):
    first = [
        (embed.at[:, pl.ds(0, LANES)], EMBED),
        (embed.at[:, pl.ds(LANES, LANES)], EMBED + 768),
        (merge.at[:, pl.ds(0, LANES)], MERGE),
        (merge.at[:, pl.ds(LANES, LANES)], MERGE + 512),
        (qkv.at[0], QUERY),
    ]
    second = [(qkv.at[1], KEY), (qkv.at[2], VALUE)]
    second += [(out.at[:, pl.ds(column * LANES, LANES)], OUT + column * LANES) for column in range(8)]
    second += [
        (pos.at[:, pl.ds(0, LANES)], POS),
        (pos.at[:, pl.ds(LANES, LANES)], POS + PADDED),
    ]
    for parity, pieces in enumerate((first, second)):

        @pl.when(parity_ref[0] == parity)
        def _(pieces=pieces):
            copies, results = [], []
            for number, (piece, at) in enumerate(pieces):
                place = pl.ds(at, piece.shape[0])
                copies.append(pltpu.make_async_copy(piece, buffer.at[place], sems.at[2 * number]))
                results.append(
                    pltpu.make_async_copy(buffer.at[place], packed.at[place], sems.at[2 * number + 1])
                )
                copies[-1].start()
            for copy, result in zip(copies, results):
                copy.wait()
                result.start()
            for result in results:
                result.wait()


def packed_half(parity, embed, merge, pos, qkv, out):
    return pl.pallas_call(
        pack_body,
        out_shape=jax.ShapeDtypeStruct((HALF, LANES), jnp.bfloat16),
        in_specs=[SMEM] + [ANY] * 5,
        out_specs=ANY,
        scratch_shapes=[pltpu.VMEM((HALF, LANES), jnp.bfloat16), pltpu.SemaphoreType.DMA((24,))],
        compiler_params=LIMITED,
        name="pack_weights",
    )(parity, *map(in_hbm, (embed, merge, pos, qkv, out)))


def columns(ref, section, low, height):
    return jnp.concatenate(
        [ref[section, pl.ds(low, height), :], ref[section, pl.ds(low + height, height), :]], axis=1
    )


def stage_body(ints_ref, pix_near, pix_own, pix_far, packed, weights, base_ref, pix, sems):
    source = ints_ref[SLOT_AT + ints_ref[SECTION_AT]]
    sections = packed.shape[0] // 2
    spans = [(0, EMBED, MERGE), (1, POS, HALF), (0, MERGE, HALF), (1, KEY, POS)]
    copies = []
    for part, low, high in spans:
        for section in range(sections):
            place = (2 * section + part, pl.ds(low, high - low))
            copies.append(
                pltpu.make_async_copy(packed.at[place], weights.at[place], sems.at[1 + len(copies)])
            )
    core = ints_ref[CORE_AT]
    same_chip = ((source == 1) & (core == 1)) | ((source == 3) & (core == 0))
    away = (source == 1) | (source == 3)
    for pix_ref, wanted in ((pix_near, same_chip), (pix_own, ~away), (pix_far, away & ~same_chip)):

        @pl.when(wanted)
        def _(pix_ref=pix_ref):
            copy = pltpu.make_async_copy(pix_ref, pix, sems.at[0])
            copy.start()
            copy.wait()

    for copy in copies:
        copy.start()
    for copy in copies[: 2 * sections]:
        copy.wait()
    rows = pix[...]
    row_ok = lax.broadcasted_iota(jnp.int32, (PADDED, 2 * LANES), 0) < ROWS
    for section in range(sections):
        pos = jnp.where(row_ok, columns(weights, 2 * section + 1, POS, PADDED).astype(jnp.float32), 0.0)
        base_ref[:, pl.ds(section * 2 * LANES, 2 * LANES)] = pos + jnp.dot(
            rows, columns(weights, 2 * section, EMBED, 768), preferred_element_type=jnp.float32
        )
    for copy in copies[2 * sections :]:
        copy.wait()


def staged(ints, pixels, packed):
    width = LANES * packed.shape[0]
    return pl.pallas_call(
        stage_body,
        out_shape=[pltpu.VMEM(packed.shape, jnp.bfloat16), pltpu.VMEM((PADDED, width), jnp.float32)],
        in_specs=[SMEM] + [ANY] * 4,
        out_specs=[VMEM] * 2,
        scratch_shapes=[
            pltpu.VMEM(pixels[0].shape, jnp.bfloat16),
            pltpu.SemaphoreType.DMA((1 + 2 * packed.shape[0],)),
        ],
        compiler_params=LIMITED,
        name="stage_weights",
    )(ints, *map(in_hbm, (*pixels, packed)))


def classify_body(*refs):
    feat_refs = refs[:4]
    base_ref, weights, gain_ref, source_ref, out_ref, feat = refs[4:]
    place = lax.axis_index("section")
    sections = weights.shape[0] // 2
    for number, feat_ref in enumerate(feat_refs):

        @pl.when(place == number)
        def _(feat_ref=feat_ref):
            feat[...] = feat_ref[...]

    feat_rows = feat[...]
    tokens = base_ref[...] + jnp.concatenate(
        [
            jnp.dot(feat_rows, columns(weights, 2 * section, MERGE, 512), preferred_element_type=jnp.float32)
            for section in range(sections)
        ],
        axis=1,
    )
    width = tokens.shape[1]
    mean = jnp.sum(tokens, axis=-1, keepdims=True) / width
    centred = tokens - mean
    var = jnp.sum(centred * centred, axis=-1, keepdims=True) / width
    attn_in = (centred * lax.rsqrt(var + EPSILON) * gain_ref[pl.ds(0, 1), :]).astype(jnp.bfloat16)
    token_sum = jnp.sum(tokens, axis=0, keepdims=True)
    key_ok = lax.broadcasted_iota(jnp.int32, (PADDED, PADDED), 1) < ROWS
    lane = lax.broadcasted_iota(jnp.int32, (PADDED, 2 * HEAD_DIM), 1)
    row_ok = lax.broadcasted_iota(jnp.int32, (PADDED, 2 * HEAD_DIM), 0) < ROWS
    context_sums = []
    for section in range(sections):
        first, second = 2 * section, 2 * section + 1
        piece = jnp.concatenate(
            [
                weights[first, pl.ds(QUERY, 1024), :],
                weights[second, pl.ds(KEY, 1024), :],
                weights[second, pl.ds(VALUE, 1024), :],
            ],
            axis=1,
        )
        qkv = jnp.dot(attn_in, piece, preferred_element_type=jnp.float32).astype(jnp.bfloat16)
        query, key, value = qkv[:, :128], qkv[:, 128:256], qkv[:, 256:]
        contexts = []
        for head in range(2):
            mine = (lane >= HEAD_DIM) if head else (lane < HEAD_DIM)
            scores = lax.dot_general(
                jnp.where(mine, query, jnp.zeros_like(query)),
                key,
                (((1,), (1,)), ((), ())),
                preferred_element_type=jnp.float32,
            ) * (1.0 / math.sqrt(HEAD_DIM))
            scores = jnp.where(key_ok, scores, -jnp.inf)
            top = jnp.max(scores, axis=-1, keepdims=True)
            numer = jnp.exp(scores - top)
            share = 1.0 / jnp.sum(numer, axis=-1, keepdims=True)
            summed = jnp.dot(numer.astype(jnp.bfloat16), value, preferred_element_type=jnp.float32)
            contexts.append(summed * share)
        context = jnp.where(lane < HEAD_DIM, contexts[0], contexts[1]).astype(jnp.bfloat16)
        context = jnp.where(row_ok, context.astype(jnp.float32), 0.0)
        context_sums.append(jnp.sum(context, axis=0, keepdims=True))
    context_mean = jnp.concatenate(context_sums, axis=1) / ROWS
    high = context_mean.astype(jnp.bfloat16)
    rest = context_mean - high.astype(jnp.float32)
    middle = rest.astype(jnp.bfloat16)
    low = (rest - middle.astype(jnp.float32)).astype(jnp.bfloat16)
    pieces = jnp.concatenate([high, middle, low, jnp.zeros((13, high.shape[1]), jnp.bfloat16)], axis=0)
    out_weight = jnp.concatenate(
        [
            jnp.concatenate(
                [weights[2 * section + 1, pl.ds(OUT + LANES * column, LANES), :] for column in range(8)], axis=1
            )
            for section in range(sections)
        ],
        axis=0,
    )
    mixed = jnp.dot(pieces, out_weight, preferred_element_type=jnp.float32)
    pooled = token_sum / ROWS + jnp.sum(mixed, axis=0, keepdims=True)
    pooled_mean = jnp.sum(pooled, axis=-1, keepdims=True) / width
    centred = pooled - pooled_mean
    var = jnp.sum(centred * centred, axis=-1, keepdims=True) / width
    result = centred * lax.rsqrt(var + EPSILON) * gain_ref[pl.ds(1, 1), :]
    out_ref[...] = jnp.where(source_ref[...] == 0, 0.0, result)


def classify(source, feats, base, weights, gain):
    return pl.pallas_call(
        classify_body,
        out_shape=jax.ShapeDtypeStruct((1, gain.shape[1]), jnp.float32),
        in_specs=[VMEM] * 8,
        out_specs=VMEM,
        scratch_shapes=[pltpu.VMEM(feats[0].shape, jnp.bfloat16)],
        compiler_params=LIMITED,
        name="classify",
    )(*map(resident, (*feats, base, weights, gain, source)))


def after(value, *others):
    return lax.optimization_barrier((value,) + others)[0]


def per_device(
    tile_features,
    patches,
    det_kernel,
    det_gain,
    det_in,
    det_out,
    det_scale,
    cls_embed,
    cls_merge,
    cls_pos,
    cls_qkv,
    cls_out,
    cls_gain,
    crop_plan,
    slot_from,
):
    sections = lax.axis_size("section")
    count = lax.axis_size(REP)
    section = lax.axis_index("section").astype(jnp.int32)
    core = lax.axis_index("core").astype(jnp.int32)
    width = tile_features.shape[3]
    slabs = width // LANES
    last = sections - 1
    upward = [(index, index + 1) for index in range(count - 1)]
    downward = [(target, origin) for origin, target in upward]
    swap = [(index, index ^ 1) for index in range(count)]
    ints = jnp.concatenate([crop_plan.reshape(-1), slot_from.reshape(-1), section.reshape(1), core.reshape(1)])

    half = packed_half(core.reshape(1), cls_embed, cls_merge, cls_pos, cls_qkv.transpose(1, 0, 2), cls_out)
    weights = lax.all_gather(half, ("section", "core"), axis=0)

    shard = jnp.stack([det_in[0].T, det_out[0]], axis=0)
    line = spread_in_groups(shard, line_groups(True))
    plane = spread_in_groups(after(line, half), line_groups(False))
    cut = cut_pixels(ints, patches.reshape(2, CELLS, patches.shape[3]))
    below = lax.ppermute(ints, REP, upward)
    above = lax.ppermute(ints, REP, downward)
    params = jnp.concatenate(
        [det_kernel[0].reshape(49, width), det_gain, det_scale, jnp.zeros((5, width), jnp.float32)], axis=0
    )
    params = params.reshape(56, slabs, LANES).transpose(1, 0, 2)
    start = tile_features.reshape(2, CELLS, width)
    tiles = [start[0], start[1]]
    early = early_norm(tiles[0], params)
    every = jnp.concatenate([ints, below, above])
    plane = after(plane, every, early, *cut)
    cut = lax.optimization_barrier((*cut, plane))[:3]
    beyond = [(index, index + 1) for index in range(1, count - 1, 2)]
    beyond += [(target, origin) for origin, target in beyond]
    pixels = (lax.ppermute(cut[0], REP, swap), cut[1], lax.ppermute(cut[2], REP, beyond))
    own = plane.reshape((SIDE * SIDE,) + shard.shape)
    other = lax.ppermute(own, REP, swap)

    for number in range(sections):
        if number == 0:
            first = early_block(tiles[0], params, own, other, early)
        else:
            tile = after(tiles[0], *pixels) if number == 1 else tiles[0]
            first = detector_block(number, tile, params, own, other)
        before = (first,) if number == last else ()
        second = detector_block(number, after(tiles[1], first), params, own, other, *before)
        if number < last:
            tiles = [lax.ppermute(tile, "section", [(number, number + 1)]) for tile in (first, second)]

    within = [(last * count + origin, last * count + target) for origin, target in swap]
    across = [(last * count + origin, last * count + target) for origin, target in beyond]
    far = lax.ppermute(second, ("section",) + REP, across)
    near = lax.ppermute(second, ("section",) + REP, within)
    crops = pick_crops(after(every, weights), (near, second, far), sections)
    feats = [lax.ppermute(crops[slot], "section", [(last, slot)]) for slot in range(last)] + [crops[last]]
    weights, base = staged(after(ints, *crops), pixels, weights)
    source = lax.dynamic_index_in_dim(slot_from[0], section, 0)
    source = jnp.broadcast_to(source[None], (1, cls_gain.shape[1]))
    result = classify(source, feats, base, weights, cls_gain)
    return result[None]


def solution(mesh):
    sections = mesh.shape["section"]
    fine = jax.sharding.Mesh(mesh.devices.reshape(sections, SIDE, SIDE, 2), ("section",) + REP)
    return jax.shard_map(
        per_device,
        mesh=fine,
        in_specs=(
            P(REP, None, None, None),
            P(REP, None, None, None),
            P("section", None, None, None),
            P("section", None),
            P("section", None, REP),
            P("section", REP, None),
            P("section", None),
            P(None, "section"),
            P(None, "section"),
            P(None, "section"),
            P(None, None, "section"),
            P("section", None),
            P(),
            P(REP, None, None, None),
            P(REP, None),
        ),
        out_specs=P(REP, "section", None),
        check_vma=False,
    )
```

```python
import functools
import math

import jax
import jax.numpy as jnp
from jax import lax
from jax.experimental import pallas as pl
from jax.experimental.pallas import tpu as pltpu
from jax.sharding import PartitionSpec as P

HEAD_DIM = 64
TILE = 16
CELLS = TILE * TILE
CROP = 14
ROWS = CROP * CROP
PADDED = 208
LANES = 128
SIDE = 8
REP = ("y", "z", "core")
EPSILON = 1e-06
SLOT_AT = 36
SECTION_AT = 40
CORE_AT = 41
INTS = 42

ANY = pl.BlockSpec(memory_space=pl.ANY)
SMEM = pl.BlockSpec(memory_space=pltpu.SMEM)
VMEM = pl.BlockSpec(memory_space=pltpu.VMEM)
LIMITED = pltpu.CompilerParams(vmem_limit_bytes=16 << 20)


def rep_index(y, z, core):
    return (y * SIDE + z) * 2 + core


def line_groups(first):
    along_z = [[rep_index(y, z, 0 if first else 1) for z in range(SIDE)] for y in range(SIDE)]
    along_y = [[rep_index(y, z, 1 if first else 0) for y in range(SIDE)] for z in range(SIDE)]
    return along_z + along_y


def resident(array):
    return pltpu.with_memory_space_constraint(array, pltpu.VMEM)


def spread_in_groups(block, groups):
    copies = jnp.broadcast_to(block[None], (SIDE,) + block.shape)
    return lax.all_to_all(copies, REP, 0, 0, axis_index_groups=groups)


def in_hbm(array):
    return pltpu.with_memory_space_constraint(array, pltpu.HBM)


def active(number):
    return lax.axis_index("section") == number


def conv_norm(tile_ref, param_ref, normed_ref, wide, conv):
    slabs = wide.shape[0]
    wide[:, :, 0:8, :] = jnp.zeros((slabs, TILE, 8, LANES), jnp.float32)
    wide[:, :, 24:32, :] = jnp.zeros((slabs, TILE, 8, LANES), jnp.float32)
    for slab in range(slabs):
        part = tile_ref[:, slab * LANES : (slab + 1) * LANES].astype(jnp.float32)
        wide[slab, :, 8:24, :] = part.reshape(TILE, TILE, LANES)

    def one_slab(slab, carry):
        sums = [None] * TILE
        for col in range(7):
            taps = [param_ref[slab, pl.ds(row * 7 + col, 1), :] for row in range(7)]
            for source in range(TILE):
                cells = wide[slab, source, pl.ds(5 + col, TILE), :]
                for row in range(7):
                    target = source + 3 - row
                    if 0 <= target < TILE:
                        term = cells * taps[row]
                        sums[target] = term if sums[target] is None else sums[target] + term
        for target in range(TILE):
            conv[slab, pl.ds(target * TILE, TILE), :] = sums[target]
        return carry

    lax.fori_loop(0, slabs, one_slab, 0)
    width = slabs * LANES
    total = conv[0]
    for slab in range(1, slabs):
        total = total + conv[slab]
    mean = jnp.sum(total, axis=-1, keepdims=True) / width
    squares = None
    for slab in range(slabs):
        centred = conv[slab] - mean
        squares = centred * centred if squares is None else squares + centred * centred
    scale = lax.rsqrt(jnp.sum(squares, axis=-1, keepdims=True) / width + EPSILON)
    for slab in range(slabs):
        normed_ref[:, slab * LANES : (slab + 1) * LANES] = (
            (conv[slab] - mean) * scale * param_ref[slab, pl.ds(49, 1), :]
        ).astype(jnp.bfloat16)


def early_body(tile_ref, param_ref, normed_ref, wide, conv):
    @pl.when(active(0))
    def _():
        conv_norm(tile_ref, param_ref, normed_ref, wide, conv)


def conv_scratch(tile):
    cells, width = tile.shape
    slabs = width // LANES
    return [
        pltpu.VMEM((slabs, TILE, 32, LANES), jnp.float32),
        pltpu.VMEM((slabs, cells, LANES), jnp.float32),
    ]


def early_norm(tile, params):
    return pl.pallas_call(
        early_body,
        out_shape=pltpu.VMEM(tile.shape, jnp.bfloat16),
        in_specs=[VMEM, VMEM],
        out_specs=VMEM,
        scratch_shapes=conv_scratch(tile),
        compiler_params=LIMITED,
        name="early_norm",
    )(resident(tile), resident(params))


def mlp(normed_ref, own_ref, other_ref, tile_ref, param_ref, out_ref):
    width = tile_ref.shape[1]
    slabs = width // LANES
    rows = normed_ref[...]
    update = None
    step = 64
    for ref in (own_ref, other_ref):
        for chunk in range(0, ref.shape[0], step):
            into = ref[pl.ds(chunk, step), 0].reshape(step * 16, width)
            outof = ref[pl.ds(chunk, step), 1].reshape(step * 16, width)
            hidden = lax.dot_general(
                rows, into, (((1,), (1,)), ((), ())), preferred_element_type=jnp.float32
            )
            hidden = jax.nn.gelu(hidden, approximate=True).astype(jnp.bfloat16)
            term = jnp.dot(hidden, outof, preferred_element_type=jnp.float32)
            update = term if update is None else update + term
    for slab in range(slabs):
        part = slice(slab * LANES, (slab + 1) * LANES)
        out_ref[:, part] = (
            tile_ref[:, part].astype(jnp.float32) + param_ref[slab, pl.ds(50, 1), :] * update[:, part]
        ).astype(jnp.bfloat16)


def early_block_body(tile_ref, param_ref, own_ref, other_ref, normed_ref, out_ref):
    @pl.when(active(0))
    def _():
        mlp(normed_ref, own_ref, other_ref, tile_ref, param_ref, out_ref)


def block_body(tile_ref, param_ref, own_ref, other_ref, *refs, number):
    rest, (out_ref, normed, wide, conv) = refs[:-4], refs[-4:]

    @pl.when(active(number))
    def _():
        conv_norm(tile_ref, param_ref, normed, wide, conv)
        mlp(normed, own_ref, other_ref, tile_ref, param_ref, out_ref)
        if rest:
            before_ref, pair_ref = rest
            pair_ref[0] = before_ref[...]
            pair_ref[1] = out_ref[...]


def early_block(tile, params, own, other, normed):
    return pl.pallas_call(
        early_block_body,
        out_shape=pltpu.VMEM(tile.shape, jnp.bfloat16),
        in_specs=[VMEM] * 5,
        out_specs=VMEM,
        compiler_params=LIMITED,
        name="early_block",
    )(*map(resident, (tile, params, own, other, normed)))


def detector_block(number, tile, params, own, other, *before):
    out_shape = [pltpu.VMEM((2,) + tile.shape, jnp.bfloat16)] * len(before)
    out_shape += [pltpu.VMEM(tile.shape, jnp.bfloat16)]
    return pl.pallas_call(
        functools.partial(block_body, number=number),
        out_shape=out_shape,
        in_specs=[VMEM] * (4 + len(before)),
        out_specs=[VMEM] * len(out_shape),
        scratch_shapes=[pltpu.VMEM(tile.shape, jnp.bfloat16)] + conv_scratch(tile),
        compiler_params=LIMITED,
        name="detector_block",
    )(*map(resident, (tile, params, own, other, *before)))


def selection(top, left):
    row = lax.broadcasted_iota(jnp.int32, (PADDED, CELLS), 0)
    cell = lax.broadcasted_iota(jnp.int32, (PADDED, CELLS), 1)
    crop_row = (row * 4682) >> 16
    wanted = (top + crop_row) * TILE + left + (row - crop_row * CROP)
    return jnp.where((cell == wanted) & (row < ROWS), 1.0, 0.0).astype(jnp.bfloat16)


def cut_body(ints_ref, tile_ref, *refs):
    out_refs, buffer, sems = refs[:3], refs[3], refs[4]
    core = ints_ref[CORE_AT]
    bases = [ints_ref[SECTION_AT] * 9 + 3 * turn for turn in (2 - 2 * core, 1, 2 * core)]
    copies = []
    for turn, base in enumerate(bases):
        copies.append(pltpu.make_async_copy(tile_ref.at[ints_ref[base]], buffer.at[turn], sems.at[turn]))
        copies[-1].start()
    for turn, base in enumerate(bases):
        chosen = selection(ints_ref[base + 1], ints_ref[base + 2])
        copies[turn].wait()
        rows = jnp.dot(chosen, buffer[turn], preferred_element_type=jnp.float32)
        out_refs[turn][...] = rows.astype(jnp.bfloat16)


def cut_pixels(ints, tiles):
    micro, cells, width = tiles.shape
    return pl.pallas_call(
        cut_body,
        out_shape=[pltpu.VMEM((PADDED, width), jnp.bfloat16)] * 3,
        in_specs=[SMEM, ANY],
        out_specs=[VMEM] * 3,
        scratch_shapes=[pltpu.VMEM((3, cells, width), jnp.bfloat16), pltpu.SemaphoreType.DMA((3,))],
        compiler_params=LIMITED,
        name="cut_pixels",
    )(ints, tiles)


def pick_body(ints_ref, *refs):
    pairs, far_refs, out_refs = refs[:2], refs[2:4], refs[4:]

    @pl.when(active(len(out_refs) - 1))
    def _():
        core = ints_ref[CORE_AT]
        for slot, out_ref in enumerate(out_refs):
            source = ints_ref[SLOT_AT + slot]
            base = slot * 9

            def entry(part, source=source, base=base):
                inner = jnp.where(source == 3, ints_ref[2 * INTS + base + part], ints_ref[base + 3 + part])
                return jnp.where(source == 1, ints_ref[INTS + base + 6 + part], inner)

            same_chip = ((source == 1) & (core == 1)) | ((source == 3) & (core == 0))
            away = (source == 1) | (source == 3)
            micro = entry(0)
            chosen = selection(entry(1), entry(2))
            for index, far_ref in enumerate(far_refs):

                @pl.when(away & ~same_chip & (micro == index))
                def _(chosen=chosen, far_ref=far_ref, out_ref=out_ref):
                    rows = jnp.dot(chosen, far_ref[...], preferred_element_type=jnp.float32)
                    out_ref[...] = rows.astype(jnp.bfloat16)

            for pair, wanted in zip(pairs, (same_chip, ~away)):

                @pl.when(wanted)
                def _(chosen=chosen, pair=pair, micro=micro, out_ref=out_ref):
                    rows = jnp.dot(chosen, pair[micro], preferred_element_type=jnp.float32)
                    out_ref[...] = rows.astype(jnp.bfloat16)


def pick_crops(ints, pairs, slots):
    width = pairs[-1].shape[1]
    return pl.pallas_call(
        pick_body,
        out_shape=[pltpu.VMEM((PADDED, width), jnp.bfloat16)] * slots,
        in_specs=[SMEM] + [VMEM] * len(pairs),
        out_specs=[VMEM] * slots,
        compiler_params=LIMITED,
        name="pick_crops",
    )(ints, *map(resident, pairs))


EMBED, MERGE, QUERY = 0, 1536, 2560
KEY, VALUE, OUT, POS, HALF = 0, 1024, 2048, 3072, 3584


def pack_body(parity_ref, embed, merge, pos, qkv, out, packed, buffer, sems):
    first = [
        (embed.at[:, pl.ds(0, LANES)], EMBED),
        (embed.at[:, pl.ds(LANES, LANES)], EMBED + 768),
        (merge.at[:, pl.ds(0, LANES)], MERGE),
        (merge.at[:, pl.ds(LANES, LANES)], MERGE + 512),
        (qkv.at[0], QUERY),
    ]
    second = [(qkv.at[1], KEY), (qkv.at[2], VALUE)]
    second += [(out.at[:, pl.ds(column * LANES, LANES)], OUT + column * LANES) for column in range(8)]
    second += [
        (pos.at[:, pl.ds(0, LANES)], POS),
        (pos.at[:, pl.ds(LANES, LANES)], POS + PADDED),
    ]
    for parity, pieces in enumerate((first, second)):

        @pl.when(parity_ref[0] == parity)
        def _(pieces=pieces):
            copies, results = [], []
            for number, (piece, at) in enumerate(pieces):
                place = pl.ds(at, piece.shape[0])
                copies.append(pltpu.make_async_copy(piece, buffer.at[place], sems.at[2 * number]))
                results.append(
                    pltpu.make_async_copy(buffer.at[place], packed.at[place], sems.at[2 * number + 1])
                )
                copies[-1].start()
            for copy, result in zip(copies, results):
                copy.wait()
                result.start()
            for result in results:
                result.wait()


def packed_half(parity, embed, merge, pos, qkv, out):
    return pl.pallas_call(
        pack_body,
        out_shape=jax.ShapeDtypeStruct((HALF, LANES), jnp.bfloat16),
        in_specs=[SMEM] + [ANY] * 5,
        out_specs=ANY,
        scratch_shapes=[pltpu.VMEM((HALF, LANES), jnp.bfloat16), pltpu.SemaphoreType.DMA((24,))],
        compiler_params=LIMITED,
        name="pack_weights",
    )(parity, *map(in_hbm, (embed, merge, pos, qkv, out)))


def columns(ref, section, low, height):
    return jnp.concatenate(
        [ref[section, pl.ds(low, height), :], ref[section, pl.ds(low + height, height), :]], axis=1
    )


def stage_body(ints_ref, pix_near, pix_own, pix_far, packed, weights, base_ref, pix, sems):
    source = ints_ref[SLOT_AT + ints_ref[SECTION_AT]]
    sections = packed.shape[0] // 2
    spans = [(0, EMBED, MERGE), (1, POS, HALF), (0, MERGE, HALF), (1, KEY, POS)]
    copies = []
    for part, low, high in spans:
        for section in range(sections):
            place = (2 * section + part, pl.ds(low, high - low))
            copies.append(
                pltpu.make_async_copy(packed.at[place], weights.at[place], sems.at[1 + len(copies)])
            )
    core = ints_ref[CORE_AT]
    same_chip = ((source == 1) & (core == 1)) | ((source == 3) & (core == 0))
    away = (source == 1) | (source == 3)
    for pix_ref, wanted in ((pix_near, same_chip), (pix_own, ~away), (pix_far, away & ~same_chip)):

        @pl.when(wanted)
        def _(pix_ref=pix_ref):
            copy = pltpu.make_async_copy(pix_ref, pix, sems.at[0])
            copy.start()
            copy.wait()

    for copy in copies:
        copy.start()
    for copy in copies[: 2 * sections]:
        copy.wait()
    rows = pix[...]
    row_ok = lax.broadcasted_iota(jnp.int32, (PADDED, 2 * LANES), 0) < ROWS
    for section in range(sections):
        pos = jnp.where(row_ok, columns(weights, 2 * section + 1, POS, PADDED).astype(jnp.float32), 0.0)
        base_ref[:, pl.ds(section * 2 * LANES, 2 * LANES)] = pos + jnp.dot(
            rows, columns(weights, 2 * section, EMBED, 768), preferred_element_type=jnp.float32
        )
    for copy in copies[2 * sections :]:
        copy.wait()


def staged(ints, pixels, packed):
    width = LANES * packed.shape[0]
    return pl.pallas_call(
        stage_body,
        out_shape=[pltpu.VMEM(packed.shape, jnp.bfloat16), pltpu.VMEM((PADDED, width), jnp.float32)],
        in_specs=[SMEM] + [ANY] * 4,
        out_specs=[VMEM] * 2,
        scratch_shapes=[
            pltpu.VMEM(pixels[0].shape, jnp.bfloat16),
            pltpu.SemaphoreType.DMA((1 + 2 * packed.shape[0],)),
        ],
        compiler_params=LIMITED,
        name="stage_weights",
    )(ints, *map(in_hbm, (*pixels, packed)))


def classify_body(*refs):
    feat_refs = refs[:4]
    base_ref, weights, gain_ref, source_ref, out_ref, feat = refs[4:]
    place = lax.axis_index("section")
    sections = weights.shape[0] // 2
    for number, feat_ref in enumerate(feat_refs):

        @pl.when(place == number)
        def _(feat_ref=feat_ref):
            feat[...] = feat_ref[...]

    feat_rows = feat[...]
    tokens = base_ref[...] + jnp.concatenate(
        [
            jnp.dot(feat_rows, columns(weights, 2 * section, MERGE, 512), preferred_element_type=jnp.float32)
            for section in range(sections)
        ],
        axis=1,
    )
    width = tokens.shape[1]
    mean = jnp.sum(tokens, axis=-1, keepdims=True) / width
    centred = tokens - mean
    var = jnp.sum(centred * centred, axis=-1, keepdims=True) / width
    attn_in = (centred * lax.rsqrt(var + EPSILON) * gain_ref[pl.ds(0, 1), :]).astype(jnp.bfloat16)
    token_sum = jnp.sum(tokens, axis=0, keepdims=True)
    key_ok = lax.broadcasted_iota(jnp.int32, (PADDED, PADDED), 1) < ROWS
    lane = lax.broadcasted_iota(jnp.int32, (PADDED, 2 * HEAD_DIM), 1)
    row_ok = lax.broadcasted_iota(jnp.int32, (PADDED, 2 * HEAD_DIM), 0) < ROWS
    context_sums = []
    for section in range(sections):
        first, second = 2 * section, 2 * section + 1
        piece = jnp.concatenate(
            [
                weights[first, pl.ds(QUERY, 1024), :],
                weights[second, pl.ds(KEY, 1024), :],
                weights[second, pl.ds(VALUE, 1024), :],
            ],
            axis=1,
        )
        qkv = jnp.dot(attn_in, piece, preferred_element_type=jnp.float32).astype(jnp.bfloat16)
        query, key, value = qkv[:, :128], qkv[:, 128:256], qkv[:, 256:]
        contexts = []
        for head in range(2):
            mine = (lane >= HEAD_DIM) if head else (lane < HEAD_DIM)
            scores = lax.dot_general(
                jnp.where(mine, query, jnp.zeros_like(query)),
                key,
                (((1,), (1,)), ((), ())),
                preferred_element_type=jnp.float32,
            ) * (1.0 / math.sqrt(HEAD_DIM))
            scores = jnp.where(key_ok, scores, -jnp.inf)
            top = jnp.max(scores, axis=-1, keepdims=True)
            numer = jnp.exp(scores - top)
            share = 1.0 / jnp.sum(numer, axis=-1, keepdims=True)
            summed = jnp.dot(numer.astype(jnp.bfloat16), value, preferred_element_type=jnp.float32)
            contexts.append(summed * share)
        context = jnp.where(lane < HEAD_DIM, contexts[0], contexts[1]).astype(jnp.bfloat16)
        context = jnp.where(row_ok, context.astype(jnp.float32), 0.0)
        context_sums.append(jnp.sum(context, axis=0, keepdims=True))
    context_mean = jnp.concatenate(context_sums, axis=1) / ROWS
    high = context_mean.astype(jnp.bfloat16)
    rest = context_mean - high.astype(jnp.float32)
    middle = rest.astype(jnp.bfloat16)
    low = (rest - middle.astype(jnp.float32)).astype(jnp.bfloat16)
    pieces = jnp.concatenate([high, middle, low, jnp.zeros((13, high.shape[1]), jnp.bfloat16)], axis=0)
    out_weight = jnp.concatenate(
        [
            jnp.concatenate(
                [weights[2 * section + 1, pl.ds(OUT + LANES * column, LANES), :] for column in range(8)], axis=1
            )
            for section in range(sections)
        ],
        axis=0,
    )
    mixed = jnp.dot(pieces, out_weight, preferred_element_type=jnp.float32)
    pooled = token_sum / ROWS + jnp.sum(mixed, axis=0, keepdims=True)
    pooled_mean = jnp.sum(pooled, axis=-1, keepdims=True) / width
    centred = pooled - pooled_mean
    var = jnp.sum(centred * centred, axis=-1, keepdims=True) / width
    result = centred * lax.rsqrt(var + EPSILON) * gain_ref[pl.ds(1, 1), :]
    out_ref[...] = jnp.where(source_ref[...] == 0, 0.0, result)


def classify(source, feats, base, weights, gain):
    return pl.pallas_call(
        classify_body,
        out_shape=jax.ShapeDtypeStruct((1, gain.shape[1]), jnp.float32),
        in_specs=[VMEM] * 8,
        out_specs=VMEM,
        scratch_shapes=[pltpu.VMEM(feats[0].shape, jnp.bfloat16)],
        compiler_params=LIMITED,
        name="classify",
    )(*map(resident, (*feats, base, weights, gain, source)))


def after(value, *others):
    return lax.optimization_barrier((value,) + others)[0]


def per_device(
    tile_features,
    patches,
    det_kernel,
    det_gain,
    det_in,
    det_out,
    det_scale,
    cls_embed,
    cls_merge,
    cls_pos,
    cls_qkv,
    cls_out,
    cls_gain,
    crop_plan,
    slot_from,
):
    sections = lax.axis_size("section")
    count = lax.axis_size(REP)
    section = lax.axis_index("section").astype(jnp.int32)
    core = lax.axis_index("core").astype(jnp.int32)
    width = tile_features.shape[3]
    slabs = width // LANES
    last = sections - 1
    upward = [(index, index + 1) for index in range(count - 1)]
    downward = [(target, origin) for origin, target in upward]
    swap = [(index, index ^ 1) for index in range(count)]
    ints = jnp.concatenate([crop_plan.reshape(-1), slot_from.reshape(-1), section.reshape(1), core.reshape(1)])

    half = packed_half(core.reshape(1), cls_embed, cls_merge, cls_pos, cls_qkv.transpose(1, 0, 2), cls_out)
    weights = lax.all_gather(half, ("section", "core"), axis=0)

    shard = jnp.stack([det_in[0].T, det_out[0]], axis=0)
    line = spread_in_groups(shard, line_groups(True))
    plane = spread_in_groups(after(line, half), line_groups(False))
    cut = cut_pixels(ints, patches.reshape(2, CELLS, patches.shape[3]))
    below = lax.ppermute(ints, REP, upward)
    above = lax.ppermute(ints, REP, downward)
    params = jnp.concatenate(
        [det_kernel[0].reshape(49, width), det_gain, det_scale, jnp.zeros((5, width), jnp.float32)], axis=0
    )
    params = params.reshape(56, slabs, LANES).transpose(1, 0, 2)
    start = tile_features.reshape(2, CELLS, width)
    tiles = [start[0], start[1]]
    early = early_norm(tiles[0], params)
    every = jnp.concatenate([ints, below, above])
    source = lax.dynamic_index_in_dim(slot_from[0], section, 0)
    source = jnp.broadcast_to(source[None], (1, cls_gain.shape[1]))
    plane, source = lax.optimization_barrier((plane, source, every, early, *cut))[:2]
    cut = lax.optimization_barrier((*cut, plane))[:3]
    beyond = [(index, index + 1) for index in range(1, count - 1, 2)]
    beyond += [(target, origin) for origin, target in beyond]
    pixels = (lax.ppermute(cut[0], REP, swap), cut[1], lax.ppermute(cut[2], REP, beyond))
    own = plane.reshape((SIDE * SIDE,) + shard.shape)
    other = lax.ppermute(own, REP, swap)

    for number in range(sections):
        if number == 0:
            first = early_block(tiles[0], params, own, other, early)
        else:
            tile = after(tiles[0], *pixels) if number == 1 else tiles[0]
            (first,) = detector_block(number, tile, params, own, other)
        before = (first,) if number == last else ()
        *pair, second = detector_block(number, after(tiles[1], first), params, own, other, *before)
        if number < last:
            tiles = [lax.ppermute(tile, "section", [(number, number + 1)]) for tile in (first, second)]

    within = [(last * count + origin, last * count + target) for origin, target in swap]
    across = [(last * count + origin, last * count + target) for origin, target in beyond]
    far_first = lax.ppermute(first, ("section",) + REP, across)
    far_second = lax.ppermute(after(second, far_first), ("section",) + REP, across)
    near = lax.ppermute(pair[0], ("section",) + REP, within)
    crops = pick_crops(after(every, weights), (near, pair[0], far_first, far_second), sections)
    feats = [lax.ppermute(crops[slot], "section", [(last, slot)]) for slot in range(last)] + [crops[last]]
    weights, base = staged(after(ints, *crops), pixels, weights)
    result = classify(source, feats, base, weights, cls_gain)
    return result[None]


def solution(mesh):
    sections = mesh.shape["section"]
    fine = jax.sharding.Mesh(mesh.devices.reshape(sections, SIDE, SIDE, 2), ("section",) + REP)
    return jax.shard_map(
        per_device,
        mesh=fine,
        in_specs=(
            P(REP, None, None, None),
            P(REP, None, None, None),
            P("section", None, None, None),
            P("section", None),
            P("section", None, REP),
            P("section", REP, None),
            P("section", None),
            P(None, "section"),
            P(None, "section"),
            P(None, "section"),
            P(None, None, "section"),
            P("section", None),
            P(),
            P(REP, None, None, None),
            P(REP, None),
        ),
        out_specs=P(REP, "section", None),
        check_vma=False,
    )
```

```python
import functools
import math

import jax
import jax.numpy as jnp
from jax import lax
from jax.experimental import pallas as pl
from jax.experimental.pallas import tpu as pltpu
from jax.sharding import PartitionSpec as P

HEAD_DIM = 64
TILE = 16
CELLS = TILE * TILE
CROP = 14
ROWS = CROP * CROP
PADDED = 208
LANES = 128
SIDE = 8
REP = ("y", "z", "core")
EPSILON = 1e-06
SLOT_AT = 36
SECTION_AT = 40
CORE_AT = 41
INTS = 42

ANY = pl.BlockSpec(memory_space=pl.ANY)
SMEM = pl.BlockSpec(memory_space=pltpu.SMEM)
VMEM = pl.BlockSpec(memory_space=pltpu.VMEM)
LIMITED = pltpu.CompilerParams(vmem_limit_bytes=16 << 20)


def rep_index(y, z, core):
    return (y * SIDE + z) * 2 + core


def line_groups(first):
    along_z = [[rep_index(y, z, 0 if first else 1) for z in range(SIDE)] for y in range(SIDE)]
    along_y = [[rep_index(y, z, 1 if first else 0) for y in range(SIDE)] for z in range(SIDE)]
    return along_z + along_y


def resident(array):
    return pltpu.with_memory_space_constraint(array, pltpu.VMEM)


def spread_in_groups(block, groups):
    copies = jnp.broadcast_to(block[None], (SIDE,) + block.shape)
    return lax.all_to_all(copies, REP, 0, 0, axis_index_groups=groups)


def in_hbm(array):
    return pltpu.with_memory_space_constraint(array, pltpu.HBM)


def active(number):
    return lax.axis_index("section") == number


def conv_norm(tile_ref, param_ref, normed_ref, wide, conv):
    slabs = wide.shape[0]
    wide[:, :, 0:8, :] = jnp.zeros((slabs, TILE, 8, LANES), jnp.float32)
    wide[:, :, 24:32, :] = jnp.zeros((slabs, TILE, 8, LANES), jnp.float32)
    for slab in range(slabs):
        part = tile_ref[:, slab * LANES : (slab + 1) * LANES].astype(jnp.float32)
        wide[slab, :, 8:24, :] = part.reshape(TILE, TILE, LANES)

    def one_slab(slab, carry):
        sums = [None] * TILE
        for col in range(7):
            taps = [param_ref[slab, pl.ds(row * 7 + col, 1), :] for row in range(7)]
            for source in range(TILE):
                cells = wide[slab, source, pl.ds(5 + col, TILE), :]
                for row in range(7):
                    target = source + 3 - row
                    if 0 <= target < TILE:
                        term = cells * taps[row]
                        sums[target] = term if sums[target] is None else sums[target] + term
        for target in range(TILE):
            conv[slab, pl.ds(target * TILE, TILE), :] = sums[target]
        return carry

    lax.fori_loop(0, slabs, one_slab, 0)
    width = slabs * LANES
    total = conv[0]
    for slab in range(1, slabs):
        total = total + conv[slab]
    mean = jnp.sum(total, axis=-1, keepdims=True) / width
    squares = None
    for slab in range(slabs):
        centred = conv[slab] - mean
        squares = centred * centred if squares is None else squares + centred * centred
    scale = lax.rsqrt(jnp.sum(squares, axis=-1, keepdims=True) / width + EPSILON)
    for slab in range(slabs):
        normed_ref[:, slab * LANES : (slab + 1) * LANES] = (
            (conv[slab] - mean) * scale * param_ref[slab, pl.ds(49, 1), :]
        ).astype(jnp.bfloat16)


def early_body(tile_ref, param_ref, normed_ref, wide, conv):
    @pl.when(active(0))
    def _():
        conv_norm(tile_ref, param_ref, normed_ref, wide, conv)


def conv_scratch(tile):
    cells, width = tile.shape
    slabs = width // LANES
    return [
        pltpu.VMEM((slabs, TILE, 32, LANES), jnp.float32),
        pltpu.VMEM((slabs, cells, LANES), jnp.float32),
    ]


def early_norm(tile, params):
    return pl.pallas_call(
        early_body,
        out_shape=pltpu.VMEM(tile.shape, jnp.bfloat16),
        in_specs=[VMEM, VMEM],
        out_specs=VMEM,
        scratch_shapes=conv_scratch(tile),
        compiler_params=LIMITED,
        name="early_norm",
    )(resident(tile), resident(params))


def mlp(normed_ref, own_ref, other_ref, tile_ref, param_ref, out_ref):
    width = tile_ref.shape[1]
    slabs = width // LANES
    rows = normed_ref[...]
    update = None
    step = 64
    for ref in (own_ref, other_ref):
        for chunk in range(0, ref.shape[0], step):
            into = ref[pl.ds(chunk, step), 0].reshape(step * 16, width)
            outof = ref[pl.ds(chunk, step), 1].reshape(step * 16, width)
            hidden = lax.dot_general(
                rows, into, (((1,), (1,)), ((), ())), preferred_element_type=jnp.float32
            )
            hidden = jax.nn.gelu(hidden, approximate=True).astype(jnp.bfloat16)
            term = jnp.dot(hidden, outof, preferred_element_type=jnp.float32)
            update = term if update is None else update + term
    for slab in range(slabs):
        part = slice(slab * LANES, (slab + 1) * LANES)
        out_ref[:, part] = (
            tile_ref[:, part].astype(jnp.float32) + param_ref[slab, pl.ds(50, 1), :] * update[:, part]
        ).astype(jnp.bfloat16)


def early_block_body(tile_ref, param_ref, own_ref, other_ref, normed_ref, out_ref):
    @pl.when(active(0))
    def _():
        mlp(normed_ref, own_ref, other_ref, tile_ref, param_ref, out_ref)


def block_body(tile_ref, param_ref, own_ref, other_ref, *refs, number):
    rest, (out_ref, normed, wide, conv) = refs[:-4], refs[-4:]

    @pl.when(active(number))
    def _():
        conv_norm(tile_ref, param_ref, normed, wide, conv)
        mlp(normed, own_ref, other_ref, tile_ref, param_ref, out_ref)
        if rest:
            before_ref, pair_ref = rest
            pair_ref[0] = before_ref[...]
            pair_ref[1] = out_ref[...]


def early_block(tile, params, own, other, normed):
    return pl.pallas_call(
        early_block_body,
        out_shape=pltpu.VMEM(tile.shape, jnp.bfloat16),
        in_specs=[VMEM] * 5,
        out_specs=VMEM,
        compiler_params=LIMITED,
        name="early_block",
    )(*map(resident, (tile, params, own, other, normed)))


def detector_block(number, tile, params, own, other, *before):
    out_shape = [pltpu.VMEM((2,) + tile.shape, jnp.bfloat16)] * len(before)
    out_shape += [pltpu.VMEM(tile.shape, jnp.bfloat16)]
    return pl.pallas_call(
        functools.partial(block_body, number=number),
        out_shape=out_shape,
        in_specs=[VMEM] * (4 + len(before)),
        out_specs=[VMEM] * len(out_shape),
        scratch_shapes=[pltpu.VMEM(tile.shape, jnp.bfloat16)] + conv_scratch(tile),
        compiler_params=LIMITED,
        name="detector_block",
    )(*map(resident, (tile, params, own, other, *before)))


def selection(top, left):
    row = lax.broadcasted_iota(jnp.int32, (PADDED, CELLS), 0)
    cell = lax.broadcasted_iota(jnp.int32, (PADDED, CELLS), 1)
    crop_row = (row * 4682) >> 16
    wanted = (top + crop_row) * TILE + left + (row - crop_row * CROP)
    return jnp.where((cell == wanted) & (row < ROWS), 1.0, 0.0).astype(jnp.bfloat16)


def cut_body(ints_ref, tile_ref, *refs):
    out_refs, buffer, sems = refs[:3], refs[3], refs[4]
    core = ints_ref[CORE_AT]
    bases = [ints_ref[SECTION_AT] * 9 + 3 * turn for turn in (2 - 2 * core, 1, 2 * core)]
    copies = []
    for turn, base in enumerate(bases):
        copies.append(pltpu.make_async_copy(tile_ref.at[ints_ref[base]], buffer.at[turn], sems.at[turn]))
        copies[-1].start()
    for turn, base in enumerate(bases):
        chosen = selection(ints_ref[base + 1], ints_ref[base + 2])
        copies[turn].wait()
        rows = jnp.dot(chosen, buffer[turn], preferred_element_type=jnp.float32)
        out_refs[turn][...] = rows.astype(jnp.bfloat16)


def cut_pixels(ints, tiles):
    micro, cells, width = tiles.shape
    return pl.pallas_call(
        cut_body,
        out_shape=[pltpu.VMEM((PADDED, width), jnp.bfloat16)] * 3,
        in_specs=[SMEM, ANY],
        out_specs=[VMEM] * 3,
        scratch_shapes=[pltpu.VMEM((3, cells, width), jnp.bfloat16), pltpu.SemaphoreType.DMA((3,))],
        compiler_params=LIMITED,
        name="cut_pixels",
    )(ints, tiles)


def pick_body(ints_ref, *refs):
    pairs, far_refs, out_refs = refs[:2], refs[2:4], refs[4:]

    @pl.when(active(len(out_refs) - 1))
    def _():
        core = ints_ref[CORE_AT]
        for slot, out_ref in enumerate(out_refs):
            source = ints_ref[SLOT_AT + slot]
            base = slot * 9

            def entry(part, source=source, base=base):
                inner = jnp.where(source == 3, ints_ref[2 * INTS + base + part], ints_ref[base + 3 + part])
                return jnp.where(source == 1, ints_ref[INTS + base + 6 + part], inner)

            same_chip = ((source == 1) & (core == 1)) | ((source == 3) & (core == 0))
            away = (source == 1) | (source == 3)
            micro = entry(0)
            chosen = selection(entry(1), entry(2))
            for index, far_ref in enumerate(far_refs):

                @pl.when(away & ~same_chip & (micro == index))
                def _(chosen=chosen, far_ref=far_ref, out_ref=out_ref):
                    rows = jnp.dot(chosen, far_ref[...], preferred_element_type=jnp.float32)
                    out_ref[...] = rows.astype(jnp.bfloat16)

            for pair, wanted in zip(pairs, (same_chip, ~away)):

                @pl.when(wanted)
                def _(chosen=chosen, pair=pair, micro=micro, out_ref=out_ref):
                    rows = jnp.dot(chosen, pair[micro], preferred_element_type=jnp.float32)
                    out_ref[...] = rows.astype(jnp.bfloat16)


def pick_crops(ints, pairs, slots):
    width = pairs[-1].shape[1]
    return pl.pallas_call(
        pick_body,
        out_shape=[pltpu.VMEM((PADDED, width), jnp.bfloat16)] * slots,
        in_specs=[SMEM] + [VMEM] * len(pairs),
        out_specs=[VMEM] * slots,
        compiler_params=LIMITED,
        name="pick_crops",
    )(ints, *map(resident, pairs))


EMBED, MERGE, QUERY = 0, 1536, 2560
KEY, VALUE, OUT, POS, HALF = 0, 1024, 2048, 3072, 3584


def pack_body(parity_ref, embed, merge, pos, qkv, out, packed, buffer, sems):
    first = [
        (embed.at[:, pl.ds(0, LANES)], EMBED),
        (embed.at[:, pl.ds(LANES, LANES)], EMBED + 768),
        (merge.at[:, pl.ds(0, LANES)], MERGE),
        (merge.at[:, pl.ds(LANES, LANES)], MERGE + 512),
        (qkv.at[0], QUERY),
    ]
    second = [(qkv.at[1], KEY), (qkv.at[2], VALUE)]
    second += [(out.at[:, pl.ds(column * LANES, LANES)], OUT + column * LANES) for column in range(8)]
    second += [
        (pos.at[:, pl.ds(0, LANES)], POS),
        (pos.at[:, pl.ds(LANES, LANES)], POS + PADDED),
    ]
    for parity, pieces in enumerate((first, second)):

        @pl.when(parity_ref[0] == parity)
        def _(pieces=pieces):
            copies, results = [], []
            for number, (piece, at) in enumerate(pieces):
                place = pl.ds(at, piece.shape[0])
                copies.append(pltpu.make_async_copy(piece, buffer.at[place], sems.at[2 * number]))
                results.append(
                    pltpu.make_async_copy(buffer.at[place], packed.at[place], sems.at[2 * number + 1])
                )
                copies[-1].start()
            for copy, result in zip(copies, results):
                copy.wait()
                result.start()
            for result in results:
                result.wait()


def packed_half(parity, embed, merge, pos, qkv, out):
    return pl.pallas_call(
        pack_body,
        out_shape=jax.ShapeDtypeStruct((HALF, LANES), jnp.bfloat16),
        in_specs=[SMEM] + [ANY] * 5,
        out_specs=ANY,
        scratch_shapes=[pltpu.VMEM((HALF, LANES), jnp.bfloat16), pltpu.SemaphoreType.DMA((24,))],
        compiler_params=LIMITED,
        name="pack_weights",
    )(parity, *map(in_hbm, (embed, merge, pos, qkv, out)))


def columns(ref, section, low, height):
    return jnp.concatenate(
        [ref[section, pl.ds(low, height), :], ref[section, pl.ds(low + height, height), :]], axis=1
    )


def stage_body(ints_ref, pix_near, pix_own, pix_far, packed, weights, base_ref, pix, sems):
    source = ints_ref[SLOT_AT + ints_ref[SECTION_AT]]
    sections = packed.shape[0] // 2
    spans = [(0, EMBED, MERGE), (1, POS, HALF), (0, MERGE, HALF), (1, KEY, POS)]
    copies = []
    for part, low, high in spans:
        for section in range(sections):
            place = (2 * section + part, pl.ds(low, high - low))
            copies.append(
                pltpu.make_async_copy(packed.at[place], weights.at[place], sems.at[1 + len(copies)])
            )
    for copy in copies:
        copy.start()
    core = ints_ref[CORE_AT]
    same_chip = ((source == 1) & (core == 1)) | ((source == 3) & (core == 0))
    away = (source == 1) | (source == 3)
    for pix_ref, wanted in ((pix_near, same_chip), (pix_own, ~away), (pix_far, away & ~same_chip)):

        @pl.when(wanted)
        def _(pix_ref=pix_ref):
            copy = pltpu.make_async_copy(pix_ref, pix, sems.at[0])
            copy.start()
            copy.wait()

    for copy in copies[: 2 * sections]:
        copy.wait()
    rows = pix[...]
    row_ok = lax.broadcasted_iota(jnp.int32, (PADDED, 2 * LANES), 0) < ROWS
    for section in range(sections):
        pos = jnp.where(row_ok, columns(weights, 2 * section + 1, POS, PADDED).astype(jnp.float32), 0.0)
        base_ref[:, pl.ds(section * 2 * LANES, 2 * LANES)] = pos + jnp.dot(
            rows, columns(weights, 2 * section, EMBED, 768), preferred_element_type=jnp.float32
        )
    for copy in copies[2 * sections :]:
        copy.wait()


def staged(ints, pixels, packed):
    width = LANES * packed.shape[0]
    return pl.pallas_call(
        stage_body,
        out_shape=[pltpu.VMEM(packed.shape, jnp.bfloat16), pltpu.VMEM((PADDED, width), jnp.float32)],
        in_specs=[SMEM] + [ANY] * 4,
        out_specs=[VMEM] * 2,
        scratch_shapes=[
            pltpu.VMEM(pixels[0].shape, jnp.bfloat16),
            pltpu.SemaphoreType.DMA((1 + 2 * packed.shape[0],)),
        ],
        compiler_params=LIMITED,
        name="stage_weights",
    )(ints, *map(in_hbm, (*pixels, packed)))


def classify_body(*refs):
    feat_refs = refs[:4]
    base_ref, weights, gain_ref, source_ref, out_ref, feat = refs[4:]
    place = lax.axis_index("section")
    sections = weights.shape[0] // 2
    for number, feat_ref in enumerate(feat_refs):

        @pl.when(place == number)
        def _(feat_ref=feat_ref):
            feat[...] = feat_ref[...]

    feat_rows = feat[...]
    tokens = base_ref[...] + jnp.concatenate(
        [
            jnp.dot(feat_rows, columns(weights, 2 * section, MERGE, 512), preferred_element_type=jnp.float32)
            for section in range(sections)
        ],
        axis=1,
    )
    width = tokens.shape[1]
    mean = jnp.sum(tokens, axis=-1, keepdims=True) / width
    centred = tokens - mean
    var = jnp.sum(centred * centred, axis=-1, keepdims=True) / width
    attn_in = (centred * lax.rsqrt(var + EPSILON) * gain_ref[pl.ds(0, 1), :]).astype(jnp.bfloat16)
    token_sum = jnp.sum(tokens, axis=0, keepdims=True)
    key_ok = lax.broadcasted_iota(jnp.int32, (PADDED, PADDED), 1) < ROWS
    lane = lax.broadcasted_iota(jnp.int32, (PADDED, 2 * HEAD_DIM), 1)
    row_ok = lax.broadcasted_iota(jnp.int32, (PADDED, 2 * HEAD_DIM), 0) < ROWS
    context_sums = []
    for section in range(sections):
        first, second = 2 * section, 2 * section + 1
        piece = jnp.concatenate(
            [
                weights[first, pl.ds(QUERY, 1024), :],
                weights[second, pl.ds(KEY, 1024), :],
                weights[second, pl.ds(VALUE, 1024), :],
            ],
            axis=1,
        )
        qkv = jnp.dot(attn_in, piece, preferred_element_type=jnp.float32).astype(jnp.bfloat16)
        query, key, value = qkv[:, :128], qkv[:, 128:256], qkv[:, 256:]
        contexts = []
        for head in range(2):
            mine = (lane >= HEAD_DIM) if head else (lane < HEAD_DIM)
            scores = lax.dot_general(
                jnp.where(mine, query, jnp.zeros_like(query)),
                key,
                (((1,), (1,)), ((), ())),
                preferred_element_type=jnp.float32,
            ) * (1.0 / math.sqrt(HEAD_DIM))
            scores = jnp.where(key_ok, scores, -jnp.inf)
            top = jnp.max(scores, axis=-1, keepdims=True)
            numer = jnp.exp(scores - top)
            share = 1.0 / jnp.sum(numer, axis=-1, keepdims=True)
            summed = jnp.dot(numer.astype(jnp.bfloat16), value, preferred_element_type=jnp.float32)
            contexts.append(summed * share)
        context = jnp.where(lane < HEAD_DIM, contexts[0], contexts[1]).astype(jnp.bfloat16)
        context = jnp.where(row_ok, context.astype(jnp.float32), 0.0)
        context_sums.append(jnp.sum(context, axis=0, keepdims=True))
    context_mean = jnp.concatenate(context_sums, axis=1) / ROWS
    high = context_mean.astype(jnp.bfloat16)
    rest = context_mean - high.astype(jnp.float32)
    middle = rest.astype(jnp.bfloat16)
    low = (rest - middle.astype(jnp.float32)).astype(jnp.bfloat16)
    pieces = jnp.concatenate([high, middle, low, jnp.zeros((13, high.shape[1]), jnp.bfloat16)], axis=0)
    out_weight = jnp.concatenate(
        [
            jnp.concatenate(
                [weights[2 * section + 1, pl.ds(OUT + LANES * column, LANES), :] for column in range(8)], axis=1
            )
            for section in range(sections)
        ],
        axis=0,
    )
    mixed = jnp.dot(pieces, out_weight, preferred_element_type=jnp.float32)
    pooled = token_sum / ROWS + jnp.sum(mixed, axis=0, keepdims=True)
    pooled_mean = jnp.sum(pooled, axis=-1, keepdims=True) / width
    centred = pooled - pooled_mean
    var = jnp.sum(centred * centred, axis=-1, keepdims=True) / width
    result = centred * lax.rsqrt(var + EPSILON) * gain_ref[pl.ds(1, 1), :]
    out_ref[...] = jnp.where(source_ref[...] == 0, 0.0, result)


def classify(source, feats, base, weights, gain):
    return pl.pallas_call(
        classify_body,
        out_shape=jax.ShapeDtypeStruct((1, gain.shape[1]), jnp.float32),
        in_specs=[VMEM] * 8,
        out_specs=VMEM,
        scratch_shapes=[pltpu.VMEM(feats[0].shape, jnp.bfloat16)],
        compiler_params=LIMITED,
        name="classify",
    )(*map(resident, (*feats, base, weights, gain, source)))


def after(value, *others):
    return lax.optimization_barrier((value,) + others)[0]


def per_device(
    tile_features,
    patches,
    det_kernel,
    det_gain,
    det_in,
    det_out,
    det_scale,
    cls_embed,
    cls_merge,
    cls_pos,
    cls_qkv,
    cls_out,
    cls_gain,
    crop_plan,
    slot_from,
):
    sections = lax.axis_size("section")
    count = lax.axis_size(REP)
    section = lax.axis_index("section").astype(jnp.int32)
    core = lax.axis_index("core").astype(jnp.int32)
    width = tile_features.shape[3]
    slabs = width // LANES
    last = sections - 1
    upward = [(index, index + 1) for index in range(count - 1)]
    downward = [(target, origin) for origin, target in upward]
    swap = [(index, index ^ 1) for index in range(count)]
    ints = jnp.concatenate([crop_plan.reshape(-1), slot_from.reshape(-1), section.reshape(1), core.reshape(1)])

    half = packed_half(core.reshape(1), cls_embed, cls_merge, cls_pos, cls_qkv.transpose(1, 0, 2), cls_out)
    weights = lax.all_gather(half, ("section", "core"), axis=0)

    shard = jnp.stack([det_in[0].T, det_out[0]], axis=0)
    line = spread_in_groups(shard, line_groups(True))
    plane = spread_in_groups(after(line, half), line_groups(False))
    cut = cut_pixels(ints, patches.reshape(2, CELLS, patches.shape[3]))
    below = lax.ppermute(ints, REP, upward)
    above = lax.ppermute(ints, REP, downward)
    params = jnp.concatenate(
        [det_kernel[0].reshape(49, width), det_gain, det_scale, jnp.zeros((5, width), jnp.float32)], axis=0
    )
    params = params.reshape(56, slabs, LANES).transpose(1, 0, 2)
    start = tile_features.reshape(2, CELLS, width)
    tiles = [start[0], start[1]]
    early = early_norm(tiles[0], params)
    every = jnp.concatenate([ints, below, above])
    source = lax.dynamic_index_in_dim(slot_from[0], section, 0)
    source = jnp.broadcast_to(source[None], (1, cls_gain.shape[1]))
    plane, source = lax.optimization_barrier((plane, source, every, early, *cut))[:2]
    cut = lax.optimization_barrier((*cut, plane))[:3]
    beyond = [(index, index + 1) for index in range(1, count - 1, 2)]
    beyond += [(target, origin) for origin, target in beyond]
    pixels = (lax.ppermute(cut[0], REP, swap), cut[1], lax.ppermute(cut[2], REP, beyond))
    own = plane.reshape((SIDE * SIDE,) + shard.shape)
    other = lax.ppermute(own, REP, swap)

    for number in range(sections):
        if number == 0:
            first = early_block(tiles[0], params, own, other, early)
        else:
            tile = after(tiles[0], *pixels) if number == 1 else tiles[0]
            (first,) = detector_block(number, tile, params, own, other)
        before = (first,) if number == last else ()
        *pair, second = detector_block(number, after(tiles[1], first), params, own, other, *before)
        if number < last:
            tiles = [lax.ppermute(tile, "section", [(number, number + 1)]) for tile in (first, second)]

    within = [(last * count + origin, last * count + target) for origin, target in swap]
    across = [(last * count + origin, last * count + target) for origin, target in beyond]
    far_first = lax.ppermute(first, ("section",) + REP, across)
    far_second = lax.ppermute(after(second, far_first), ("section",) + REP, across)
    near = lax.ppermute(pair[0], ("section",) + REP, within)
    crops = pick_crops(after(every, weights), (near, pair[0], far_first, far_second), sections)
    feats = [lax.ppermute(crops[slot], "section", [(last, slot)]) for slot in range(last)] + [crops[last]]
    weights, base = staged(after(ints, *crops), pixels, weights)
    result = classify(source, feats, base, weights, cls_gain)
    return result[None]


def solution(mesh):
    sections = mesh.shape["section"]
    fine = jax.sharding.Mesh(mesh.devices.reshape(sections, SIDE, SIDE, 2), ("section",) + REP)
    return jax.shard_map(
        per_device,
        mesh=fine,
        in_specs=(
            P(REP, None, None, None),
            P(REP, None, None, None),
            P("section", None, None, None),
            P("section", None),
            P("section", None, REP),
            P("section", REP, None),
            P("section", None),
            P(None, "section"),
            P(None, "section"),
            P(None, "section"),
            P(None, None, "section"),
            P("section", None),
            P(),
            P(REP, None, None, None),
            P(REP, None),
        ),
        out_specs=P(REP, "section", None),
        check_vma=False,
    )
```
